32 devices in a mesh: rep: 2 (over x), tm: 16 (over z, y, core).
Axes of the slice: x: 2, y: 2, z: 4, core: 2. Of those that a mesh axis runs over, the one named last changes fastest.
Arguments:
- exo_tokens: bfloat16 [2048, 32, 1024], P('rep', 'tm'), parts along dimension 0, may hold values from -6 to 6
- queries: bfloat16 [2048, 1024], P(('rep', 'tm')), parts along dimension 0, may hold values from -80 to 80, as said below
- key_weight: bfloat16 [1024, 1024], replicated, may hold values from -0.1875 to 0.1875
- value_weight: bfloat16 [1024, 1024], replicated, may hold values from -0.1875 to 0.1875
- out_weight: bfloat16 [1024, 1024], replicated, may hold values from -0.1875 to 0.1875
- gaze_valid: int32 [2048], P(('rep', 'tm')), parts along dimension 0, may hold values 0 or 1
- window_offset: int32 [2048], P(('rep', 'tm')), parts along dimension 0, may hold values from 0 to 16
- cotangent: bfloat16 [2048, 1024], P(('rep', 'tm')), parts along dimension 0, may hold values from -6 to 6
Outputs:
- attended: bfloat16 [2048, 1024], P(('rep', 'tm')), parts along dimension 0
- d_queries: bfloat16 [2048, 1024], P(('rep', 'tm')), parts along dimension 0
- d_key_weight: float32 [2048, 1024], P(('rep', 'tm')), parts along dimension 0
- d_value_weight: float32 [2048, 1024], P(('rep', 'tm')), parts along dimension 0
- d_out_weight: float32 [2048, 1024], P(('rep', 'tm')), parts along dimension 0
The draws below stay inside these ranges and needn't reach their ends.
There are 2 independent parts, one for each index of `rep`. The reference program is written for one: setup_inputs(seed, part) draws one part's arguments, and reference() takes and returns one part's arrays. A program takes and returns all parts, laid end to end along the dimension named above; an argument that names none is the same for every part. Nothing has to cross between parts.
Inputs may be any that keep to these rules, and one draw needn't show every extreme that they name: `queries`: ego gaze query vectors.
All inputs are finite; a program needn't handle non-finite values. No bound on the sum of `gaze_valid` on one device may be relied on, other than what follows from the above.
Results may differ from the reference program's by a relative error of at most 0.025.
The reference program's roundings to bfloat16 on the way (of `keys`, `values`, `probs_b`, `context`, `masked_grad`, `d_context` and `d_scores`) count: a program that leaves them out, or rounds other values in their place, can miss the bound.
Values may be sent and summed in bfloat16 or wider, within the bound.
No kernel may reach another device: no remote copies, remote signals or barrier semaphores. Data moves between devices by JAX's collectives and lax.ppermute only.
A program may use at most 192 MiB of HBM per device.

```python
import jax
import jax.numpy as jnp
from jax import lax

D = 1024
H = 16
HD = 64
CAM = 4
TPF = 8
W = 16
FB = 64
FRAMES = 1024


def draw_queries(key, part):
    first_key = jax.random.fold_in(key, 0)
    return jnp.clip(jax.random.normal(first_key, (FRAMES, D), jnp.float32), -4.0, 4.0).astype(jnp.bfloat16)


def with_ends(entries, rng, smallest, top_value):
    index_at = [jax.random.randint(jax.random.fold_in(rng, axis), (), 0, length) for axis, length in enumerate(entries.shape)]
    main_axis = entries.shape.index(max(entries.shape))
    next_to = index_at[:main_axis] + [(index_at[main_axis] + 1) % entries.shape[main_axis]] + index_at[main_axis + 1:]
    return entries.at[tuple(index_at)].set(smallest).at[tuple(next_to)].set(top_value)


def raised(drawn, own_key, source, target, blocks, factor):
    owner, partner = [(jnp.arange(drawn.shape[dim]) // (drawn.shape[dim] // blocks)).reshape([-1 if axis == dim else 1 for axis in range(drawn.ndim)]) for dim in (source, target)]
    chosen = jax.random.permutation(own_key, blocks)[partner]
    strong = (owner == chosen) | (owner == (partner + blocks // 2) % blocks)
    return jnp.where(strong, factor * drawn, drawn)


def block_levels(key, shape, shards, least, high):
    gain, own = 1.0, jax.random.fold_in(key, 6)
    for axis_at, parts in shards:
        draws = jnp.exp(jax.random.uniform(jax.random.fold_in(own, axis_at), (parts,), jnp.float32, least / len(shards), high / len(shards)))
        gain = gain * jnp.repeat(draws, shape[axis_at] // parts).reshape([-1 if axis == axis_at else 1 for axis in range(len(shape))])
    return gain


def noise(rng, extent, deviation, bound, shards=(), kind=jnp.bfloat16):
    loudness = block_levels(rng, extent, shards, -0.22, 0.18) if shards else 1.0
    entries = jax.random.normal(rng, extent, jnp.float32) * deviation * loudness
    return jnp.minimum(jnp.maximum(entries, -bound), bound).astype(kind)


def heavy_noise(stream_key, dims, spread, reach, cuts, heavy, kind=jnp.bfloat16):
    values = spread * jax.random.normal(stream_key, dims, jnp.float32)
    if cuts:
        values = values * block_levels(stream_key, dims, cuts, -0.22, 0.18)
    return jnp.clip(raised(values, jax.random.fold_in(stream_key, 3), *heavy), -reach, reach).astype(kind)


def setup_inputs(seed: int = 0, part: int = 0) -> dict:
    seeds = jax.random.split(jax.random.key(seed), 9)
    own_keys = jax.random.split(jax.random.fold_in(seeds[8], part), 9)
    exo_tokens = heavy_noise(own_keys[0], (FRAMES, CAM * TPF, D), 1.0, 6.0, ((1, 16),), (1, 2, 16, 2.0))
    queries = draw_queries(jax.random.fold_in(jax.random.fold_in(seeds[8], part), 71), part)
    key_weight = noise(seeds[2], (D, D), D ** -0.5, 0.1875)
    value_weight = noise(seeds[3], (D, D), D ** -0.5, 0.1875)
    out_weight = noise(seeds[4], (D, D), D ** -0.5, 0.1875)
    gaze_valid = with_ends((jax.random.randint(own_keys[5], (FRAMES,), 0, 4) < 3).astype(jnp.int32), jax.random.fold_in(own_keys[5], 1), 0, 1)
    window_offset = with_ends(jax.random.randint(own_keys[6], (FRAMES,), 0, W + 1), jax.random.fold_in(own_keys[6], 1), 0, W).astype(jnp.int32)
    cotangent = noise(own_keys[7], (FRAMES, D), 1.0, 6.0, ((0, 16),))
    return {"exo_tokens": exo_tokens, "queries": queries, "key_weight": key_weight, "value_weight": value_weight, "out_weight": out_weight, "gaze_valid": gaze_valid, "window_offset": window_offset, "cotangent": cotangent}


def attend_block(q_rows, keys, values, grad_rows, valid_rows, offset_rows, out_weight, first, total):
    n_query = q_rows.shape[0]
    n_frames = keys.shape[0]
    n_tok = keys.shape[1]
    width = q_rows.shape[1]
    scale = HD ** -0.5
    t_abs = first + jnp.arange(n_query, dtype=jnp.int32)
    f_abs = first - W + jnp.arange(n_frames, dtype=jnp.int32)
    lower = t_abs - W + offset_rows
    upper = t_abs + offset_rows
    allow = (f_abs[None, :] >= lower[:, None]) & (f_abs[None, :] <= upper[:, None])
    allow = allow & (f_abs[None, :] >= 0) & (f_abs[None, :] < total)
    allow_keys = jnp.repeat(allow, n_tok, axis=1)
    q_heads = q_rows.reshape(n_query, H, HD).astype(jnp.float32)
    k_heads = keys.reshape(n_frames * n_tok, H, HD).astype(jnp.float32)
    v_heads = values.reshape(n_frames * n_tok, H, HD).astype(jnp.float32)
    scores = jnp.einsum("thd,khd->htk", q_heads, k_heads) * scale
    scores = jnp.where(allow_keys[None], scores, -1e30)
    top = jnp.max(scores, axis=-1, keepdims=True)
    expo = jnp.exp(scores - top)
    probs = expo / jnp.sum(expo, axis=-1, keepdims=True)
    probs_b = probs.astype(jnp.bfloat16)
    context = jnp.einsum("htk,khd->thd", probs_b.astype(jnp.float32), v_heads).reshape(n_query, width).astype(jnp.bfloat16)
    valid_col = valid_rows.astype(jnp.float32)[:, None]
    attended = (jnp.dot(context, out_weight, preferred_element_type=jnp.float32) * valid_col).astype(jnp.bfloat16)
    masked_grad = (grad_rows.astype(jnp.float32) * valid_col).astype(jnp.bfloat16)
    d_context = jnp.dot(masked_grad, out_weight.T, preferred_element_type=jnp.float32).astype(jnp.bfloat16)
    d_heads = d_context.reshape(n_query, H, HD).astype(jnp.float32)
    d_probs = jnp.einsum("thd,khd->htk", d_heads, v_heads)
    d_scores = probs * (d_probs - jnp.sum(probs * d_probs, axis=-1, keepdims=True)) * scale
    d_scores = d_scores.astype(jnp.bfloat16).astype(jnp.float32)
    d_query = jnp.einsum("htk,khd->thd", d_scores, k_heads).reshape(n_query, width).astype(jnp.bfloat16)
    key_part = jnp.einsum("htk,thd->khd", d_scores, q_heads).reshape(n_frames, n_tok, width).astype(jnp.bfloat16)
    value_part = jnp.einsum("htk,thd->khd", probs_b.astype(jnp.float32), d_heads).reshape(n_frames, n_tok, width).astype(jnp.bfloat16)
    return attended, d_query, key_part, value_part, context, masked_grad


def reference(exo_tokens, queries, key_weight, value_weight, out_weight, gaze_valid, window_offset, cotangent):
    n_tok = CAM * TPF
    flat = exo_tokens.reshape(-1, D)
    keys = jnp.dot(flat, key_weight, preferred_element_type=jnp.float32).astype(jnp.bfloat16).reshape(FRAMES, n_tok, D)
    values = jnp.dot(flat, value_weight, preferred_element_type=jnp.float32).astype(jnp.bfloat16).reshape(FRAMES, n_tok, D)
    margin = jnp.zeros((W, n_tok, D), jnp.bfloat16)
    keys_pad = jnp.concatenate([margin, keys, margin], axis=0)
    values_pad = jnp.concatenate([margin, values, margin], axis=0)
    span = FB + 2 * W

    def advance(carry, index):
        acc_key, acc_value = carry
        first = index * FB
        key_rows = lax.dynamic_slice_in_dim(keys_pad, first, span, 0)
        value_rows = lax.dynamic_slice_in_dim(values_pad, first, span, 0)
        q_rows = lax.dynamic_slice_in_dim(queries, first, FB, 0)
        grad_rows = lax.dynamic_slice_in_dim(cotangent, first, FB, 0)
        valid_rows = lax.dynamic_slice_in_dim(gaze_valid, first, FB, 0)
        offset_rows = lax.dynamic_slice_in_dim(window_offset, first, FB, 0)
        attended, d_query, key_part, value_part, context, masked_grad = attend_block(
            q_rows, key_rows, value_rows, grad_rows, valid_rows, offset_rows, out_weight, first, FRAMES)
        acc_key = lax.dynamic_update_slice_in_dim(
            acc_key, lax.dynamic_slice_in_dim(acc_key, first, span, 0) + key_part.astype(jnp.float32), first, 0)
        acc_value = lax.dynamic_update_slice_in_dim(
            acc_value, lax.dynamic_slice_in_dim(acc_value, first, span, 0) + value_part.astype(jnp.float32), first, 0)
        return (acc_key, acc_value), (attended, d_query, context, masked_grad)

    start = (jnp.zeros((FRAMES + 2 * W, n_tok, D), jnp.float32), jnp.zeros((FRAMES + 2 * W, n_tok, D), jnp.float32))
    (acc_key, acc_value), (attended, d_query, context, masked_grad) = lax.scan(
        advance, start, jnp.arange(FRAMES // FB, dtype=jnp.int32))
    attended = attended.reshape(FRAMES, D)
    d_query = d_query.reshape(FRAMES, D)
    context = context.reshape(FRAMES, D)
    masked_grad = masked_grad.reshape(FRAMES, D)
    flat_f = flat.astype(jnp.float32)
    key_sum = acc_key[W:W + FRAMES].reshape(-1, D)
    value_sum = acc_value[W:W + FRAMES].reshape(-1, D)
    d_key_weight = jnp.dot(flat_f.T, key_sum, precision=lax.Precision.HIGHEST)
    d_value_weight = jnp.dot(flat_f.T, value_sum, precision=lax.Precision.HIGHEST)
    d_out_weight = jnp.dot(context.astype(jnp.float32).T, masked_grad.astype(jnp.float32), precision=lax.Precision.HIGHEST)
    return attended, d_query, d_key_weight, d_value_weight, d_out_weight
```

```python
import functools

import jax
import jax.numpy as jnp
from jax import lax
from jax.experimental import pallas as pl
from jax.experimental.pallas import tpu as pltpu
from jax.sharding import PartitionSpec as P

H = 16
HD = 64
W = 16
GROUP = 4
LANES = GROUP * HD
CHUNK = 256
F32 = jnp.float32
BF16 = jnp.bfloat16


def tn_dot(a, b):
    return lax.dot_general(a, b, (((0,), (0,)), ((), ())), preferred_element_type=F32)


def nt_dot(a, b):
    return lax.dot_general(a, b, (((1,), (1,)), ((), ())), preferred_element_type=F32)


def nn_dot(a, b):
    return jnp.dot(a, b, preferred_element_type=F32)


def attention_kernel(
    tok, n_query, n_main, n_halo,
    lo_ref, hi_ref, q_ref, g_ref, km_ref, kh_ref, vm_ref, vh_ref,
    ctx_ref, dq_ref, kpm_ref, kph_ref, vpm_ref, vph_ref,
    s_ref, dp_ref, bq_ref, bg_ref, acc_ctx, acc_dq,
):
    scale = HD ** (-0.5)
    wide = GROUP * n_query
    row_head = lax.broadcasted_iota(jnp.int32, (wide, LANES), 0) // n_query
    col_head = lax.broadcasted_iota(jnp.int32, (wide, LANES), 1) // HD
    own = row_head == col_head
    zero = jnp.zeros((wide, LANES), BF16)
    bq_ref[...] = jnp.where(own, jnp.concatenate([q_ref[...]] * GROUP, axis=0), zero)
    bg_ref[...] = jnp.where(own, jnp.concatenate([g_ref[...]] * GROUP, axis=0), zero)
    lo = lo_ref[...]
    hi = hi_ref[...]
    rows = lax.broadcasted_iota(jnp.int32, (CHUNK, wide), 0)
    halo_rows = n_halo // 2

    def score(k_ref, v_ref, at, out_at, period, base, top):
        frame = (rows + at) % period // tok + base
        seen = (frame >= lo) & (frame <= hi)
        s = nt_dot(k_ref[pl.ds(at, CHUNK), :], bq_ref[...]) * scale
        s = jnp.where(seen, s, -1e30)
        s_ref[pl.ds(out_at, CHUNK), :] = s
        dp_ref[pl.ds(out_at, CHUNK), :] = nt_dot(v_ref[pl.ds(at, CHUNK), :], bg_ref[...])
        return jnp.maximum(top, jnp.max(s.reshape(CHUNK // 8, 8, wide), axis=0))

    top = jnp.full((8, wide), -1e30, F32)

    def main_score(c, top):
        at = pl.multiple_of(c * CHUNK, CHUNK)
        return score(km_ref, vm_ref, at, at, n_query * tok, 0, top)

    def halo_score(c, top):
        at = pl.multiple_of(c * CHUNK, CHUNK)
        base = jnp.where(at < halo_rows, -W, n_query)
        return score(kh_ref, vh_ref, at, n_main + at, W * tok, base, top)

    top = lax.fori_loop(0, n_main // CHUNK, main_score, top)
    top = lax.fori_loop(0, n_halo // CHUNK, halo_score, top)
    top = jnp.max(top, axis=0, keepdims=True)

    def expo(c, sums):
        total, weighted = sums
        at = pl.ds(pl.multiple_of(c * CHUNK, CHUNK), CHUNK)
        e = jnp.exp(s_ref[at, :] - top)
        s_ref[at, :] = e
        t = e * dp_ref[at, :]
        total = total + jnp.sum(e.reshape(CHUNK // 8, 8, wide), axis=0)
        weighted = weighted + jnp.sum(t.reshape(CHUNK // 8, 8, wide), axis=0)
        return total, weighted

    none = jnp.zeros((8, wide), F32)
    total, weighted = lax.fori_loop(0, (n_main + n_halo) // CHUNK, expo, (none, none))
    inverse = 1.0 / jnp.sum(total, axis=0, keepdims=True)
    mean = jnp.sum(weighted, axis=0, keepdims=True) * inverse

    acc_ctx[...] = jnp.zeros_like(acc_ctx)
    acc_dq[...] = jnp.zeros_like(acc_dq)

    def back(k_ref, v_ref, kp_ref, vp_ref, at, in_at):
        here = pl.ds(at, CHUNK)
        p = s_ref[pl.ds(in_at, CHUNK), :] * inverse
        ds = (p * (dp_ref[pl.ds(in_at, CHUNK), :] - mean) * scale).astype(BF16)
        pb = p.astype(BF16)
        acc_ctx[...] += tn_dot(pb, v_ref[here, :])
        acc_dq[...] += tn_dot(ds, k_ref[here, :])
        kp_ref[here, :] = nn_dot(ds, bq_ref[...]).astype(BF16)
        vp_ref[here, :] = nn_dot(pb, bg_ref[...]).astype(BF16)

    def main_back(c, carry):
        at = pl.multiple_of(c * CHUNK, CHUNK)
        back(km_ref, vm_ref, kpm_ref, vpm_ref, at, at)
        return carry

    def halo_back(c, carry):
        at = pl.multiple_of(c * CHUNK, CHUNK)
        back(kh_ref, vh_ref, kph_ref, vph_ref, at, n_main + at)
        return carry

    lax.fori_loop(0, n_main // CHUNK, main_back, 0)
    lax.fori_loop(0, n_halo // CHUNK, halo_back, 0)

    def diagonal(acc):
        kept = jnp.where(own, acc, 0.0)
        out = kept[:n_query]
        for h in range(1, GROUP):
            out = out + kept[h * n_query : (h + 1) * n_query]
        return out.astype(BF16)

    ctx_ref[...] = diagonal(acc_ctx[...])
    dq_ref[...] = diagonal(acc_dq[...])


def attention(tok, lo, hi, queries, d_context, k_main, k_halo, v_main, v_halo):
    n_query, width = queries.shape
    n_main, n_halo = k_main.shape[0], k_halo.shape[0]
    wide = GROUP * n_query
    flat = pl.BlockSpec((1, wide), lambda g: (0, 0))

    def cols(n):
        return pl.BlockSpec((n, LANES), lambda g: (0, g))

    def shape(n):
        return jax.ShapeDtypeStruct((n, width), BF16)

    n_keys = n_main + n_halo
    return pl.pallas_call(
        functools.partial(attention_kernel, tok, n_query, n_main, n_halo),
        grid=(width // LANES,),
        in_specs=[flat, flat, cols(n_query), cols(n_query)]
        + [cols(n_main), cols(n_halo), cols(n_main), cols(n_halo)],
        out_specs=[cols(n_query), cols(n_query)]
        + [cols(n_main), cols(n_halo), cols(n_main), cols(n_halo)],
        out_shape=[shape(n_query), shape(n_query)]
        + [shape(n_main), shape(n_halo), shape(n_main), shape(n_halo)],
        scratch_shapes=[
            pltpu.VMEM((n_keys, wide), F32),
            pltpu.VMEM((n_keys, wide), F32),
            pltpu.VMEM((wide, LANES), BF16),
            pltpu.VMEM((wide, LANES), BF16),
            pltpu.VMEM((wide, LANES), F32),
            pltpu.VMEM((wide, LANES), F32),
        ],
        compiler_params=pltpu.CompilerParams(dimension_semantics=("arbitrary",)),
        cost_estimate=pl.CostEstimate(
            flops=12 * n_keys * wide * width,
            bytes_accessed=8 * n_keys * width,
            transcendentals=n_keys * H * n_query,
        ),
        name="banded_attention",
    )(lo, hi, queries, d_context, k_main, k_halo, v_main, v_halo)


def scatter_sum(term, bits, order):
    n_dev = 1 << bits
    me = lax.axis_index("tm")
    rows, cols = term.shape
    left = list(range(bits - 1, -1, -1))
    block = term.reshape([2] * bits + [rows // n_dev, cols])
    for bit in order:
        axis = left.index(bit)
        left.remove(bit)
        mine = (me >> bit) & 1
        away = lax.dynamic_index_in_dim(block, 1 - mine, axis, keepdims=False)
        keep = lax.dynamic_index_in_dim(block, mine, axis, keepdims=False)
        come = lax.ppermute(away, "tm", [(i, i ^ (1 << bit)) for i in range(n_dev)])
        block = keep.astype(F32) + come.astype(F32)
        if left:
            block = block.astype(BF16)
    return block


def shards(
    exo_tokens, queries, key_weight, value_weight, out_weight, gaze_valid, window_offset, cotangent
):
    n_query, width = queries.shape
    tok = exo_tokens.shape[1]
    n_dev = lax.axis_size("tm")
    bits = n_dev.bit_length() - 1
    total = n_query * n_dev
    first = lax.axis_index("tm") * n_query
    own_rows = lax.all_to_all(
        exo_tokens.reshape(-1, width), "tm", split_axis=0, concat_axis=0, tiled=True
    )
    by_source = own_rows.reshape(n_dev, n_query * tok, width)
    edge = W * tok
    up = [(i, i + 1) for i in range(n_dev - 1)]
    down = [(target, source) for source, target in up]
    low = lax.ppermute(by_source[:, -edge:].reshape(-1, width), "tm", up)
    high = lax.ppermute(by_source[:, :edge].reshape(-1, width), "tm", down)
    halo = jnp.concatenate([low, high], axis=0)

    valid_col = gaze_valid.astype(F32)[:, None]
    masked_grad = (cotangent.astype(F32) * valid_col).astype(BF16)
    d_context = nt_dot(masked_grad, out_weight).astype(BF16)
    at = jnp.arange(n_query, dtype=jnp.int32)
    lower = jnp.maximum(at - W + window_offset, -first)
    upper = jnp.minimum(at + window_offset, total - 1 - first)
    lo = jnp.tile(lower[None, :], (1, GROUP))
    hi = jnp.tile(upper[None, :], (1, GROUP))

    k_main = nn_dot(own_rows, key_weight).astype(BF16)
    v_main = nn_dot(own_rows, value_weight).astype(BF16)
    k_halo = nn_dot(halo, key_weight).astype(BF16)
    v_halo = nn_dot(halo, value_weight).astype(BF16)
    context, d_query, kp_main, kp_halo, vp_main, vp_halo = attention(
        tok, lo, hi, queries, d_context, k_main, k_halo, v_main, v_halo
    )
    attended = (nn_dot(context, out_weight) * valid_col).astype(BF16)

    ascending = list(range(bits))
    rotated = [0] + list(range(2, bits)) + [1] if bits > 1 else ascending
    half = width // 2
    out_term = tn_dot(context, masked_grad).astype(BF16)
    d_out = jnp.concatenate(
        [
            scatter_sum(out_term[:, :half], bits, ascending),
            scatter_sum(out_term[:, half:], bits, rotated),
        ],
        axis=1,
    )
    d_key = scatter_sum(
        (tn_dot(own_rows, kp_main) + tn_dot(halo, kp_halo)).astype(BF16), bits, ascending
    )
    d_value = scatter_sum(
        (tn_dot(own_rows, vp_main) + tn_dot(halo, vp_halo)).astype(BF16), bits, rotated
    )
    return (attended, d_query, d_key, d_value, d_out)


def solution(mesh):
    in_specs = (
        P("rep", "tm", None),
        P(("rep", "tm"), None),
        P(),
        P(),
        P(),
        P(("rep", "tm")),
        P(("rep", "tm")),
        P(("rep", "tm"), None),
    )
    out_specs = (
        P(("rep", "tm"), None),
        P(("rep", "tm"), None),
        P(("rep", "tm"), None),
        P(("rep", "tm"), None),
        P(("rep", "tm"), None),
    )
    return jax.shard_map(shards, mesh=mesh, in_specs=in_specs, out_specs=out_specs, check_vma=False)
```

```python
import functools

import jax
import jax.numpy as jnp
from jax import lax
from jax.experimental import pallas as pl
from jax.experimental.pallas import tpu as pltpu
from jax.sharding import PartitionSpec as P

H = 16
HD = 64
W = 16
GROUP = 4
LANES = GROUP * HD
CALLS = 2
CHUNK = 256
F32 = jnp.float32
BF16 = jnp.bfloat16


def tn_dot(a, b):
    return lax.dot_general(a, b, (((0,), (0,)), ((), ())), preferred_element_type=F32)


def nt_dot(a, b):
    return lax.dot_general(a, b, (((1,), (1,)), ((), ())), preferred_element_type=F32)


def nn_dot(a, b):
    return jnp.dot(a, b, preferred_element_type=F32)


def own_head(n_query):
    wide = GROUP * n_query
    row_head = lax.broadcasted_iota(jnp.int32, (wide, LANES), 0) // (n_query // 2) % GROUP
    col_head = lax.broadcasted_iota(jnp.int32, (wide, LANES), 1) // HD
    return row_head == col_head


def spread(x, own):
    part = x.shape[0] // 2
    rows = jnp.concatenate([x[:part]] * GROUP + [x[part:]] * GROUP, 0)
    return jnp.where(own, rows, jnp.zeros_like(rows))


def scaled(x):
    return (x.astype(F32) * HD ** (-0.5)).astype(BF16)


def fill_bias(lo_ref, hi_ref, bias_ref, n_query):
    wide = GROUP * n_query
    lo = lo_ref[...]
    hi = hi_ref[...]
    rows = lax.broadcasted_iota(jnp.int32, (CHUNK, wide), 0)
    near = rows % W
    far = rows % (2 * W)
    second = lax.broadcasted_iota(jnp.int32, (CHUNK, wide), 1) >= wide // 2
    frames = (
        near + jnp.where(second, n_query - W, 0),
        far + W,
        near + jnp.where(second, n_query, -W),
    )
    for i, frame in enumerate(frames):
        bias_ref[i] = jnp.where((frame >= lo) & (frame <= hi), 0.0, -1e30)


def load_edge(ref, side):
    return ref[:, :, side].reshape(CHUNK, LANES)


def load_halo(ref, side):
    return ref[side].reshape(CHUNK, LANES)


def load_mid(ref, c):
    runs = ref.shape[0] // 2
    return ref[pl.ds(c * runs, runs)].reshape(CHUNK, LANES)


def pair_dot(ref, load, x_ref):
    mid = x_ref.shape[0] // 2
    return jnp.concatenate(
        [nt_dot(load(ref, 0), x_ref[:mid, :]), nt_dot(load(ref, 1), x_ref[mid:, :])], 1
    )


def fold(x):
    return x.reshape(CHUNK // 8, 8, x.shape[1])


def stats_kernel(
    lo_ref, hi_ref, q_ref, g_ref, ke_ref, km_ref, kh_ref, ve_ref, vm_ref, vh_ref,
    out_ref, s_ref, bias_ref, bq_ref, bg_ref,
):
    n_query = q_ref.shape[0]
    wide = GROUP * n_query
    own = own_head(n_query)
    bq_ref[...] = scaled(spread(q_ref[...], own))
    bg_ref[...] = scaled(spread(g_ref[...], own))

    @pl.when(pl.program_id(1) == 0)
    def _():
        fill_bias(lo_ref, hi_ref, bias_ref, n_query)

    def score(at, table, s, top):
        s = s + bias_ref[table]
        s_ref[at] = s
        return jnp.maximum(top, jnp.max(fold(s), axis=0))

    top = jnp.full((8, wide), -1e30, F32)
    top = score(0, 0, pair_dot(ke_ref, load_edge, bq_ref), top)
    for c in range(2):
        top = score(1 + c, 1, nt_dot(load_mid(km_ref, c), bq_ref[...]), top)
    top = score(3, 2, pair_dot(kh_ref, load_halo, bq_ref), top)
    top = jnp.max(top, axis=0, keepdims=True)

    total = jnp.zeros((8, wide), F32)
    weighted = jnp.zeros((8, wide), F32)
    for c in range(4):
        if c == 0:
            dp = pair_dot(ve_ref, load_edge, bg_ref)
        elif c == 3:
            dp = pair_dot(vh_ref, load_halo, bg_ref)
        else:
            dp = nt_dot(load_mid(vm_ref, c - 1), bg_ref[...])
        e = jnp.exp(s_ref[c] - top)
        total = total + jnp.sum(fold(e), axis=0)
        weighted = weighted + jnp.sum(fold(e * dp), axis=0)
    out_ref[0:1, :] = top
    out_ref[1:2, :] = jnp.sum(total, axis=0, keepdims=True)
    out_ref[2:3, :] = jnp.sum(weighted, axis=0, keepdims=True)


def grads_kernel(
    lo_ref, hi_ref, one_ref, two_ref, q_ref, g_ref,
    ke_ref, km_ref, kh_ref, ve_ref, vm_ref, vh_ref,
    ctx_ref, dq_ref, pe_ref, pm_ref, ph_ref,
    bias_ref, bq_ref, bg_ref, bqs_ref, bgs_ref, acc_ctx, acc_dq,
):
    n_query = q_ref.shape[0]
    part = n_query // 2
    wide = GROUP * n_query
    mid = wide // 2
    own = own_head(n_query)
    bq_ref[...] = spread(q_ref[...], own)
    bg_ref[...] = spread(g_ref[...], own)
    bqs_ref[...] = scaled(bq_ref[...])
    bgs_ref[...] = scaled(bg_ref[...])

    @pl.when(pl.program_id(1) == 0)
    def _():
        fill_bias(lo_ref, hi_ref, bias_ref, n_query)

    top = jnp.maximum(one_ref[0:1, :], two_ref[0:1, :])
    one = jnp.exp(one_ref[0:1, :] - top)
    two = jnp.exp(two_ref[0:1, :] - top)
    inverse = 1.0 / (one_ref[1:2, :] * one + two_ref[1:2, :] * two)
    mean = (one_ref[2:3, :] * one + two_ref[2:3, :] * two) * inverse
    acc_ctx[...] = jnp.zeros_like(acc_ctx)
    acc_dq[...] = jnp.zeros_like(acc_dq)

    def soft(table, s, dp):
        p = jnp.exp(s + bias_ref[table] - top) * inverse
        return p.astype(BF16), (p * (dp - mean)).astype(BF16)

    def pair(k_ref, v_ref, load, table, store):
        pb, ds = soft(table, pair_dot(k_ref, load, bqs_ref), pair_dot(v_ref, load, bgs_ref))
        for side, lanes in ((0, slice(0, mid)), (1, slice(mid, wide))):
            acc_ctx[lanes, :] += tn_dot(pb[:, lanes], load(v_ref, side))
            acc_dq[lanes, :] += tn_dot(ds[:, lanes], load(k_ref, side))
            store(side, slice(0, LANES), nn_dot(ds[:, lanes], bq_ref[lanes, :]))
            store(side, slice(LANES, 2 * LANES), nn_dot(pb[:, lanes], bg_ref[lanes, :]))

    def store_edge(side, cols, x):
        shape = pe_ref.shape
        pe_ref[:, :, side, :, cols] = x.astype(BF16).reshape(shape[0], shape[1], W, LANES)

    def store_halo(side, cols, x):
        shape = ph_ref.shape
        ph_ref[side, :, :, :, cols] = x.astype(BF16).reshape(shape[1], shape[2], W, LANES)

    pair(ke_ref, ve_ref, load_edge, 0, store_edge)

    def middle(c, carry):
        runs = pm_ref.shape[0] // 2
        k = load_mid(km_ref, c)
        v = load_mid(vm_ref, c)
        pb, ds = soft(1, nt_dot(k, bqs_ref[...]), nt_dot(v, bgs_ref[...]))
        acc_ctx[...] += tn_dot(pb, v)
        acc_dq[...] += tn_dot(ds, k)
        shape = (runs, pm_ref.shape[1], 2 * W, LANES)
        here = pl.ds(c * runs, runs)
        pm_ref[here, :, :, :LANES] = nn_dot(ds, bq_ref[...]).astype(BF16).reshape(shape)
        pm_ref[here, :, :, LANES:] = nn_dot(pb, bg_ref[...]).astype(BF16).reshape(shape)
        return carry

    lax.fori_loop(0, 2, middle, 0)
    pair(kh_ref, vh_ref, load_halo, 2, store_halo)

    def diagonal(acc, out_ref):
        kept = jnp.where(own, acc, 0.0)
        for i in range(2):
            rows = [kept[(i * GROUP + h) * part : (i * GROUP + h + 1) * part] for h in range(GROUP)]
            out_ref[i * part : (i + 1) * part, :] = functools.reduce(jnp.add, rows)

    diagonal(acc_ctx[...], ctx_ref)
    diagonal(acc_dq[...], dq_ref)


def attention(first_group, groups, lo, hi, stats, queries, d_context, keys, values):
    n_query = queries.shape[1]
    src, tok = keys[0].shape[0], keys[0].shape[2]
    wide = GROUP * n_query
    flat = pl.BlockSpec((None, 1, wide), lambda b, g: (b, 0, 0))
    rows = pl.BlockSpec((None, n_query, LANES), lambda b, g: (b, 0, first_group + g))
    table = pl.BlockSpec((None, None, 3, wide), lambda b, g: (b, g, 0, 0))

    def edge(first, k=1):
        shape = (src, None, tok, 2, W, k * LANES)
        return pl.BlockSpec(shape, lambda b, g: (0, b, 0, 0, 0, first + g))

    def mid(first, k=1):
        shape = (src, None, tok, 2 * W, k * LANES)
        return pl.BlockSpec(shape, lambda b, g: (0, b, 0, 0, first + g))

    def halo(first, k=1):
        shape = (2, src, None, tok, W, k * LANES)
        return pl.BlockSpec(shape, lambda b, g: (0, 0, b, 0, 0, first + g))

    sections = [edge(first_group), mid(first_group), halo(first_group)]
    operand = pltpu.VMEM((wide, LANES), BF16)
    total = pltpu.VMEM((wide, LANES), F32)
    bias = pltpu.VMEM((3, CHUNK, wide), F32)
    scores = 8 * CHUNK * wide * groups
    common = dict(
        grid=(2, groups),
        compiler_params=pltpu.CompilerParams(dimension_semantics=("arbitrary", "arbitrary")),
    )
    if stats is None:
        return pl.pallas_call(
            stats_kernel,
            in_specs=[flat, flat, rows, rows] + sections * 2,
            out_specs=table,
            out_shape=jax.ShapeDtypeStruct((2, groups, 3, wide), F32),
            scratch_shapes=[pltpu.VMEM((4, CHUNK, wide), F32), bias, operand, operand],
            cost_estimate=pl.CostEstimate(
                flops=4 * scores * LANES, bytes_accessed=6 * scores, transcendentals=scores
            ),
            name="softmax_stats",
            **common,
        )(lo, hi, queries, d_context, *keys, *values)

    def shape(x):
        return jax.ShapeDtypeStruct(x.shape[:-1] + (2 * groups * LANES,), BF16)

    partial = jax.ShapeDtypeStruct((2, n_query, groups * LANES), F32)
    partial_spec = pl.BlockSpec((None, n_query, LANES), lambda b, g: (b, 0, g))
    return pl.pallas_call(
        grads_kernel,
        in_specs=[flat, flat, table, table, rows, rows] + sections * 2,
        out_specs=[partial_spec, partial_spec, edge(0, 2), mid(0, 2), halo(0, 2)],
        out_shape=[partial, partial] + [shape(x) for x in keys],
        scratch_shapes=[bias] + [operand] * 4 + [total] * 2,
        cost_estimate=pl.CostEstimate(
            flops=12 * scores * LANES, bytes_accessed=12 * scores, transcendentals=scores
        ),
        name="banded_grads",
        **common,
    )(lo, hi, *stats, queries, d_context, *keys, *values)


class ScatterSum:
    def __init__(self, term, bits, order):
        self.order = list(order)
        self.left = list(range(bits - 1, -1, -1))
        self.block = term.reshape([2] * bits + [term.shape[0] >> bits, term.shape[1]])

    def send(self):
        bit = self.order.pop(0)
        axis = self.left.index(bit)
        self.left.remove(bit)
        mine = (lax.axis_index("tm") >> bit) & 1
        away = lax.dynamic_index_in_dim(self.block, 1 - mine, axis, keepdims=False)
        self.keep = lax.dynamic_index_in_dim(self.block, mine, axis, keepdims=False)
        return away, 1 << bit

    def receive(self, come):
        block = self.keep.astype(F32) + come.astype(F32)
        self.block = block.astype(BF16) if self.left else block


class Gather:
    def __init__(self, block, bits):
        self.block = block
        self.order = list(range(bits - 1, -1, -1))

    def send(self):
        return self.block, 1 << self.order.pop(0)

    def receive(self, come):
        self.block = jnp.concatenate([self.block, come], axis=0)


class Swap:
    def __init__(self, block, bit):
        self.block = block
        self.order = [bit]

    def send(self):
        return self.block, 1 << self.order.pop(0)

    def receive(self, come):
        self.come = come


def beside(moving, work, *args):
    n_dev = lax.axis_size("tm")
    moving = [m for m in moving if m.order]
    sends = [m.send() for m in moving]
    args, aways = lax.optimization_barrier((args, [away for away, _ in sends]))
    comes = [
        lax.ppermute(away, "tm", [(i, i ^ step) for i in range(n_dev)])
        for away, (_, step) in zip(aways, sends)
    ]
    result, comes = lax.optimization_barrier((work(*args), comes))
    for m, come in zip(moving, comes):
        m.receive(come)
    return result


def shards(
    exo_tokens, queries, key_weight, value_weight, out_weight, gaze_valid, window_offset, cotangent
):
    n_query, width = queries.shape
    tok = exo_tokens.shape[1]
    n_dev = lax.axis_size("tm")
    bits = n_dev.bit_length() - 1
    src = n_dev // 2
    total = n_query * n_dev
    me = lax.axis_index("tm")
    upper_half = me >= src
    spot = me % src

    by_block = exo_tokens.reshape(2, src, n_query, tok, width)
    halves = [list(range(src)), list(range(src, n_dev))]
    outer = jnp.stack([by_block[:, :, :W], by_block[:, :, -W:]], axis=2)
    outer = outer.transpose(1, 0, 4, 2, 3, 5)
    inner = by_block[:, :, W:-W].transpose(1, 0, 3, 2, 4)
    edge = lax.all_to_all(outer, "tm", 0, 0, axis_index_groups=halves, tiled=True)
    middle = lax.all_to_all(inner, "tm", 0, 0, axis_index_groups=halves, tiled=True)
    ring = [(i, i // src * src + (i + 1) % src) for i in range(n_dev)]
    low = lax.ppermute(edge[:, :, :, 1], "tm", ring)
    high = lax.ppermute(edge[:, :, :, 0], "tm", [(target, source) for source, target in ring])
    low = jnp.where(spot == 0, jnp.flip(low, 1), low)
    high = jnp.where(spot == src - 1, jnp.flip(high, 1), high)
    halo = jnp.stack([low, high], axis=0)

    valid_col = gaze_valid.astype(F32)[:, None]
    masked_grad = (cotangent.astype(F32) * valid_col).astype(BF16)
    far = bits - 1
    gather = Gather(masked_grad, bits)
    swap_q, swap_o = Swap(queries, far), Swap(window_offset, far)
    beside([gather, swap_q, swap_o], lambda: ())

    def both(own, other):
        return jnp.where(upper_half, jnp.stack([other, own]), jnp.stack([own, other]))

    q_pair = both(queries, swap_q.come)
    d_context = nt_dot(gather.block, out_weight).astype(BF16)
    g_pair = both(d_context[:n_query], d_context[n_query:])
    offsets = both(window_offset, swap_o.come)
    at = jnp.arange(n_query, dtype=jnp.int32)
    first = (spot + jnp.array([0, src], jnp.int32))[:, None] * n_query
    lower = jnp.maximum(at - W + offsets, -first)
    upper = jnp.minimum(at + offsets, total - 1 - first)

    def lanes(x):
        return jnp.tile(x.reshape(2, 2, 1, n_query // 2), (1, 1, GROUP, 1)).reshape(2, 1, -1)

    lo, hi = lanes(lower), lanes(upper)

    def project(x):
        flat = x.reshape(-1, width)
        return (
            nn_dot(flat, key_weight).astype(BF16).reshape(x.shape),
            nn_dot(flat, value_weight).astype(BF16).reshape(x.shape),
        )

    ke, ve = project(edge)
    km, vm = beside([gather], project, middle)
    kh, vh = project(halo)
    keys, values = (ke, km, kh), (ve, vm, vh)
    sources = [x.reshape(-1, width) for x in (edge, middle, halo)]

    groups = width // LANES // CALLS

    def measure(call, moving):
        work = functools.partial(attention, call * groups, groups, lo, hi, None)
        return Swap(beside(moving, work, q_pair, g_pair, keys, values), far)

    swaps = [measure(0, [gather])]
    for call in range(1, CALLS):
        swaps.append(measure(call, [gather, swaps[-1]]))

    def own_part(x):
        return jnp.where(upper_half, x[1], x[0])

    def other_part(x):
        return jnp.where(upper_half, x[0], x[1])

    moving = [gather] + swaps
    owns, trades, shares = [], [], []
    if CALLS == 1:
        beside(moving, lambda: ())
    for call in range(CALLS):
        stats = (swaps[call].block, swaps[call].come)
        work = functools.partial(attention, call * groups, groups, lo, hi, stats)
        context, d_query, *grads = beside(moving, work, q_pair, g_pair, keys, values)
        owns.append(jnp.stack([own_part(context), own_part(d_query)]))
        trades.append(Swap(jnp.stack([other_part(context), other_part(d_query)]), far))
        moving.append(trades[-1])

        def weigh(*parts):
            terms = [tn_dot(x, g.reshape(x.shape[0], -1)) for x, g in zip(sources, parts)]
            return functools.reduce(jnp.add, terms).astype(BF16)

        term = beside(moving, weigh, *grads)
        cut = term.shape[1] // 2
        orders = [list(range(bits)), [0] + list(range(2, bits)) + [1]]
        for i, order in enumerate(orders):
            shares.append(ScatterSum(term[:, i * cut : (i + 1) * cut], bits, order))
            moving.append(shares[-1])

    pairs = [own + trade.come for own, trade in zip(owns, trades)]
    context = jnp.concatenate([x[0] for x in pairs], axis=1).astype(BF16)
    d_query = jnp.concatenate([x[1] for x in pairs], axis=1).astype(BF16)

    def finish(context):
        attended = (nn_dot(context, out_weight) * valid_col).astype(BF16)
        columns = context.reshape(n_query, n_dev, -1).swapaxes(0, 1)
        return attended, lax.all_to_all(columns, "tm", split_axis=0, concat_axis=0, tiled=True)

    attended, columns = beside(moving, finish, context)
    columns = columns.reshape([2] * bits + [n_query, -1])
    for bit in range(bits):
        axis = bits - 1 - bit
        columns = jnp.where((me >> bit) & 1 == 1, jnp.flip(columns, axis), columns)
    columns = columns.transpose(list(range(bits - 1, -1, -1)) + [bits, bits + 1])
    d_out = beside(moving, lambda c: tn_dot(c.reshape(total, -1), gather.block), columns)
    while any(m.order for m in moving):
        beside(moving, lambda: ())
    blocks = [s.block.reshape(s.block.shape[0], -1, 2, LANES) for s in shares]
    return (
        attended,
        d_query,
        jnp.concatenate([b[:, i, 0] for b in blocks for i in range(b.shape[1])], axis=1),
        jnp.concatenate([b[:, i, 1] for b in blocks for i in range(b.shape[1])], axis=1),
        d_out,
    )


def solution(mesh):
    in_specs = (
        P("rep", "tm", None),
        P(("rep", "tm"), None),
        P(),
        P(),
        P(),
        P(("rep", "tm")),
        P(("rep", "tm")),
        P(("rep", "tm"), None),
    )
    out_specs = (
        P(("rep", "tm"), None),
        P(("rep", "tm"), None),
        P(("rep", "tm"), None),
        P(("rep", "tm"), None),
        P(("rep", "tm"), None),
    )
    return jax.shard_map(shards, mesh=mesh, in_specs=in_specs, out_specs=out_specs, check_vma=False)
```

```python
import functools

import jax
import jax.numpy as jnp
from jax import lax
from jax.experimental import pallas as pl
from jax.experimental.pallas import tpu as pltpu
from jax.sharding import PartitionSpec as P


HD = 64
W = 16
GROUP = 4
LANES = GROUP * HD
CALLS = 2
CHUNK = 256
F32 = jnp.float32
BF16 = jnp.bfloat16


def tn_dot(a, b):
    return lax.dot_general(a, b, (((0,), (0,)), ((), ())), preferred_element_type=F32)


def nt_dot(a, b):
    return lax.dot_general(a, b, (((1,), (1,)), ((), ())), preferred_element_type=F32)


def nn_dot(a, b):
    return jnp.dot(a, b, preferred_element_type=F32)


def own_head(n_query):
    wide = GROUP * n_query
    row_head = lax.broadcasted_iota(jnp.int32, (wide, LANES), 0) // (n_query // 2) % GROUP
    col_head = lax.broadcasted_iota(jnp.int32, (wide, LANES), 1) // HD
    return row_head == col_head


def spread(x, own):
    part = x.shape[0] // 2
    rows = jnp.concatenate([x[:part]] * GROUP + [x[part:]] * GROUP, 0)
    return jnp.where(own, rows, jnp.zeros_like(rows))


def scaled(x):
    return (x.astype(F32) * HD ** (-0.5)).astype(BF16)


def fill_bias(lo_ref, hi_ref, bias_ref, n_query):
    wide = GROUP * n_query
    lo = lo_ref[...]
    hi = hi_ref[...]
    rows = lax.broadcasted_iota(jnp.int32, (CHUNK, wide), 0)
    near = rows % W
    second = lax.broadcasted_iota(jnp.int32, (CHUNK, wide), 1) >= wide // 2
    frames = (
        near + jnp.where(second, n_query - W, 0),
        near + W,
        near + 2 * W,
        near + jnp.where(second, n_query, -W),
    )
    for i, frame in enumerate(frames):
        bias_ref[i] = jnp.where((frame >= lo) & (frame <= hi), 0.0, -1e30)


def load(ref, side):
    return ref[:, side].reshape(CHUNK, LANES)


def pair_dot(ref, x_ref):
    mid = x_ref.shape[0] // 2
    return jnp.concatenate(
        [nt_dot(load(ref, 0), x_ref[:mid, :]), nt_dot(load(ref, 1), x_ref[mid:, :])], 1
    )


def fold(x):
    return x.reshape(CHUNK // 8, 8, x.shape[1])


def stats_kernel(
    lo_ref, hi_ref, q_ref, g_ref, ke_ref, km_ref, kh_ref, ve_ref, vm_ref, vh_ref,
    out_ref, s_ref, bias_ref, bq_ref, bg_ref,
):
    n_query = q_ref.shape[0]
    wide = GROUP * n_query
    own = own_head(n_query)
    bq_ref[...] = scaled(spread(q_ref[...], own))
    bg_ref[...] = scaled(spread(g_ref[...], own))

    @pl.when(pl.program_id(1) == 0)
    def _():
        fill_bias(lo_ref, hi_ref, bias_ref, n_query)

    def score(at, s, top):
        s = s + bias_ref[at]
        s_ref[at] = s
        return jnp.maximum(top, jnp.max(fold(s), axis=0))

    top = jnp.full((8, wide), -1e30, F32)
    top = score(0, pair_dot(ke_ref, bq_ref), top)
    for c in range(2):
        top = score(1 + c, nt_dot(load(km_ref, c), bq_ref[...]), top)
    top = score(3, pair_dot(kh_ref, bq_ref), top)
    top = jnp.max(top, axis=0, keepdims=True)

    total = jnp.zeros((8, wide), F32)
    weighted = jnp.zeros((8, wide), F32)
    for c in range(4):
        if c == 0:
            dp = pair_dot(ve_ref, bg_ref)
        elif c == 3:
            dp = pair_dot(vh_ref, bg_ref)
        else:
            dp = nt_dot(load(vm_ref, c - 1), bg_ref[...])
        e = jnp.exp(s_ref[c] - top)
        total = total + jnp.sum(fold(e), axis=0)
        weighted = weighted + jnp.sum(fold(e * dp), axis=0)
    out_ref[0:1, :] = top
    out_ref[1:2, :] = jnp.sum(total, axis=0, keepdims=True)
    out_ref[2:3, :] = jnp.sum(weighted, axis=0, keepdims=True)


def grads_kernel(
    lo_ref, hi_ref, one_ref, two_ref, q_ref, g_ref,
    ke_ref, km_ref, kh_ref, ve_ref, vm_ref, vh_ref,
    ctx_ref, dq_ref, part_ref,
    bias_ref, bq_ref, bg_ref, bqs_ref, bgs_ref, acc_ctx, acc_dq,
):
    n_query = q_ref.shape[0]
    part = n_query // 2
    wide = GROUP * n_query
    mid = wide // 2
    own = own_head(n_query)
    bq_ref[...] = spread(q_ref[...], own)
    bg_ref[...] = spread(g_ref[...], own)
    bqs_ref[...] = scaled(bq_ref[...])
    bgs_ref[...] = scaled(bg_ref[...])

    @pl.when(pl.program_id(1) == 0)
    def _():
        fill_bias(lo_ref, hi_ref, bias_ref, n_query)

    top = jnp.maximum(one_ref[0:1, :], two_ref[0:1, :])
    one = jnp.exp(one_ref[0:1, :] - top)
    two = jnp.exp(two_ref[0:1, :] - top)
    inverse = 1.0 / (one_ref[1:2, :] * one + two_ref[1:2, :] * two)
    mean = (one_ref[2:3, :] * one + two_ref[2:3, :] * two) * inverse
    acc_ctx[...] = jnp.zeros_like(acc_ctx)
    acc_dq[...] = jnp.zeros_like(acc_dq)

    def soft(table, s, dp):
        p = jnp.exp(s + bias_ref[table] - top) * inverse
        return p.astype(BF16), (p * (dp - mean)).astype(BF16)

    shape = part_ref.shape[1:2] + part_ref.shape[3:5] + (LANES,)

    def keep(section, side, kp, vp):
        part_ref[section, :, side, :, :, :LANES] = kp.astype(BF16).reshape(shape)
        part_ref[section, :, side, :, :, LANES:] = vp.astype(BF16).reshape(shape)

    def pair(k_ref, v_ref, section, table):
        pb, ds = soft(table, pair_dot(k_ref, bqs_ref), pair_dot(v_ref, bgs_ref))
        for side, lanes in ((0, slice(0, mid)), (1, slice(mid, wide))):
            acc_ctx[lanes, :] += tn_dot(pb[:, lanes], load(v_ref, side))
            acc_dq[lanes, :] += tn_dot(ds[:, lanes], load(k_ref, side))
            keep(
                section, side,
                nn_dot(ds[:, lanes], bq_ref[lanes, :]), nn_dot(pb[:, lanes], bg_ref[lanes, :]),
            )

    pair(ke_ref, ve_ref, 0, 0)

    def middle(c, carry):
        k = load(km_ref, c)
        v = load(vm_ref, c)
        pb, ds = soft(1 + c, nt_dot(k, bqs_ref[...]), nt_dot(v, bgs_ref[...]))
        acc_ctx[...] += tn_dot(pb, v)
        acc_dq[...] += tn_dot(ds, k)
        keep(1, c, nn_dot(ds, bq_ref[...]), nn_dot(pb, bg_ref[...]))
        return carry

    lax.fori_loop(0, 2, middle, 0)
    pair(kh_ref, vh_ref, 2, 3)

    def diagonal(acc, out_ref):
        kept = jnp.where(own, acc, 0.0)
        for i in range(2):
            rows = [kept[(i * GROUP + h) * part : (i * GROUP + h + 1) * part] for h in range(GROUP)]
            out_ref[i * part : (i + 1) * part, :] = functools.reduce(jnp.add, rows)

    diagonal(acc_ctx[...], ctx_ref)
    diagonal(acc_dq[...], dq_ref)


def attention(first_group, groups, lo, hi, stats, queries, d_context, tokens):
    n_query, width = queries.shape[1:]
    src, _, tok = tokens[0].shape[:3]
    wide = GROUP * n_query
    flat = pl.BlockSpec((None, 1, wide), lambda b, g: (b, 0, 0))
    rows = pl.BlockSpec((None, n_query, LANES), lambda b, g: (b, 0, first_group + g))
    table = pl.BlockSpec((None, None, 3, wide), lambda b, g: (b, first_group + g, 0, 0))

    def section(first):
        shape = (src, 2, tok, None, W, LANES)
        return pl.BlockSpec(shape, lambda b, g: (0, 0, 0, b, 0, first + g))

    sections = [section(first_group)] * 3 + [section(width // LANES + first_group)] * 3
    operand = pltpu.VMEM((wide, LANES), BF16)
    total = pltpu.VMEM((wide, LANES), F32)
    bias = pltpu.VMEM((4, CHUNK, wide), F32)
    scores = 8 * CHUNK * wide * groups
    common = dict(
        grid=(2, groups),
        compiler_params=pltpu.CompilerParams(dimension_semantics=("arbitrary", "arbitrary")),
    )
    if stats is None:
        return pl.pallas_call(
            stats_kernel,
            in_specs=[flat, flat, rows, rows] + sections,
            out_specs=table,
            out_shape=jax.ShapeDtypeStruct((2, groups, 3, wide), F32),
            scratch_shapes=[pltpu.VMEM((4, CHUNK, wide), F32), bias, operand, operand],
            cost_estimate=pl.CostEstimate(
                flops=4 * scores * LANES, bytes_accessed=6 * scores, transcendentals=scores
            ),
            name="softmax_stats",
            **common,
        )(lo, hi, queries, d_context, *tokens, *tokens)

    parts = pl.BlockSpec(
        (3, src, 2, tok, None, W, 2 * LANES), lambda b, g: (0, 0, 0, 0, b, 0, g)
    )
    partial = jax.ShapeDtypeStruct((2, n_query, groups * LANES), F32)
    partial_spec = pl.BlockSpec((None, n_query, LANES), lambda b, g: (b, 0, g))
    return pl.pallas_call(
        grads_kernel,
        in_specs=[flat, flat, table, table, rows, rows] + sections,
        out_specs=[partial_spec, partial_spec, parts],
        out_shape=[
            partial,
            partial,
            jax.ShapeDtypeStruct((3, src, 2, tok, 2, W, 2 * groups * LANES), BF16),
        ],
        scratch_shapes=[bias] + [operand] * 4 + [total] * 2,
        cost_estimate=pl.CostEstimate(
            flops=12 * scores * LANES, bytes_accessed=12 * scores, transcendentals=scores
        ),
        name="banded_grads",
        **common,
    )(lo, hi, *stats, queries, d_context, *tokens, *tokens)


class ScatterSum:
    def __init__(self, term, bits, order):
        self.order = list(order)
        self.left = list(range(bits - 1, -1, -1))
        self.block = term.reshape([2] * bits + [term.shape[0] >> bits, term.shape[1]])

    def send(self):
        bit = self.order.pop(0)
        axis = self.left.index(bit)
        self.left.remove(bit)
        mine = (lax.axis_index("tm") >> bit) & 1
        away = lax.dynamic_index_in_dim(self.block, 1 - mine, axis, keepdims=False)
        self.keep = lax.dynamic_index_in_dim(self.block, mine, axis, keepdims=False)
        return away, 1 << bit

    def receive(self, come):
        block = self.keep.astype(F32) + come.astype(F32)
        self.block = block.astype(BF16) if self.left else block


class Gather:
    def __init__(self, block, bits):
        self.block = block
        self.order = list(range(bits - 1, -1, -1))

    def send(self):
        return self.block, 1 << self.order.pop(0)

    def receive(self, come):
        self.block = jnp.concatenate([self.block, come], axis=0)


class Swap:
    def __init__(self, block, bit):
        self.block = block
        self.order = [bit]

    def send(self):
        return self.block, 1 << self.order.pop(0)

    def receive(self, come):
        self.come = come


def beside(moving, work, *args):
    n_dev = lax.axis_size("tm")
    moving = [m for m in moving if m.order]
    sends = [m.send() for m in moving]
    args, aways = lax.optimization_barrier((args, [away for away, _ in sends]))
    comes = [
        lax.ppermute(away, "tm", [(i, i ^ step) for i in range(n_dev)])
        for away, (_, step) in zip(aways, sends)
    ]
    result, comes = lax.optimization_barrier((work(*args), comes))
    for m, come in zip(moving, comes):
        m.receive(come)
    return result


def shards(
    exo_tokens, queries, key_weight, value_weight, out_weight, gaze_valid, window_offset, cotangent
):
    n_query, width = queries.shape
    tok = exo_tokens.shape[1]
    n_dev = lax.axis_size("tm")
    bits = n_dev.bit_length() - 1
    src = n_dev // 2
    total = n_query * n_dev
    me = lax.axis_index("tm")
    upper_half = me >= src
    spot = me % src

    fence = lax.optimization_barrier
    valid_col = gaze_valid.astype(F32)[:, None]
    masked_grad = (cotangent.astype(F32) * valid_col).astype(BF16)
    far = bits - 1
    gather = Gather(masked_grad, bits)
    swap_q, swap_o = Swap(queries, far), Swap(window_offset, far)

    def frames(exo, *cuts):
        by_block = exo.reshape(2, src, n_query, tok, width)
        runs = jnp.stack([by_block[:, :, cut : cut + W] for cut in cuts], axis=2)
        return runs.transpose(1, 2, 4, 0, 3, 5)

    later = fence(exo_tokens)
    outer = beside(
        [gather, swap_q, swap_o], lambda exo: frames(exo, 0, n_query - W), exo_tokens
    )
    inner = frames(later, W, 2 * W)
    halves = [list(range(src)), list(range(src, n_dev))]
    edge = lax.all_to_all(outer, "tm", 0, 0, axis_index_groups=halves, tiled=True)

    def both(own, other):
        return jnp.where(upper_half, jnp.stack([other, own]), jnp.stack([own, other]))

    q_pair = both(queries, swap_q.come)
    d_context = nt_dot(gather.block, out_weight).astype(BF16)
    g_pair = both(d_context[:n_query], d_context[n_query:])
    offsets = both(window_offset, swap_o.come)
    at = jnp.arange(n_query, dtype=jnp.int32)
    first = (spot + jnp.array([0, src], jnp.int32))[:, None] * n_query
    lower = jnp.maximum(at - W + offsets, -first)
    upper = jnp.minimum(at + offsets, total - 1 - first)

    def lanes(x):
        return jnp.tile(x.reshape(2, 2, 1, n_query // 2), (1, 1, GROUP, 1)).reshape(2, 1, -1)

    lo, hi = lanes(lower), lanes(upper)
    weights = jnp.concatenate([key_weight, value_weight], axis=1)
    edge, inner, q_pair, g_pair, lo, hi, weights = fence(
        (edge, inner, q_pair, g_pair, lo, hi, weights)
    )

    def project(x):
        flat = nn_dot(x.reshape(-1, width), weights).astype(BF16)
        return flat.reshape(x.shape[:-1] + (2 * width,))

    low = jnp.where(spot == src - 1, jnp.flip(edge[:, 1], 2), edge[:, 1])
    high = jnp.where(spot == 0, jnp.flip(edge[:, 0], 2), edge[:, 0])
    low, high, inner = fence((low, high, inner))
    ring = [(i, i // src * src + (i + 1) % src) for i in range(n_dev)]
    low = lax.ppermute(low, "tm", ring)
    high = lax.ppermute(high, "tm", [(target, source) for source, target in ring])
    middle = lax.all_to_all(inner, "tm", 0, 0, axis_index_groups=halves, tiled=True)
    edge_kv, low, high = fence((project(edge), low, high))
    halo = jnp.stack([low, high], axis=1)
    halo_kv, middle = fence((project(halo), middle))
    middle_kv = beside([gather], project, middle)
    tokens = (edge_kv, middle_kv, halo_kv)

    groups = width // LANES // CALLS
    stats = beside(
        [gather],
        functools.partial(attention, 0, width // LANES, lo, hi, None),
        q_pair, g_pair, tokens,
    )
    swap = Swap(stats, far)
    sources = beside(
        [gather, swap],
        lambda *x: jnp.concatenate([y.reshape(-1, width) for y in x], axis=0),
        edge, middle, halo,
    )

    def own_part(x):
        return jnp.where(upper_half, x[1], x[0])

    def other_part(x):
        return jnp.where(upper_half, x[0], x[1])

    moving = [gather]
    owns, trades, shares = [], [], []
    for call in range(CALLS):
        work = functools.partial(attention, call * groups, groups, lo, hi, (swap.block, swap.come))
        context, d_query, grads = beside(moving, work, q_pair, g_pair, tokens)
        owns.append(jnp.stack([own_part(context), own_part(d_query)]))
        trades.append(Swap(jnp.stack([other_part(context), other_part(d_query)]), far))
        moving.append(trades[-1])
        term = beside(
            moving,
            lambda g: tn_dot(sources, g.reshape(sources.shape[0], -1)).astype(BF16),
            grads,
        )
        shares.append(ScatterSum(term, bits, range(bits)))
        moving.append(shares[-1])

    pairs = [own + trade.come for own, trade in zip(owns, trades)]
    context = jnp.concatenate([x[0] for x in pairs], axis=1).astype(BF16)
    d_query = jnp.concatenate([x[1] for x in pairs], axis=1).astype(BF16)

    def finish(context):
        attended = (nn_dot(context, out_weight) * valid_col).astype(BF16)
        columns = context.reshape(n_query, n_dev, -1).swapaxes(0, 1)
        return attended, lax.all_to_all(columns, "tm", split_axis=0, concat_axis=0, tiled=True)

    attended, columns = beside(moving, finish, context)
    columns = columns.reshape([2] * bits + [n_query, -1])
    for bit in range(bits):
        axis = bits - 1 - bit
        columns = jnp.where((me >> bit) & 1 == 1, jnp.flip(columns, axis), columns)
    columns = columns.transpose(list(range(bits - 1, -1, -1)) + [bits, bits + 1])
    d_out = beside(moving, lambda c: tn_dot(c.reshape(total, -1), gather.block), columns)
    while any(m.order for m in moving):
        beside(moving, lambda: ())
    blocks = [s.block.reshape(s.block.shape[0], -1, 2, LANES) for s in shares]
    return (
        attended,
        d_query,
        jnp.concatenate([b[:, i, 0] for b in blocks for i in range(b.shape[1])], axis=1),
        jnp.concatenate([b[:, i, 1] for b in blocks for i in range(b.shape[1])], axis=1),
        d_out,
    )


def solution(mesh):
    in_specs = (
        P("rep", "tm", None),
        P(("rep", "tm"), None),
        P(),
        P(),
        P(),
        P(("rep", "tm")),
        P(("rep", "tm")),
        P(("rep", "tm"), None),
    )
    out_specs = (
        P(("rep", "tm"), None),
        P(("rep", "tm"), None),
        P(("rep", "tm"), None),
        P(("rep", "tm"), None),
        P(("rep", "tm"), None),
    )

    return jax.shard_map(shards, mesh=mesh, in_specs=in_specs, out_specs=out_specs, check_vma=False)
```

```python
import functools

import jax
import jax.numpy as jnp
from jax import lax
from jax.experimental import pallas as pl
from jax.experimental.pallas import tpu as pltpu
from jax.sharding import PartitionSpec as P


HD = 64
W = 16
GROUP = 4
LANES = GROUP * HD
CALLS = 2
CHUNK = 256
F32 = jnp.float32
BF16 = jnp.bfloat16


def tn_dot(a, b):
    return lax.dot_general(a, b, (((0,), (0,)), ((), ())), preferred_element_type=F32)


def nt_dot(a, b):
    return lax.dot_general(a, b, (((1,), (1,)), ((), ())), preferred_element_type=F32)


def nn_dot(a, b):
    return jnp.dot(a, b, preferred_element_type=F32)


def own_head(n_query):
    wide = GROUP * n_query
    row_head = lax.broadcasted_iota(jnp.int32, (wide, LANES), 0) // (n_query // 2) % GROUP
    col_head = lax.broadcasted_iota(jnp.int32, (wide, LANES), 1) // HD
    return row_head == col_head


def spread(x, own):
    part = x.shape[0] // 2
    rows = jnp.concatenate([x[:part]] * GROUP + [x[part:]] * GROUP, 0)
    return jnp.where(own, rows, jnp.zeros_like(rows))


def scaled(x):
    return (x.astype(F32) * HD ** (-0.5)).astype(BF16)


def fill_bias(lo_ref, hi_ref, bias_ref, n_query):
    wide = GROUP * n_query
    lo = lo_ref[...]
    hi = hi_ref[...]
    rows = lax.broadcasted_iota(jnp.int32, (CHUNK, wide), 0)
    near = rows % W
    second = lax.broadcasted_iota(jnp.int32, (CHUNK, wide), 1) >= wide // 2
    frames = (
        near + jnp.where(second, n_query - W, 0),
        near + W,
        near + 2 * W,
        near + jnp.where(second, n_query, -W),
    )
    for i, frame in enumerate(frames):
        bias_ref[i] = jnp.where((frame >= lo) & (frame <= hi), 0.0, -1e30)


def load(ref, side):
    return ref[:, side].reshape(CHUNK, LANES)


def sides(ref):
    return load(ref, 0), load(ref, 1)


def halo_sides(near_ref, far_ref):
    lower = pl.program_id(0) == 0
    return (
        jnp.where(lower, load(far_ref, 0), load(near_ref, 1)),
        jnp.where(lower, load(near_ref, 0), load(far_ref, 1)),
    )


def pair_dot(rows, x_ref):
    mid = x_ref.shape[0] // 2
    return jnp.concatenate([nt_dot(rows[0], x_ref[:mid, :]), nt_dot(rows[1], x_ref[mid:, :])], 1)


def fold(x):
    return x.reshape(CHUNK // 8, 8, x.shape[1])


def stats_kernel(
    lo_ref, hi_ref, q_ref, g_ref,
    ke_ref, km_ref, kn_ref, kf_ref, ve_ref, vm_ref, vn_ref, vf_ref,
    out_ref, s_ref, bias_ref, bq_ref, bg_ref,
):
    n_query = q_ref.shape[0]
    wide = GROUP * n_query
    own = own_head(n_query)
    bq_ref[...] = scaled(spread(q_ref[...], own))
    bg_ref[...] = scaled(spread(g_ref[...], own))

    @pl.when(pl.program_id(1) == 0)
    def _():
        fill_bias(lo_ref, hi_ref, bias_ref, n_query)

    def score(at, s, top):
        s = s + bias_ref[at]
        s_ref[at] = s
        return jnp.maximum(top, jnp.max(fold(s), axis=0))

    top = jnp.full((8, wide), -1e30, F32)
    top = score(0, pair_dot(sides(ke_ref), bq_ref), top)
    for c in range(2):
        top = score(1 + c, nt_dot(load(km_ref, c), bq_ref[...]), top)
    top = score(3, pair_dot(halo_sides(kn_ref, kf_ref), bq_ref), top)
    top = jnp.max(top, axis=0, keepdims=True)

    total = jnp.zeros((8, wide), F32)
    weighted = jnp.zeros((8, wide), F32)
    for c in range(4):
        if c == 0:
            dp = pair_dot(sides(ve_ref), bg_ref)
        elif c == 3:
            dp = pair_dot(halo_sides(vn_ref, vf_ref), bg_ref)
        else:
            dp = nt_dot(load(vm_ref, c - 1), bg_ref[...])
        e = jnp.exp(s_ref[c] - top)
        total = total + jnp.sum(fold(e), axis=0)
        weighted = weighted + jnp.sum(fold(e * dp), axis=0)
    out_ref[0:1, :] = top
    out_ref[1:2, :] = jnp.sum(total, axis=0, keepdims=True)
    out_ref[2:3, :] = jnp.sum(weighted, axis=0, keepdims=True)


def grads_kernel(
    lo_ref, hi_ref, one_ref, two_ref, q_ref, g_ref,
    ke_ref, km_ref, kn_ref, kf_ref, ve_ref, vm_ref, vn_ref, vf_ref,
    out_ref, part_ref,
    bias_ref, bq_ref, bg_ref, bqs_ref, bgs_ref, acc_ctx, acc_dq,
):
    n_query = q_ref.shape[0]
    part = n_query // 2
    wide = GROUP * n_query
    mid = wide // 2
    own = own_head(n_query)
    bq_ref[...] = spread(q_ref[...], own)
    bg_ref[...] = spread(g_ref[...], own)
    bqs_ref[...] = scaled(bq_ref[...])
    bgs_ref[...] = scaled(bg_ref[...])

    @pl.when(pl.program_id(1) == 0)
    def _():
        fill_bias(lo_ref, hi_ref, bias_ref, n_query)

    top = jnp.maximum(one_ref[0:1, :], two_ref[0:1, :])
    one = jnp.exp(one_ref[0:1, :] - top)
    two = jnp.exp(two_ref[0:1, :] - top)
    inverse = 1.0 / (one_ref[1:2, :] * one + two_ref[1:2, :] * two)
    mean = (one_ref[2:3, :] * one + two_ref[2:3, :] * two) * inverse
    acc_ctx[...] = jnp.zeros_like(acc_ctx)
    acc_dq[...] = jnp.zeros_like(acc_dq)

    def soft(table, s, dp):
        p = jnp.exp(s + bias_ref[table] - top) * inverse
        return p.astype(BF16), (p * (dp - mean)).astype(BF16)

    shape = part_ref.shape[1:2] + part_ref.shape[3:5] + (LANES,)

    def keep(section, side, kp, vp):
        part_ref[section, :, side, :, :, :LANES] = kp.astype(BF16).reshape(shape)
        part_ref[section, :, side, :, :, LANES:] = vp.astype(BF16).reshape(shape)

    def pair(k, v, section, table):
        pb, ds = soft(table, pair_dot(k, bqs_ref), pair_dot(v, bgs_ref))
        for side, lanes in ((0, slice(0, mid)), (1, slice(mid, wide))):
            acc_ctx[lanes, :] += tn_dot(pb[:, lanes], v[side])
            acc_dq[lanes, :] += tn_dot(ds[:, lanes], k[side])
            keep(
                section, side,
                nn_dot(ds[:, lanes], bq_ref[lanes, :]), nn_dot(pb[:, lanes], bg_ref[lanes, :]),
            )

    pair(sides(ke_ref), sides(ve_ref), 0, 0)

    def middle(c, carry):
        k = load(km_ref, c)
        v = load(vm_ref, c)
        pb, ds = soft(1 + c, nt_dot(k, bqs_ref[...]), nt_dot(v, bgs_ref[...]))
        acc_ctx[...] += tn_dot(pb, v)
        acc_dq[...] += tn_dot(ds, k)
        keep(1, c, nn_dot(ds, bq_ref[...]), nn_dot(pb, bg_ref[...]))
        return carry

    lax.fori_loop(0, 2, middle, 0)
    pair(halo_sides(kn_ref, kf_ref), halo_sides(vn_ref, vf_ref), 2, 3)

    def diagonal(acc, which):
        kept = jnp.where(own, acc, 0.0)
        for i in range(2):
            rows = [kept[(i * GROUP + h) * part : (i * GROUP + h + 1) * part] for h in range(GROUP)]
            out_ref[which, i * part : (i + 1) * part, :] = functools.reduce(jnp.add, rows)

    diagonal(acc_ctx[...], 0)
    diagonal(acc_dq[...], 1)


def attention(first_group, groups, lo, hi, stats, queries, d_context, tokens):
    n_query, width = queries.shape[1:]
    src, _, tok = tokens[0].shape[:3]
    wide = GROUP * n_query
    flat = pl.BlockSpec((None, 1, wide), lambda b, g: (b, 0, 0))
    rows = pl.BlockSpec((None, n_query, LANES), lambda b, g: (b, 0, first_group + g))
    table = pl.BlockSpec((None, None, 3, wide), lambda b, g: (b, first_group + g, 0, 0))

    def section(first, block):
        shape = (src, 2, tok, None, W, LANES)
        return pl.BlockSpec(shape, lambda b, g: (0, 0, 0, block(b), 0, first + g))

    def sections(first):
        far = pl.BlockSpec((src, 2, tok, W, LANES), lambda b, g: (0, 0, 0, 0, first + g))
        return [section(first, lambda b: b)] * 2 + [section(first, lambda b: 1 - b), far]

    edge, middle, ext = tokens
    tokens = (edge, middle, edge, ext)
    sections = sections(first_group) + sections(width // LANES + first_group)
    operand = pltpu.VMEM((wide, LANES), BF16)
    total = pltpu.VMEM((wide, LANES), F32)
    bias = pltpu.VMEM((4, CHUNK, wide), F32)
    scores = 8 * CHUNK * wide * groups
    common = dict(
        grid=(2, groups),
        compiler_params=pltpu.CompilerParams(dimension_semantics=("arbitrary", "arbitrary")),
    )
    if stats is None:
        return pl.pallas_call(
            stats_kernel,
            in_specs=[flat, flat, rows, rows] + sections,
            out_specs=table,
            out_shape=jax.ShapeDtypeStruct((2, groups, 3, wide), F32),
            scratch_shapes=[pltpu.VMEM((4, CHUNK, wide), F32), bias, operand, operand],
            cost_estimate=pl.CostEstimate(
                flops=4 * scores * LANES, bytes_accessed=6 * scores, transcendentals=scores
            ),
            name="softmax_stats",
            **common,
        )(lo, hi, queries, d_context, *tokens, *tokens)

    parts = pl.BlockSpec(
        (3, src, 2, tok, None, W, 2 * LANES), lambda b, g: (0, 0, 0, 0, b, 0, g)
    )
    return pl.pallas_call(
        grads_kernel,
        in_specs=[flat, flat, table, table, rows, rows] + sections,
        out_specs=[
            pl.BlockSpec((None, 2, n_query, LANES), lambda b, g: (b, 0, 0, g)),
            parts,
        ],
        out_shape=[
            jax.ShapeDtypeStruct((2, 2, n_query, groups * LANES), F32),
            jax.ShapeDtypeStruct((3, src, 2, tok, 2, W, 2 * groups * LANES), BF16),
        ],
        scratch_shapes=[bias] + [operand] * 4 + [total] * 2,
        cost_estimate=pl.CostEstimate(
            flops=12 * scores * LANES, bytes_accessed=12 * scores, transcendentals=scores
        ),
        name="banded_grads",
        **common,
    )(lo, hi, *stats, queries, d_context, *tokens, *tokens)


def flips(n_dev, bit):
    return [(i, i ^ (1 << bit)) for i in range(n_dev)]


class ScatterSum:
    def __init__(self, term, bits):
        self.order = list(range(bits))
        self.left = list(range(bits - 1, -1, -1))
        self.n_dev = 1 << bits
        self.block = term.reshape([2] * bits + [term.shape[0] >> bits, term.shape[1]])

    def send(self):
        bit = self.order.pop(0)
        axis = self.left.index(bit)
        self.left.remove(bit)
        mine = (lax.axis_index("tm") >> bit) & 1
        away = lax.dynamic_index_in_dim(self.block, 1 - mine, axis, keepdims=False)
        self.keep = lax.dynamic_index_in_dim(self.block, mine, axis, keepdims=False)
        return away, flips(self.n_dev, bit)

    def receive(self, come):
        block = self.keep.astype(F32) + come.astype(F32)
        self.block = block.astype(BF16) if self.left else block


class Gather:
    def __init__(self, block, bits):
        self.block = block
        self.n_dev = 1 << bits
        self.order = list(range(bits - 1, -1, -1))

    def send(self):
        return self.block, flips(self.n_dev, self.order.pop(0))

    def receive(self, come):
        self.block = jnp.concatenate([self.block, come], axis=0)


class Move:
    def __init__(self, block, perm):
        self.block = block
        self.order = [perm]

    def send(self):
        return self.block, self.order.pop(0)

    def receive(self, come):
        self.come = come


def beside(moving, work, *args):
    moving = [m for m in moving if m.order]
    sends = [m.send() for m in moving]
    args, aways = lax.optimization_barrier((args, [away for away, _ in sends]))
    comes = [lax.ppermute(away, "tm", perm) for away, (_, perm) in zip(aways, sends)]
    result, comes = lax.optimization_barrier((work(*args), comes))
    for m, come in zip(moving, comes):
        m.receive(come)
    return result


def shards(
    exo_tokens, queries, key_weight, value_weight, out_weight, gaze_valid, window_offset, cotangent
):
    n_query, width = queries.shape
    tok = exo_tokens.shape[1]
    n_dev = lax.axis_size("tm")
    bits = n_dev.bit_length() - 1
    src = n_dev // 2
    total = n_query * n_dev
    me = lax.axis_index("tm")
    upper_half = me >= src
    spot = me % src
    fence = lax.optimization_barrier

    owner_one = [(s, 2 * s) for s in range(src)] + [(src + s, 2 * s + 1) for s in range(src)]
    owner_two = [(s, 2 * s + 1) for s in range(src)] + [(src + s, 2 * s) for s in range(src)]
    valid_col = gaze_valid.astype(F32)[:, None]
    masked_grad = (cotangent.astype(F32) * valid_col).astype(BF16)
    note = jnp.zeros((W, width), BF16).at[0, :n_query].set(window_offset.astype(BF16))
    letter = jnp.concatenate([queries, masked_grad, note], axis=0)
    one = lax.ppermute(letter, "tm", [(b, a) for a, b in owner_one])
    two = lax.ppermute(letter, "tm", [(b, a) for a, b in owner_two])

    def frames(exo, *cuts):
        by_block = exo.reshape(src, 2, n_query, tok, width)
        runs = jnp.stack([by_block[:, :, cut : cut + W] for cut in cuts], axis=1)
        return runs.transpose(0, 1, 4, 2, 3, 5)

    later = fence(exo_tokens)
    outer = frames(exo_tokens, 0, n_query - W)
    inner = frames(later, W, 2 * W)
    halves = [list(range(src)), list(range(src, n_dev))]
    edge = lax.all_to_all(outer, "tm", 0, 0, axis_index_groups=halves, tiled=True)
    weights = jnp.concatenate([key_weight, value_weight], axis=1)
    edge, inner, weights = fence((edge, inner, weights))
    middle = lax.all_to_all(inner, "tm", 0, 0, axis_index_groups=halves, tiled=True)

    pair = jnp.where(upper_half, jnp.stack([two, one]), jnp.stack([one, two]))
    q_pair = pair[:, :n_query]
    g_pair = nt_dot(pair[:, n_query : 2 * n_query].reshape(-1, width), out_weight)
    g_pair = g_pair.astype(BF16).reshape(q_pair.shape)
    offsets = pair[:, 2 * n_query, :n_query].astype(jnp.int32)
    at = jnp.arange(n_query, dtype=jnp.int32)
    first = (2 * spot + jnp.arange(2, dtype=jnp.int32))[:, None] * n_query
    lower = jnp.maximum(at - W + offsets, -first)
    upper = jnp.minimum(at + offsets, total - 1 - first)

    def lanes(x):
        return jnp.tile(x.reshape(2, 2, 1, n_query // 2), (1, 1, GROUP, 1)).reshape(2, 1, -1)

    lo, hi = lanes(lower), lanes(upper)

    def project(x):
        flat = nn_dot(x.reshape(-1, width), weights).astype(BF16)
        return flat.reshape(x.shape[:-1] + (2 * width,))

    edge_kv = project(edge)
    up = [(i, i + 1) for i in range(n_dev - 1) if (i + 1) % src]
    low = Move(edge[:, 1, :, 1], up)
    high = Move(edge[:, 0, :, 0], [(target, source) for source, target in up])
    gather = Gather(masked_grad, bits)
    middle, edge_kv, q_pair, g_pair, lo, hi, low.block, high.block = fence(
        (middle, edge_kv, q_pair, g_pair, lo, hi, low.block, high.block)
    )
    middle_kv = beside([low, high, gather], project, middle)
    ext = jnp.stack([low.come, high.come], axis=1)
    ext_kv = beside([gather], project, ext)
    tokens = (edge_kv, middle_kv, ext_kv)

    groups = width // LANES // CALLS
    stats = beside(
        [gather],
        functools.partial(attention, 0, width // LANES, lo, hi, None),
        q_pair, g_pair, tokens,
    )
    swap = Move(stats, flips(n_dev, bits - 1))

    def all_sources(edge, middle, ext):
        below = jnp.stack([ext[:, 0], edge[:, 1, :, 0]], axis=2)
        above = jnp.stack([edge[:, 0, :, 1], ext[:, 1]], axis=2)
        halo = jnp.stack([below, above], axis=1)
        return jnp.concatenate([x.reshape(-1, width) for x in (edge, middle, halo)], axis=0)

    sources = beside([gather, swap], all_sources, edge, middle, ext)

    moving = [gather]
    trades, shares = [], []
    for call in range(CALLS):
        work = functools.partial(attention, call * groups, groups, lo, hi, (swap.block, swap.come))
        partial, grads = beside(moving, work, q_pair, g_pair, tokens)
        half = upper_half.astype(jnp.int32)
        trade = [
            Move(lax.dynamic_index_in_dim(partial, half, 0, keepdims=False), owner_one),
            Move(lax.dynamic_index_in_dim(partial, 1 - half, 0, keepdims=False), owner_two),
        ]
        trades.append(trade)
        moving += trade
        term = beside(
            moving,
            lambda g: tn_dot(sources, g.reshape(sources.shape[0], -1)).astype(BF16),
            grads,
        )
        shares.append(ScatterSum(term, bits))
        moving.append(shares[-1])

    def assemble(*parts):
        sums = [(a + b).astype(BF16) for a, b in zip(parts[::2], parts[1::2])]
        return jnp.concatenate(sums, axis=2)

    own = beside(moving, assemble, *[move.come for trade in trades for move in trade])
    context, d_query = own[0], own[1]

    def finish(context):
        attended = (nn_dot(context, out_weight) * valid_col).astype(BF16)
        columns = context.reshape(n_query, n_dev, -1).swapaxes(0, 1)
        return attended, lax.all_to_all(columns, "tm", split_axis=0, concat_axis=0, tiled=True)

    attended, columns = beside(moving, finish, context)
    columns = columns.reshape([2] * bits + [n_query, -1])
    for bit in range(bits):
        axis = bits - 1 - bit
        columns = jnp.where((me >> bit) & 1 == 1, jnp.flip(columns, axis), columns)
    columns = columns.transpose(list(range(bits - 1, -1, -1)) + [bits, bits + 1])
    d_out = beside(moving, lambda c: tn_dot(c.reshape(total, -1), gather.block), columns)
    while any(m.order for m in moving):
        beside(moving, lambda: ())
    blocks = [s.block.reshape(s.block.shape[0], -1, 2, LANES) for s in shares]
    return (
        attended,
        d_query,
        jnp.concatenate([b[:, i, 0] for b in blocks for i in range(b.shape[1])], axis=1),
        jnp.concatenate([b[:, i, 1] for b in blocks for i in range(b.shape[1])], axis=1),
        d_out,
    )


def solution(mesh):
    in_specs = (
        P("rep", "tm", None),
        P(("rep", "tm"), None),
        P(),
        P(),
        P(),
        P(("rep", "tm")),
        P(("rep", "tm")),
        P(("rep", "tm"), None),
    )
    out_specs = (
        P(("rep", "tm"), None),
        P(("rep", "tm"), None),
        P(("rep", "tm"), None),
        P(("rep", "tm"), None),
        P(("rep", "tm"), None),
    )

    return jax.shard_map(shards, mesh=mesh, in_specs=in_specs, out_specs=out_specs, check_vma=False)
```

```python
import functools

import jax
import jax.numpy as jnp
from jax import lax
from jax.experimental.layout import Layout, with_layout_constraint
from jax.experimental import pallas as pl
from jax.experimental.pallas import tpu as pltpu
from jax.sharding import PartitionSpec as P


HD = 64
W = 16
GROUP = 4
LANES = GROUP * HD
CALLS = 2
CHUNK = 256
F32 = jnp.float32
BF16 = jnp.bfloat16


def tn_dot(a, b):
    return lax.dot_general(a, b, (((0,), (0,)), ((), ())), preferred_element_type=F32)


def nt_dot(a, b):
    return lax.dot_general(a, b, (((1,), (1,)), ((), ())), preferred_element_type=F32)


def nn_dot(a, b):
    return jnp.dot(a, b, preferred_element_type=F32)


def own_head(n_query):
    wide = GROUP * n_query
    row_head = lax.broadcasted_iota(jnp.int32, (wide, LANES), 0) // (n_query // 2) % GROUP
    col_head = lax.broadcasted_iota(jnp.int32, (wide, LANES), 1) // HD
    return row_head == col_head


def spread(x, own):
    part = x.shape[0] // 2
    rows = jnp.concatenate([x[:part]] * GROUP + [x[part:]] * GROUP, 0)
    return jnp.where(own, rows, jnp.zeros_like(rows))


def scaled(x):
    return (x.astype(F32) * HD ** (-0.5)).astype(BF16)


def fill_bias(lo_ref, hi_ref, bias_ref, n_query):
    wide = GROUP * n_query
    lo = lo_ref[...]
    hi = hi_ref[...]
    rows = lax.broadcasted_iota(jnp.int32, (CHUNK, wide), 0)
    near = rows % W
    second = lax.broadcasted_iota(jnp.int32, (CHUNK, wide), 1) >= wide // 2
    frames = (
        near + jnp.where(second, n_query - W, 0),
        near + W,
        near + 2 * W,
        near + jnp.where(second, n_query, -W),
    )
    for i, frame in enumerate(frames):
        bias_ref[i] = jnp.where((frame >= lo) & (frame <= hi), 0.0, -1e30)


def load(ref, side):
    return ref[:, side].reshape(CHUNK, LANES)


def sides(ref):
    return load(ref, 0), load(ref, 1)


def halo_sides(near_ref, far_ref):
    lower = pl.program_id(0) == 0
    return (
        jnp.where(lower, load(far_ref, 0), load(near_ref, 1)),
        jnp.where(lower, load(near_ref, 0), load(far_ref, 1)),
    )


def pair_dot(rows, x_ref):
    mid = x_ref.shape[0] // 2
    return jnp.concatenate([nt_dot(rows[0], x_ref[:mid, :]), nt_dot(rows[1], x_ref[mid:, :])], 1)


def fold(x):
    return x.reshape(CHUNK // 8, 8, x.shape[1])


def stats_kernel(
    lo_ref, hi_ref, q_ref, g_ref,
    ke_ref, km_ref, kn_ref, kf_ref, ve_ref, vm_ref, vn_ref, vf_ref,
    out_ref, s_ref, bias_ref, bq_ref, bg_ref,
):
    n_query = q_ref.shape[0]
    wide = GROUP * n_query
    own = own_head(n_query)
    bq_ref[...] = scaled(spread(q_ref[...], own))
    bg_ref[...] = scaled(spread(g_ref[...], own))

    @pl.when(pl.program_id(1) == 0)
    def _():
        fill_bias(lo_ref, hi_ref, bias_ref, n_query)

    def score(at, s, top):
        s = s + bias_ref[at]
        s_ref[at] = s
        return jnp.maximum(top, jnp.max(fold(s), axis=0))

    top = jnp.full((8, wide), -1e30, F32)
    top = score(0, pair_dot(sides(ke_ref), bq_ref), top)
    for c in range(2):
        top = score(1 + c, nt_dot(load(km_ref, c), bq_ref[...]), top)
    top = score(3, pair_dot(halo_sides(kn_ref, kf_ref), bq_ref), top)
    top = jnp.max(top, axis=0, keepdims=True)

    total = jnp.zeros((8, wide), F32)
    weighted = jnp.zeros((8, wide), F32)
    for c in range(4):
        if c == 0:
            dp = pair_dot(sides(ve_ref), bg_ref)
        elif c == 3:
            dp = pair_dot(halo_sides(vn_ref, vf_ref), bg_ref)
        else:
            dp = nt_dot(load(vm_ref, c - 1), bg_ref[...])
        e = jnp.exp(s_ref[c] - top)
        total = total + jnp.sum(fold(e), axis=0)
        weighted = weighted + jnp.sum(fold(e * dp), axis=0)
    out_ref[0:1, :] = top
    out_ref[1:2, :] = jnp.sum(total, axis=0, keepdims=True)
    out_ref[2:3, :] = jnp.sum(weighted, axis=0, keepdims=True)


def grads_kernel(
    lo_ref, hi_ref, one_ref, two_ref, q_ref, g_ref,
    ke_ref, km_ref, kn_ref, kf_ref, ve_ref, vm_ref, vn_ref, vf_ref,
    out_ref, part_ref,
    bias_ref, bq_ref, bg_ref, bqs_ref, bgs_ref, acc_ctx, acc_dq,
):
    n_query = q_ref.shape[0]
    part = n_query // 2
    wide = GROUP * n_query
    mid = wide // 2
    own = own_head(n_query)
    bq_ref[...] = spread(q_ref[...], own)
    bg_ref[...] = spread(g_ref[...], own)
    bqs_ref[...] = scaled(bq_ref[...])
    bgs_ref[...] = scaled(bg_ref[...])

    @pl.when(pl.program_id(1) == 0)
    def _():
        fill_bias(lo_ref, hi_ref, bias_ref, n_query)

    top = jnp.maximum(one_ref[0:1, :], two_ref[0:1, :])
    one = jnp.exp(one_ref[0:1, :] - top)
    two = jnp.exp(two_ref[0:1, :] - top)
    inverse = 1.0 / (one_ref[1:2, :] * one + two_ref[1:2, :] * two)
    mean = (one_ref[2:3, :] * one + two_ref[2:3, :] * two) * inverse
    acc_ctx[...] = jnp.zeros_like(acc_ctx)
    acc_dq[...] = jnp.zeros_like(acc_dq)

    def soft(table, s, dp):
        p = jnp.exp(s + bias_ref[table] - top) * inverse
        return p.astype(BF16), (p * (dp - mean)).astype(BF16)

    shape = part_ref.shape[1:2] + part_ref.shape[3:5] + (LANES,)

    def keep(section, side, kp, vp):
        part_ref[section, :, side, :, :, :LANES] = kp.astype(BF16).reshape(shape)
        part_ref[section, :, side, :, :, LANES:] = vp.astype(BF16).reshape(shape)

    def pair(k, v, section, table):
        pb, ds = soft(table, pair_dot(k, bqs_ref), pair_dot(v, bgs_ref))
        for side, lanes in ((0, slice(0, mid)), (1, slice(mid, wide))):
            acc_ctx[lanes, :] += tn_dot(pb[:, lanes], v[side])
            acc_dq[lanes, :] += tn_dot(ds[:, lanes], k[side])
            keep(
                section, side,
                nn_dot(ds[:, lanes], bq_ref[lanes, :]), nn_dot(pb[:, lanes], bg_ref[lanes, :]),
            )

    pair(sides(ke_ref), sides(ve_ref), 0, 0)

    def middle(c, carry):
        k = load(km_ref, c)
        v = load(vm_ref, c)
        pb, ds = soft(1 + c, nt_dot(k, bqs_ref[...]), nt_dot(v, bgs_ref[...]))
        acc_ctx[...] += tn_dot(pb, v)
        acc_dq[...] += tn_dot(ds, k)
        keep(1, c, nn_dot(ds, bq_ref[...]), nn_dot(pb, bg_ref[...]))
        return carry

    lax.fori_loop(0, 2, middle, 0)
    pair(halo_sides(kn_ref, kf_ref), halo_sides(vn_ref, vf_ref), 2, 3)

    def diagonal(acc, which):
        kept = jnp.where(own, acc, 0.0)
        for i in range(2):
            rows = [kept[(i * GROUP + h) * part : (i * GROUP + h + 1) * part] for h in range(GROUP)]
            out_ref[which, i * part : (i + 1) * part, :] = functools.reduce(jnp.add, rows)

    diagonal(acc_ctx[...], 0)
    diagonal(acc_dq[...], 1)


def attention(first_group, groups, lo, hi, stats, queries, d_context, tokens):
    n_query, width = queries.shape[1:]
    src, _, tok = tokens[0].shape[:3]
    wide = GROUP * n_query
    flat = pl.BlockSpec((None, 1, wide), lambda b, g: (b, 0, 0))
    rows = pl.BlockSpec((None, n_query, LANES), lambda b, g: (b, 0, first_group + g))
    table = pl.BlockSpec((None, None, 3, wide), lambda b, g: (b, first_group + g, 0, 0))

    def section(first, block):
        shape = (src, 2, tok, None, W, LANES)
        return pl.BlockSpec(shape, lambda b, g: (0, 0, 0, block(b), 0, first + g))

    def sections(first):
        far = pl.BlockSpec((src, 2, tok, W, LANES), lambda b, g: (0, 0, 0, 0, first + g))
        return [section(first, lambda b: b)] * 2 + [section(first, lambda b: 1 - b), far]

    edge, middle, ext = tokens
    tokens = (edge, middle, edge, ext)
    sections = sections(first_group) + sections(width // LANES + first_group)
    operand = pltpu.VMEM((wide, LANES), BF16)
    total = pltpu.VMEM((wide, LANES), F32)
    bias = pltpu.VMEM((4, CHUNK, wide), F32)
    scores = 8 * CHUNK * wide * groups
    common = dict(
        grid=(2, groups),
        compiler_params=pltpu.CompilerParams(dimension_semantics=("arbitrary", "arbitrary")),
    )
    if stats is None:
        return pl.pallas_call(
            stats_kernel,
            in_specs=[flat, flat, rows, rows] + sections,
            out_specs=table,
            out_shape=jax.ShapeDtypeStruct((2, groups, 3, wide), F32),
            scratch_shapes=[pltpu.VMEM((4, CHUNK, wide), F32), bias, operand, operand],
            cost_estimate=pl.CostEstimate(
                flops=4 * scores * LANES, bytes_accessed=6 * scores, transcendentals=scores
            ),
            name="softmax_stats",
            **common,
        )(lo, hi, queries, d_context, *tokens, *tokens)

    parts = pl.BlockSpec(
        (3, src, 2, tok, None, W, 2 * LANES), lambda b, g: (0, 0, 0, 0, b, 0, g)
    )
    return pl.pallas_call(
        grads_kernel,
        in_specs=[flat, flat, table, table, rows, rows] + sections,
        out_specs=[
            pl.BlockSpec((None, 2, n_query, LANES), lambda b, g: (b, 0, 0, g)),
            parts,
        ],
        out_shape=[
            jax.ShapeDtypeStruct((2, 2, n_query, groups * LANES), F32),
            jax.ShapeDtypeStruct((3, src, 2, tok, 2, W, 2 * groups * LANES), BF16),
        ],
        scratch_shapes=[bias] + [operand] * 4 + [total] * 2,
        cost_estimate=pl.CostEstimate(
            flops=12 * scores * LANES, bytes_accessed=12 * scores, transcendentals=scores
        ),
        name="banded_grads",
        **common,
    )(lo, hi, *stats, queries, d_context, *tokens, *tokens)


def flips(n_dev, bit):
    return [(i, i ^ (1 << bit)) for i in range(n_dev)]


class Gather:
    def __init__(self, block, bits):
        self.block = block
        self.n_dev = 1 << bits
        self.order = list(range(bits - 1, -1, -1))

    def send(self):
        self.bit = self.order.pop(0)
        return self.block, flips(self.n_dev, self.bit)

    def receive(self, come):
        if self.bit == 0:
            self.block = jnp.stack([self.block, come])
            return
        mine = (lax.axis_index("tm") >> self.bit) & 1
        self.block = jnp.where(
            mine == 0,
            jnp.stack([self.block, come], axis=-3),
            jnp.stack([come, self.block], axis=-3),
        )


class Move:
    def __init__(self, block, perm):
        self.block = block
        self.order = [perm]

    def send(self):
        return self.block, self.order.pop(0)

    def receive(self, come):
        self.come = come


def beside(moving, work, *args):
    moving = [m for m in moving if m.order]
    sends = [m.send() for m in moving]
    args, aways = lax.optimization_barrier((args, [away for away, _ in sends]))
    comes = [lax.ppermute(away, "tm", perm) for away, (_, perm) in zip(aways, sends)]
    result, comes = lax.optimization_barrier((work(*args), comes))
    for m, come in zip(moving, comes):
        m.receive(come)
    return result


def shards(
    exo_tokens, queries, key_weight, value_weight, out_weight, gaze_valid, window_offset, cotangent
):
    n_query, width = queries.shape
    tok = exo_tokens.shape[1]
    n_dev = lax.axis_size("tm")
    bits = n_dev.bit_length() - 1
    src = n_dev // 2
    total = n_query * n_dev
    me = lax.axis_index("tm")
    upper_half = me >= src
    spot = me % src
    fence = lax.optimization_barrier

    owner_one = [(s, 2 * s) for s in range(src)] + [(src + s, 2 * s + 1) for s in range(src)]
    owner_two = [(s, 2 * s + 1) for s in range(src)] + [(src + s, 2 * s) for s in range(src)]
    valid_col = gaze_valid.astype(F32)[:, None]
    masked_grad = (cotangent.astype(F32) * valid_col).astype(BF16)
    note = jnp.zeros((W, width), BF16).at[0, :n_query].set(window_offset.astype(BF16))
    letter = jnp.concatenate([queries, masked_grad, note], axis=0)

    def frames(exo, *cuts):
        by_block = exo.reshape(src, 2, n_query, tok, width)
        runs = jnp.stack([by_block[:, :, cut : cut + W] for cut in cuts], axis=1)
        runs = runs.transpose(0, 1, 4, 2, 3, 5)
        return with_layout_constraint(runs, Layout(tuple(range(6))))

    later = fence(exo_tokens)
    outer = frames(exo_tokens, 0, n_query - W)
    inner = frames(later, W, 2 * W)
    halves = [list(range(src)), list(range(src, n_dev))]
    gather = Gather(masked_grad, bits)
    edge = lax.all_to_all(outer, "tm", 0, 0, axis_index_groups=halves, tiled=True)
    one = lax.ppermute(letter, "tm", [(b, a) for a, b in owner_one])
    two = lax.ppermute(letter, "tm", [(b, a) for a, b in owner_two])
    away, perm = gather.send()
    come = lax.ppermute(away, "tm", perm)
    weights = jnp.concatenate([key_weight, value_weight], axis=1)
    edge, inner, weights, one, two, come = fence((edge, inner, weights, one, two, come))
    gather.receive(come)
    middle = lax.all_to_all(inner, "tm", 0, 0, axis_index_groups=halves, tiled=True)
    away, perm = gather.send()
    come = lax.ppermute(away, "tm", perm)

    pair = jnp.where(upper_half, jnp.stack([two, one]), jnp.stack([one, two]))
    q_pair = pair[:, :n_query]
    g_pair = nt_dot(pair[:, n_query : 2 * n_query].reshape(-1, width), out_weight)
    g_pair = g_pair.astype(BF16).reshape(q_pair.shape)
    offsets = pair[:, 2 * n_query, :n_query].astype(jnp.int32)
    at = jnp.arange(n_query, dtype=jnp.int32)
    first = (2 * spot + jnp.arange(2, dtype=jnp.int32))[:, None] * n_query
    lower = jnp.maximum(at - W + offsets, -first)
    upper = jnp.minimum(at + offsets, total - 1 - first)

    def lanes(x):
        return jnp.tile(x.reshape(2, 2, 1, n_query // 2), (1, 1, GROUP, 1)).reshape(2, 1, -1)

    lo, hi = lanes(lower), lanes(upper)

    def project(x):
        flat = nn_dot(x.reshape(-1, width), weights).astype(BF16)
        return flat.reshape(x.shape[:-1] + (2 * width,))

    edge_kv = project(edge)
    up = [(i, i + 1) for i in range(n_dev - 1) if (i + 1) % src]
    low = Move(edge[:, 1, :, 1], up)
    high = Move(edge[:, 0, :, 0], [(target, source) for source, target in up])
    middle, come, edge_kv, q_pair, g_pair, lo, hi, low.block, high.block = fence(
        (middle, come, edge_kv, q_pair, g_pair, lo, hi, low.block, high.block)
    )
    gather.receive(come)
    middle_kv = beside([low, high], project, middle)
    ext = jnp.stack([low.come, high.come], axis=1)
    ext_kv = project(ext)
    tokens = (edge_kv, middle_kv, ext_kv)

    groups = width // LANES // CALLS
    stats = beside(
        [gather],
        functools.partial(attention, 0, width // LANES, lo, hi, None),
        q_pair, g_pair, tokens,
    )
    swap = Move(stats, flips(n_dev, bits - 1))

    def all_sources(edge, middle, ext):
        below = jnp.stack([ext[:, 0], edge[:, 1, :, 0]], axis=2)
        above = jnp.stack([edge[:, 0, :, 1], ext[:, 1]], axis=2)
        halo = jnp.stack([below, above], axis=1)
        return jnp.concatenate([x.reshape(-1, width) for x in (edge, middle, halo)], axis=0)

    sources = beside([gather, swap], all_sources, edge, middle, ext)
    while gather.order:
        beside([gather], lambda: ())

    core = me & 1
    chips = [[2 * k + c for k in range(src)] for c in range(2)]

    def meet(term):
        rows = term.reshape(src, 2, -1, term.shape[1])
        away = lax.dynamic_index_in_dim(rows, 1 - core, 1, keepdims=False)
        keep = lax.dynamic_index_in_dim(rows, core, 1, keepdims=False)
        return Move(away, flips(n_dev, 0)), keep

    def scatter(block):
        return lax.all_to_all(block, "tm", 0, 0, axis_index_groups=chips, tiled=True)

    def add(x, y):
        return (x.astype(F32) + y.astype(F32)).astype(BF16)

    def half_context(part):
        half = upper_half.astype(jnp.int32)
        return [
            Move(lax.dynamic_index_in_dim(part, half, 0, keepdims=False), owner_one),
            Move(lax.dynamic_index_in_dim(part, 1 - half, 0, keepdims=False), owner_two),
        ]

    def weigh(g):
        return tn_dot(sources, g.reshape(sources.shape[0], -1)).astype(BF16)

    def assemble(*parts):
        sums = [(a + b).astype(BF16) for a, b in zip(parts[::2], parts[1::2])]
        return jnp.concatenate(sums, axis=2)

    trades, shares, ready = [], [], None
    for call in range(CALLS):
        work = functools.partial(attention, call * groups, groups, lo, hi, (swap.block, swap.come))
        if ready is not None:
            ready, q_pair = fence((ready, q_pair))
            share = scatter(ready)
        partial, grads = work(q_pair, g_pair, tokens)
        trade = half_context(partial)
        trades += trade
        term = beside(trade, weigh, grads)
        if ready is not None:
            share, term = fence((share, term))
            shares.append(share)
        if call < CALLS - 1:
            away, keep = meet(term)
            keep = beside([away], lambda x: x, keep)
            ready = add(keep, away.come)

    context, d_query = assemble(*[move.come for move in trades])
    away, keep = meet(term)
    partner = Move(context, flips(n_dev, 0))
    keep, context = beside([away, partner], lambda *x: x, keep, context)
    ready = add(keep, away.come)

    columns = jnp.concatenate(
        [x.reshape(n_query, src, -1).swapaxes(0, 1) for x in (context, partner.come)], axis=2
    )
    if ready.shape[1] == n_query:
        packed = scatter(jnp.concatenate([ready, columns], axis=2))
        share, columns = packed[:, :, : ready.shape[2]], packed[:, :, ready.shape[2] :]
    else:
        share, columns = scatter(ready), scatter(columns)
    shares.append(share)
    attended = (nn_dot(context, out_weight) * valid_col).astype(BF16)
    columns = columns.reshape(src * n_query, -1)
    all_grad = gather.block.reshape(2, src * n_query, width)
    cut = columns.shape[1] // 2
    d_out = tn_dot(columns[:, :cut], all_grad[0]) + tn_dot(columns[:, cut:], all_grad[1])
    d_out = lax.dynamic_slice_in_dim(d_out, core * (cut // 2), cut // 2, 0)
    sums = [jnp.sum(share.astype(F32), axis=0) for share in shares]

    def heads(which):
        at = [(2 * i + which) * LANES for i in range(groups)]
        return jnp.concatenate([x[:, i : i + LANES] for x in sums for i in at], axis=1)

    return attended, d_query, heads(0), heads(1), d_out


def solution(mesh):
    in_specs = (
        P("rep", "tm", None),
        P(("rep", "tm"), None),
        P(),
        P(),
        P(),
        P(("rep", "tm")),
        P(("rep", "tm")),
        P(("rep", "tm"), None),
    )
    out_specs = (
        P(("rep", "tm"), None),
        P(("rep", "tm"), None),
        P(("rep", "tm"), None),
        P(("rep", "tm"), None),
        P(("rep", "tm"), None),
    )

    return jax.shard_map(shards, mesh=mesh, in_specs=in_specs, out_specs=out_specs, check_vma=False)
```

```python
import functools

import jax
import jax.numpy as jnp
from jax import lax
from jax.experimental.layout import Layout, with_layout_constraint
from jax.experimental import pallas as pl
from jax.experimental.pallas import tpu as pltpu
from jax.sharding import PartitionSpec as P


HD = 64
W = 16
GROUP = 4
LANES = GROUP * HD
SPLIT = (3, 1)
CHUNK = 256
F32 = jnp.float32
BF16 = jnp.bfloat16


def tn_dot(a, b):
    return lax.dot_general(a, b, (((0,), (0,)), ((), ())), preferred_element_type=F32)


def nt_dot(a, b):
    return lax.dot_general(a, b, (((1,), (1,)), ((), ())), preferred_element_type=F32)


def nn_dot(a, b):
    return jnp.dot(a, b, preferred_element_type=F32)


def own_head(n_query):
    wide = GROUP * n_query
    row_head = lax.broadcasted_iota(jnp.int32, (wide, LANES), 0) // (n_query // 2) % GROUP
    col_head = lax.broadcasted_iota(jnp.int32, (wide, LANES), 1) // HD
    return row_head == col_head


def spread(x, own):
    part = x.shape[0] // 2
    rows = jnp.concatenate([x[:part]] * GROUP + [x[part:]] * GROUP, 0)
    return jnp.where(own, rows, jnp.zeros_like(rows))


def scaled(x):
    return (x.astype(F32) * HD ** (-0.5)).astype(BF16)


def fill_bias(lo_ref, hi_ref, bias_ref, n_query):
    wide = GROUP * n_query
    lo = lo_ref[...]
    hi = hi_ref[...]
    rows = lax.broadcasted_iota(jnp.int32, (CHUNK, wide), 0)
    near = rows % W
    second = lax.broadcasted_iota(jnp.int32, (CHUNK, wide), 1) >= wide // 2
    frames = (
        near + jnp.where(second, n_query - W, 0),
        near + W,
        near + 2 * W,
        near + jnp.where(second, n_query, -W),
    )
    for i, frame in enumerate(frames):
        bias_ref[i] = jnp.where((frame >= lo) & (frame <= hi), 0.0, -1e30)


def load(ref, side):
    return ref[:, side].reshape(CHUNK, LANES)


def sides(ref):
    return load(ref, 0), load(ref, 1)


def halo_sides(near_ref, far_ref):
    lower = pl.program_id(0) == 0
    return (
        jnp.where(lower, load(far_ref, 0), load(near_ref, 1)),
        jnp.where(lower, load(near_ref, 0), load(far_ref, 1)),
    )


def pair_dot(rows, x_ref):
    mid = x_ref.shape[0] // 2
    return jnp.concatenate([nt_dot(rows[0], x_ref[:mid, :]), nt_dot(rows[1], x_ref[mid:, :])], 1)


def fold(x):
    return x.reshape(CHUNK // 8, 8, x.shape[1])


def stats_kernel(
    lo_ref, hi_ref, q_ref, g_ref,
    ke_ref, km_ref, kn_ref, kf_ref, ve_ref, vm_ref, vn_ref, vf_ref,
    out_ref, s_ref, bias_ref, bq_ref, bg_ref,
):
    n_query = q_ref.shape[0]
    wide = GROUP * n_query
    own = own_head(n_query)
    bq_ref[...] = scaled(spread(q_ref[...], own))
    bg_ref[...] = scaled(spread(g_ref[...], own))

    @pl.when(pl.program_id(1) == 0)
    def _():
        fill_bias(lo_ref, hi_ref, bias_ref, n_query)

    def score(at, s, top):
        s = s + bias_ref[at]
        s_ref[at] = s
        return jnp.maximum(top, jnp.max(fold(s), axis=0))

    top = jnp.full((8, wide), -1e30, F32)
    top = score(0, pair_dot(sides(ke_ref), bq_ref), top)
    for c in range(2):
        top = score(1 + c, nt_dot(load(km_ref, c), bq_ref[...]), top)
    top = score(3, pair_dot(halo_sides(kn_ref, kf_ref), bq_ref), top)
    top = jnp.max(top, axis=0, keepdims=True)

    total = jnp.zeros((8, wide), F32)
    weighted = jnp.zeros((8, wide), F32)
    for c in range(4):
        if c == 0:
            dp = pair_dot(sides(ve_ref), bg_ref)
        elif c == 3:
            dp = pair_dot(halo_sides(vn_ref, vf_ref), bg_ref)
        else:
            dp = nt_dot(load(vm_ref, c - 1), bg_ref[...])
        e = jnp.exp(s_ref[c] - top)
        total = total + jnp.sum(fold(e), axis=0)
        weighted = weighted + jnp.sum(fold(e * dp), axis=0)
    out_ref[0:1, :] = top
    out_ref[1:2, :] = jnp.sum(total, axis=0, keepdims=True)
    out_ref[2:3, :] = jnp.sum(weighted, axis=0, keepdims=True)


def grads_kernel(
    lo_ref, hi_ref, one_ref, two_ref, q_ref, g_ref,
    ke_ref, km_ref, kn_ref, kf_ref, ve_ref, vm_ref, vn_ref, vf_ref,
    out_ref, part_ref,
    bias_ref, bq_ref, bg_ref, bqs_ref, bgs_ref, acc_ctx, acc_dq,
):
    n_query = q_ref.shape[0]
    part = n_query // 2
    wide = GROUP * n_query
    mid = wide // 2
    own = own_head(n_query)
    bq_ref[...] = spread(q_ref[...], own)
    bg_ref[...] = spread(g_ref[...], own)
    bqs_ref[...] = scaled(bq_ref[...])
    bgs_ref[...] = scaled(bg_ref[...])

    @pl.when(pl.program_id(1) == 0)
    def _():
        fill_bias(lo_ref, hi_ref, bias_ref, n_query)

    top = jnp.maximum(one_ref[0:1, :], two_ref[0:1, :])
    one = jnp.exp(one_ref[0:1, :] - top)
    two = jnp.exp(two_ref[0:1, :] - top)
    inverse = 1.0 / (one_ref[1:2, :] * one + two_ref[1:2, :] * two)
    mean = (one_ref[2:3, :] * one + two_ref[2:3, :] * two) * inverse
    acc_ctx[...] = jnp.zeros_like(acc_ctx)
    acc_dq[...] = jnp.zeros_like(acc_dq)

    def soft(table, s, dp):
        p = jnp.exp(s + bias_ref[table] - top) * inverse
        return p.astype(BF16), (p * (dp - mean)).astype(BF16)

    shape = part_ref.shape[1:2] + part_ref.shape[3:5] + (LANES,)

    def keep(section, side, kp, vp):
        part_ref[section, :, side, :, :, :LANES] = kp.astype(BF16).reshape(shape)
        part_ref[section, :, side, :, :, LANES:] = vp.astype(BF16).reshape(shape)

    def pair(k, v, section, table):
        pb, ds = soft(table, pair_dot(k, bqs_ref), pair_dot(v, bgs_ref))
        for side, lanes in ((0, slice(0, mid)), (1, slice(mid, wide))):
            acc_ctx[lanes, :] += tn_dot(pb[:, lanes], v[side])
            acc_dq[lanes, :] += tn_dot(ds[:, lanes], k[side])
            keep(
                section, side,
                nn_dot(ds[:, lanes], bq_ref[lanes, :]), nn_dot(pb[:, lanes], bg_ref[lanes, :]),
            )

    pair(sides(ke_ref), sides(ve_ref), 0, 0)

    def middle(c, carry):
        k = load(km_ref, c)
        v = load(vm_ref, c)
        pb, ds = soft(1 + c, nt_dot(k, bqs_ref[...]), nt_dot(v, bgs_ref[...]))
        acc_ctx[...] += tn_dot(pb, v)
        acc_dq[...] += tn_dot(ds, k)
        keep(1, c, nn_dot(ds, bq_ref[...]), nn_dot(pb, bg_ref[...]))
        return carry

    lax.fori_loop(0, 2, middle, 0)
    pair(halo_sides(kn_ref, kf_ref), halo_sides(vn_ref, vf_ref), 2, 3)

    def diagonal(acc, which):
        kept = jnp.where(own, acc, 0.0)
        for i in range(2):
            rows = [kept[(i * GROUP + h) * part : (i * GROUP + h + 1) * part] for h in range(GROUP)]
            out_ref[which, i * part : (i + 1) * part, :] = functools.reduce(jnp.add, rows)

    diagonal(acc_ctx[...], 0)
    diagonal(acc_dq[...], 1)


def attention(first_group, groups, lo, hi, stats, queries, d_context, tokens):
    n_query, width = queries.shape[1:]
    src, _, tok = tokens[0].shape[:3]
    wide = GROUP * n_query
    flat = pl.BlockSpec((None, 1, wide), lambda b, g: (b, 0, 0))
    rows = pl.BlockSpec((None, n_query, LANES), lambda b, g: (b, 0, first_group + g))
    table = pl.BlockSpec((None, None, 3, wide), lambda b, g: (b, first_group + g, 0, 0))

    def section(first, block):
        shape = (src, 2, tok, None, W, LANES)
        return pl.BlockSpec(shape, lambda b, g: (0, 0, 0, block(b), 0, first + g))

    def sections(first):
        far = pl.BlockSpec((src, 2, tok, W, LANES), lambda b, g: (0, 0, 0, 0, first + g))
        return [section(first, lambda b: b)] * 2 + [section(first, lambda b: 1 - b), far]

    edge, middle, ext = tokens
    tokens = (edge, middle, edge, ext)
    sections = sections(first_group) + sections(width // LANES + first_group)
    operand = pltpu.VMEM((wide, LANES), BF16)
    total = pltpu.VMEM((wide, LANES), F32)
    bias = pltpu.VMEM((4, CHUNK, wide), F32)
    scores = 8 * CHUNK * wide * groups
    common = dict(
        grid=(2, groups),
        compiler_params=pltpu.CompilerParams(dimension_semantics=("arbitrary", "arbitrary")),
    )
    if stats is None:
        return pl.pallas_call(
            stats_kernel,
            in_specs=[flat, flat, rows, rows] + sections,
            out_specs=table,
            out_shape=jax.ShapeDtypeStruct((2, groups, 3, wide), F32),
            scratch_shapes=[pltpu.VMEM((4, CHUNK, wide), F32), bias, operand, operand],
            cost_estimate=pl.CostEstimate(
                flops=4 * scores * LANES, bytes_accessed=6 * scores, transcendentals=scores
            ),
            name="softmax_stats",
            **common,
        )(lo, hi, queries, d_context, *tokens, *tokens)

    parts = pl.BlockSpec(
        (3, src, 2, tok, None, W, 2 * LANES), lambda b, g: (0, 0, 0, 0, b, 0, g)
    )
    return pl.pallas_call(
        grads_kernel,
        in_specs=[flat, flat, table, table, rows, rows] + sections,
        out_specs=[
            pl.BlockSpec((None, 2, n_query, LANES), lambda b, g: (b, 0, 0, g)),
            parts,
        ],
        out_shape=[
            jax.ShapeDtypeStruct((2, 2, n_query, groups * LANES), F32),
            jax.ShapeDtypeStruct((3, src, 2, tok, 2, W, 2 * groups * LANES), BF16),
        ],
        scratch_shapes=[bias] + [operand] * 4 + [total] * 2,
        cost_estimate=pl.CostEstimate(
            flops=12 * scores * LANES, bytes_accessed=12 * scores, transcendentals=scores
        ),
        name="banded_grads",
        **common,
    )(lo, hi, *stats, queries, d_context, *tokens, *tokens)


def flips(n_dev, bit):
    return [(i, i ^ (1 << bit)) for i in range(n_dev)]


class Gather:
    def __init__(self, block, bits):
        self.block = block
        self.n_dev = 1 << bits
        self.order = list(range(bits - 1, -1, -1))

    def send(self):
        self.bit = self.order.pop(0)
        return self.block, flips(self.n_dev, self.bit)

    def receive(self, come):
        if self.bit == 0:
            self.block = jnp.stack([self.block, come])
            return
        mine = (lax.axis_index("tm") >> self.bit) & 1
        self.block = jnp.where(
            mine == 0,
            jnp.stack([self.block, come], axis=-3),
            jnp.stack([come, self.block], axis=-3),
        )


class Move:
    def __init__(self, block, perm):
        self.block = block
        self.order = [perm]

    def send(self):
        return self.block, self.order.pop(0)

    def receive(self, come):
        self.come = come


def beside(moving, work, *args):
    moving = [m for m in moving if m.order]
    sends = [m.send() for m in moving]
    args, aways = lax.optimization_barrier((args, [away for away, _ in sends]))
    comes = [lax.ppermute(away, "tm", perm) for away, (_, perm) in zip(aways, sends)]
    result, comes = lax.optimization_barrier((work(*args), comes))
    for m, come in zip(moving, comes):
        m.receive(come)
    return result


def shards(
    exo_tokens, queries, key_weight, value_weight, out_weight, gaze_valid, window_offset, cotangent
):
    n_query, width = queries.shape
    tok = exo_tokens.shape[1]
    n_dev = lax.axis_size("tm")
    bits = n_dev.bit_length() - 1
    src = n_dev // 2
    total = n_query * n_dev
    me = lax.axis_index("tm")
    upper_half = me >= src
    spot = me % src
    fence = lax.optimization_barrier

    owner_one = [(s, 2 * s) for s in range(src)] + [(src + s, 2 * s + 1) for s in range(src)]
    owner_two = [(s, 2 * s + 1) for s in range(src)] + [(src + s, 2 * s) for s in range(src)]
    valid_col = gaze_valid.astype(F32)[:, None]
    masked_grad = (cotangent.astype(F32) * valid_col).astype(BF16)
    note = jnp.zeros((W, width), BF16).at[0, :n_query].set(window_offset.astype(BF16))
    letter = jnp.concatenate([queries, masked_grad, note], axis=0)

    def frames(exo, *cuts):
        by_block = exo.reshape(src, 2, n_query, tok, width)
        runs = jnp.stack([by_block[:, :, cut : cut + W] for cut in cuts], axis=1)
        runs = runs.transpose(0, 1, 4, 2, 3, 5)
        return with_layout_constraint(runs, Layout(tuple(range(6))))

    later = fence(exo_tokens)
    outer = frames(exo_tokens, 0, n_query - W)
    inner = frames(later, W, 2 * W)
    halves = [list(range(src)), list(range(src, n_dev))]
    gather = Gather(masked_grad, bits)
    edge = lax.all_to_all(outer, "tm", 0, 0, axis_index_groups=halves, tiled=True)
    one = lax.ppermute(letter, "tm", [(b, a) for a, b in owner_one])
    two = lax.ppermute(letter, "tm", [(b, a) for a, b in owner_two])
    weights = jnp.concatenate([key_weight, value_weight], axis=1)
    edge, inner, weights, one, two = fence((edge, inner, weights, one, two))
    middle = lax.all_to_all(inner, "tm", 0, 0, axis_index_groups=halves, tiled=True)

    pair = jnp.where(upper_half, jnp.stack([two, one]), jnp.stack([one, two]))
    q_pair = pair[:, :n_query]
    g_pair = nt_dot(pair[:, n_query : 2 * n_query].reshape(-1, width), out_weight)
    g_pair = g_pair.astype(BF16).reshape(q_pair.shape)
    offsets = pair[:, 2 * n_query, :n_query].astype(jnp.int32)
    at = jnp.arange(n_query, dtype=jnp.int32)
    first = (2 * spot + jnp.arange(2, dtype=jnp.int32))[:, None] * n_query
    lower = jnp.maximum(at - W + offsets, -first)
    upper = jnp.minimum(at + offsets, total - 1 - first)

    def lanes(x):
        return jnp.tile(x.reshape(2, 2, 1, n_query // 2), (1, 1, GROUP, 1)).reshape(2, 1, -1)

    lo, hi = lanes(lower), lanes(upper)

    def project(x):
        flat = nn_dot(x.reshape(-1, width), weights).astype(BF16)
        return flat.reshape(x.shape[:-1] + (2 * width,))

    edge_kv = project(edge)
    up = [(i, i + 1) for i in range(n_dev - 1) if (i + 1) % src]
    low = Move(edge[:, 1, :, 1], up)
    high = Move(edge[:, 0, :, 0], [(target, source) for source, target in up])
    middle, edge_kv, q_pair, g_pair, lo, hi, low.block, high.block = fence(
        (middle, edge_kv, q_pair, g_pair, lo, hi, low.block, high.block)
    )
    middle_kv = beside([low, high], project, middle)
    ext = jnp.stack([low.come, high.come], axis=1)
    ext_kv = project(ext)
    tokens = (edge_kv, middle_kv, ext_kv)

    stats = beside(
        [gather],
        functools.partial(attention, 0, width // LANES, lo, hi, None),
        q_pair, g_pair, tokens,
    )
    swap = Move(stats, flips(n_dev, bits - 1))

    def all_sources(edge, middle, ext):
        below = jnp.stack([ext[:, 0], edge[:, 1, :, 0]], axis=2)
        above = jnp.stack([edge[:, 0, :, 1], ext[:, 1]], axis=2)
        halo = jnp.stack([below, above], axis=1)
        return jnp.concatenate([x.reshape(-1, width) for x in (edge, middle, halo)], axis=0)

    sources = beside([gather, swap], all_sources, edge, middle, ext)

    core = me & 1
    chips = [[2 * k + c for k in range(src)] for c in range(2)]

    def meet(term):
        rows = term.reshape(src, 2, -1, term.shape[1])
        away = lax.dynamic_index_in_dim(rows, 1 - core, 1, keepdims=False)
        keep = lax.dynamic_index_in_dim(rows, core, 1, keepdims=False)
        return Move(away, flips(n_dev, 0)), keep

    def scatter(block):
        return lax.all_to_all(block, "tm", 0, 0, axis_index_groups=chips, tiled=True)

    def add(x, y):
        return (x.astype(F32) + y.astype(F32)).astype(BF16)

    def half_context(part):
        half = upper_half.astype(jnp.int32)
        return [
            Move(lax.dynamic_index_in_dim(part, half, 0, keepdims=False), owner_one),
            Move(lax.dynamic_index_in_dim(part, 1 - half, 0, keepdims=False), owner_two),
        ]

    def weigh(g):
        return tn_dot(sources, g.reshape(sources.shape[0], -1)).astype(BF16)

    def assemble(*parts):
        sums = [(a + b).astype(BF16) for a, b in zip(parts[::2], parts[1::2])]
        return jnp.concatenate(sums, axis=2)

    trades, shares, ready, start = [], [], None, 0
    for call, groups in enumerate(SPLIT):
        work = functools.partial(attention, start, groups, lo, hi, (swap.block, swap.come))
        start += groups
        if ready is not None:
            ready, q_pair = fence((ready, q_pair))
            share = scatter(ready)
        partial, grads = beside([gather], work, q_pair, g_pair, tokens)
        trade = half_context(partial)
        trades += trade
        term = beside(trade + [gather], weigh, grads)
        if ready is not None:
            shares.append(share)
        if call < len(SPLIT) - 1:
            away, keep = meet(term)
            keep = beside([away, gather], lambda x: x, keep)
            ready = add(keep, away.come)

    context, d_query = assemble(*[move.come for move in trades])
    away, keep = meet(term)
    partner = Move(context, flips(n_dev, 0))
    keep, context = beside([away, partner], lambda *x: x, keep, context)
    ready, shares = fence((add(keep, away.come), shares))

    columns = jnp.concatenate(
        [x.reshape(n_query, src, -1).swapaxes(0, 1) for x in (context, partner.come)], axis=2
    )
    if ready.shape[1] == n_query:
        packed = scatter(jnp.concatenate([ready, columns], axis=2))
        share, columns = packed[:, :, : ready.shape[2]], packed[:, :, ready.shape[2] :]
    else:
        share, columns = scatter(ready), scatter(columns)
    shares.append(share)
    attended = (nn_dot(context, out_weight) * valid_col).astype(BF16)
    columns = columns.reshape(src * n_query, -1)
    all_grad = gather.block.reshape(2, src * n_query, width)
    cut = columns.shape[1] // 2
    d_out = tn_dot(columns[:, :cut], all_grad[0]) + tn_dot(columns[:, cut:], all_grad[1])
    d_out = lax.dynamic_slice_in_dim(d_out, core * (cut // 2), cut // 2, 0)
    sums = [jnp.sum(share.astype(F32), axis=0) for share in shares]

    def heads(which):
        cuts = [(x, (2 * i + which) * LANES) for x, n in zip(sums, SPLIT) for i in range(n)]
        return jnp.concatenate([x[:, i : i + LANES] for x, i in cuts], axis=1)

    return attended, d_query, heads(0), heads(1), d_out


def solution(mesh):
    in_specs = (
        P("rep", "tm", None),
        P(("rep", "tm"), None),
        P(),
        P(),
        P(),
        P(("rep", "tm")),
        P(("rep", "tm")),
        P(("rep", "tm"), None),
    )
    out_specs = (
        P(("rep", "tm"), None),
        P(("rep", "tm"), None),
        P(("rep", "tm"), None),
        P(("rep", "tm"), None),
        P(("rep", "tm"), None),
    )

    return jax.shard_map(shards, mesh=mesh, in_specs=in_specs, out_specs=out_specs, check_vma=False)
```

```python
import functools

import jax
import jax.numpy as jnp
from jax import lax
from jax.experimental.layout import Layout, with_layout_constraint
from jax.experimental import pallas as pl
from jax.experimental.pallas import tpu as pltpu
from jax.sharding import PartitionSpec as P


HD = 64
W = 16
GROUP = 4
LANES = GROUP * HD
SPLIT = (2, 2)
CHUNK = 256
F32 = jnp.float32
BF16 = jnp.bfloat16


def tn_dot(a, b):
    return lax.dot_general(a, b, (((0,), (0,)), ((), ())), preferred_element_type=F32)


def nt_dot(a, b):
    return lax.dot_general(a, b, (((1,), (1,)), ((), ())), preferred_element_type=F32)


def nn_dot(a, b):
    return jnp.dot(a, b, preferred_element_type=F32)


def own_head(n_query):
    wide = GROUP * n_query
    row_head = lax.broadcasted_iota(jnp.int32, (wide, LANES), 0) // (n_query // 2) % GROUP
    col_head = lax.broadcasted_iota(jnp.int32, (wide, LANES), 1) // HD
    return row_head == col_head


def spread(x, own):
    part = x.shape[0] // 2
    rows = jnp.concatenate([x[:part]] * GROUP + [x[part:]] * GROUP, 0)
    return jnp.where(own, rows, jnp.zeros_like(rows))


def scaled(x):
    return (x.astype(F32) * HD ** (-0.5)).astype(BF16)


def fill_bias(lo_ref, hi_ref, bias_ref, n_query):
    wide = GROUP * n_query
    lo = lo_ref[...]
    hi = hi_ref[...]
    rows = lax.broadcasted_iota(jnp.int32, (CHUNK, wide), 0)
    near = rows % W
    second = lax.broadcasted_iota(jnp.int32, (CHUNK, wide), 1) >= wide // 2
    frames = (
        near + jnp.where(second, n_query - W, 0),
        near + jnp.where(second, n_query, -W),
        near + W,
        near + 2 * W,
    )
    for i, frame in enumerate(frames):
        at = slice(i % 2 * CHUNK, (i % 2 + 1) * CHUNK)
        bias_ref[i // 2, at, :] = jnp.where((frame >= lo) & (frame <= hi), 0.0, -1e30)


def load(ref, side):
    return ref[:, side].reshape(CHUNK, LANES)


def row_groups(edge_ref, mid_ref, near_ref, far_ref):
    lower = pl.program_id(0) == 0
    below = jnp.where(lower, load(far_ref, 0), load(near_ref, 1))
    above = jnp.where(lower, load(near_ref, 0), load(far_ref, 1))
    return (
        jnp.concatenate([load(edge_ref, 0), below], 0),
        jnp.concatenate([load(edge_ref, 1), above], 0),
        jnp.concatenate([load(mid_ref, 0), load(mid_ref, 1)], 0),
    )


def group_dots(rows, x_ref):
    mid = x_ref.shape[0] // 2
    pair = jnp.concatenate([nt_dot(rows[0], x_ref[:mid, :]), nt_dot(rows[1], x_ref[mid:, :])], 1)
    return pair, nt_dot(rows[2], x_ref[...])


def fold(x):
    return x.reshape(x.shape[0] // 8, 8, x.shape[1])


def stats_kernel(
    lo_ref, hi_ref, q_ref, g_ref,
    ke_ref, km_ref, kn_ref, kf_ref, ve_ref, vm_ref, vn_ref, vf_ref,
    out_ref, bias_ref, bq_ref, bg_ref,
):
    n_query = q_ref.shape[0]
    own = own_head(n_query)
    bq_ref[...] = scaled(spread(q_ref[...], own))
    bg_ref[...] = scaled(spread(g_ref[...], own))

    @pl.when(pl.program_id(1) == 0)
    def _():
        fill_bias(lo_ref, hi_ref, bias_ref, n_query)

    scores = group_dots(row_groups(ke_ref, km_ref, kn_ref, kf_ref), bq_ref)
    d_probs = group_dots(row_groups(ve_ref, vm_ref, vn_ref, vf_ref), bg_ref)
    scores = [s + bias_ref[i] for i, s in enumerate(scores)]
    tops = [jnp.max(fold(s), axis=0) for s in scores]
    top = jnp.max(jnp.maximum(*tops), axis=0, keepdims=True)
    total, weighted = [], []
    for s, dp in zip(scores, d_probs):
        e = jnp.exp(s - top)
        total.append(jnp.sum(fold(e), axis=0))
        weighted.append(jnp.sum(fold(e * dp), axis=0))
    out_ref[0:1, :] = top
    out_ref[1:2, :] = jnp.sum(total[0] + total[1], axis=0, keepdims=True)
    out_ref[2:3, :] = jnp.sum(weighted[0] + weighted[1], axis=0, keepdims=True)


def grads_kernel(
    lo_ref, hi_ref, one_ref, two_ref, q_ref, g_ref,
    ke_ref, km_ref, kn_ref, kf_ref, ve_ref, vm_ref, vn_ref, vf_ref,
    out_ref, part_ref,
    bias_ref, bq_ref, bg_ref, bqs_ref, bgs_ref,
):
    n_query = q_ref.shape[0]
    part = n_query // 2
    wide = GROUP * n_query
    mid = wide // 2
    own = own_head(n_query)
    bq_ref[...] = spread(q_ref[...], own)
    bg_ref[...] = spread(g_ref[...], own)
    bqs_ref[...] = scaled(bq_ref[...])
    bgs_ref[...] = scaled(bg_ref[...])

    @pl.when(pl.program_id(1) == 0)
    def _():
        fill_bias(lo_ref, hi_ref, bias_ref, n_query)

    top = jnp.maximum(one_ref[0:1, :], two_ref[0:1, :])
    one = jnp.exp(one_ref[0:1, :] - top)
    two = jnp.exp(two_ref[0:1, :] - top)
    inverse = 1.0 / (one_ref[1:2, :] * one + two_ref[1:2, :] * two)
    mean = (one_ref[2:3, :] * one + two_ref[2:3, :] * two) * inverse
    keys = row_groups(ke_ref, km_ref, kn_ref, kf_ref)
    values = row_groups(ve_ref, vm_ref, vn_ref, vf_ref)
    probs, d_scores = [], []
    for i, (s, dp) in enumerate(zip(group_dots(keys, bqs_ref), group_dots(values, bgs_ref))):
        p = jnp.exp(s + bias_ref[i] - top) * inverse
        probs.append(p.astype(BF16))
        d_scores.append((p * (dp - mean)).astype(BF16))

    shape = part_ref.shape[1:2] + part_ref.shape[3:5] + (LANES,)
    low, high, both = slice(0, mid), slice(mid, wide), slice(0, wide)
    places = (((0, 0), (2, 0)), ((0, 1), (2, 1)), ((1, 0), (1, 1)))

    def back(weights, x_ref, cols):
        for which, lanes, place in zip((0, 0, 1), (low, high, both), places):
            x = nn_dot(weights[which][:, lanes], x_ref[lanes, :]).astype(BF16)
            for i, (section, side) in enumerate(place):
                rows = x[i * CHUNK : (i + 1) * CHUNK].reshape(shape)
                part_ref[section, :, side, :, :, cols] = rows

    back(d_scores, bq_ref, slice(0, LANES))
    back(probs, bg_ref, slice(LANES, 2 * LANES))

    def forward(which, weights, rows):
        for i, lanes in enumerate((low, high)):
            left = jnp.concatenate([w[:, lanes] for w in weights], 0)
            acc = tn_dot(left, jnp.concatenate([rows[i], rows[2]], 0))
            acc = jnp.where(own[lanes], acc, 0.0)
            heads = [acc[h * part : (h + 1) * part] for h in range(GROUP)]
            out_ref[which, i * part : (i + 1) * part, :] = functools.reduce(jnp.add, heads)

    forward(0, probs, values)
    forward(1, d_scores, keys)


def attention(first_group, groups, lo, hi, stats, queries, d_context, tokens):
    n_query, width = queries.shape[1:]
    src, _, tok = tokens[0].shape[:3]
    wide = GROUP * n_query
    flat = pl.BlockSpec((None, 1, wide), lambda b, g: (b, 0, 0))
    rows = pl.BlockSpec((None, n_query, LANES), lambda b, g: (b, 0, first_group + g))
    table = pl.BlockSpec((None, None, 3, wide), lambda b, g: (b, first_group + g, 0, 0))

    def section(first, block):
        shape = (src, 2, tok, None, W, LANES)
        return pl.BlockSpec(shape, lambda b, g: (0, 0, 0, block(b), 0, first + g))

    def sections(first):
        far = pl.BlockSpec((src, 2, tok, W, LANES), lambda b, g: (0, 0, 0, 0, first + g))
        return [section(first, lambda b: b)] * 2 + [section(first, lambda b: 1 - b), far]

    edge, middle, ext = tokens
    tokens = (edge, middle, edge, ext)
    sections = sections(first_group) + sections(width // LANES + first_group)
    operand = pltpu.VMEM((wide, LANES), BF16)
    bias = pltpu.VMEM((2, 2 * CHUNK, wide), F32)
    scores = 8 * CHUNK * wide * groups
    common = dict(
        grid=(2, groups),
        compiler_params=pltpu.CompilerParams(dimension_semantics=("arbitrary", "arbitrary")),
    )
    if stats is None:
        return pl.pallas_call(
            stats_kernel,
            in_specs=[flat, flat, rows, rows] + sections,
            out_specs=table,
            out_shape=jax.ShapeDtypeStruct((2, groups, 3, wide), F32),
            scratch_shapes=[bias, operand, operand],
            cost_estimate=pl.CostEstimate(
                flops=4 * scores * LANES, bytes_accessed=6 * scores, transcendentals=scores
            ),
            name="softmax_stats",
            **common,
        )(lo, hi, queries, d_context, *tokens, *tokens)

    parts = pl.BlockSpec(
        (3, src, 2, tok, None, W, 2 * LANES), lambda b, g: (0, 0, 0, 0, b, 0, g)
    )
    return pl.pallas_call(
        grads_kernel,
        in_specs=[flat, flat, table, table, rows, rows] + sections,
        out_specs=[
            pl.BlockSpec((None, 2, n_query, LANES), lambda b, g: (b, 0, 0, g)),
            parts,
        ],
        out_shape=[
            jax.ShapeDtypeStruct((2, 2, n_query, groups * LANES), F32),
            jax.ShapeDtypeStruct((3, src, 2, tok, 2, W, 2 * groups * LANES), BF16),
        ],
        scratch_shapes=[bias] + [operand] * 4,
        cost_estimate=pl.CostEstimate(
            flops=12 * scores * LANES, bytes_accessed=12 * scores, transcendentals=scores
        ),
        name="banded_grads",
        **common,
    )(lo, hi, *stats, queries, d_context, *tokens, *tokens)


def flips(n_dev, bit):
    return [(i, i ^ (1 << bit)) for i in range(n_dev)]


class Gather:
    def __init__(self, block, bits):
        self.block = block
        self.n_dev = 1 << bits
        self.order = list(range(bits - 1, -1, -1))

    def send(self):
        self.bit = self.order.pop(0)
        return self.block, flips(self.n_dev, self.bit)

    def receive(self, come):
        if self.bit == 0:
            self.block = jnp.stack([self.block, come])
            return
        mine = (lax.axis_index("tm") >> self.bit) & 1
        self.block = jnp.where(
            mine == 0,
            jnp.stack([self.block, come], axis=-3),
            jnp.stack([come, self.block], axis=-3),
        )


class Move:
    def __init__(self, block, perm):
        self.block = block
        self.order = [perm]

    def send(self):
        return self.block, self.order.pop(0)

    def receive(self, come):
        self.come = come


def beside(moving, work, *args):
    moving = [m for m in moving if m.order]
    sends = [m.send() for m in moving]
    args, aways = lax.optimization_barrier((args, [away for away, _ in sends]))
    comes = [lax.ppermute(away, "tm", perm) for away, (_, perm) in zip(aways, sends)]
    result, comes = lax.optimization_barrier((work(*args), comes))
    for m, come in zip(moving, comes):
        m.receive(come)
    return result


def shards(
    exo_tokens, queries, key_weight, value_weight, out_weight, gaze_valid, window_offset, cotangent
):
    n_query, width = queries.shape
    tok = exo_tokens.shape[1]
    n_dev = lax.axis_size("tm")
    bits = n_dev.bit_length() - 1
    src = n_dev // 2
    total = n_query * n_dev
    me = lax.axis_index("tm")
    upper_half = me >= src
    spot = me % src
    fence = lax.optimization_barrier

    owner_one = [(s, 2 * s) for s in range(src)] + [(src + s, 2 * s + 1) for s in range(src)]
    owner_two = [(s, 2 * s + 1) for s in range(src)] + [(src + s, 2 * s) for s in range(src)]
    valid_col = gaze_valid.astype(F32)[:, None]
    masked_grad = (cotangent.astype(F32) * valid_col).astype(BF16)
    note = jnp.zeros((W, width), BF16).at[0, :n_query].set(window_offset.astype(BF16))
    letter = jnp.concatenate([queries, masked_grad, note], axis=0)

    def frames(exo, *cuts):
        by_block = exo.reshape(src, 2, n_query, tok, width)
        runs = jnp.stack([by_block[:, :, cut : cut + W] for cut in cuts], axis=1)
        runs = runs.transpose(0, 1, 4, 2, 3, 5)
        return with_layout_constraint(runs, Layout(tuple(range(6))))

    later = fence(exo_tokens)
    outer = frames(exo_tokens, 0, n_query - W)
    inner = frames(later, W, 2 * W)
    halves = [list(range(src)), list(range(src, n_dev))]
    gather = Gather(masked_grad, bits)
    edge = lax.all_to_all(outer, "tm", 0, 0, axis_index_groups=halves, tiled=True)
    one = lax.ppermute(letter, "tm", [(b, a) for a, b in owner_one])
    two = lax.ppermute(letter, "tm", [(b, a) for a, b in owner_two])
    weights = jnp.concatenate([key_weight, value_weight], axis=1)
    edge, inner, weights, one, two = fence((edge, inner, weights, one, two))
    middle = lax.all_to_all(inner, "tm", 0, 0, axis_index_groups=halves, tiled=True)

    pair = jnp.where(upper_half, jnp.stack([two, one]), jnp.stack([one, two]))
    q_pair = pair[:, :n_query]
    g_pair = nt_dot(pair[:, n_query : 2 * n_query].reshape(-1, width), out_weight)
    g_pair = g_pair.astype(BF16).reshape(q_pair.shape)
    offsets = pair[:, 2 * n_query, :n_query].astype(jnp.int32)
    at = jnp.arange(n_query, dtype=jnp.int32)
    first = (2 * spot + jnp.arange(2, dtype=jnp.int32))[:, None] * n_query
    lower = jnp.maximum(at - W + offsets, -first)
    upper = jnp.minimum(at + offsets, total - 1 - first)

    def lanes(x):
        return jnp.tile(x.reshape(2, 2, 1, n_query // 2), (1, 1, GROUP, 1)).reshape(2, 1, -1)

    lo, hi = lanes(lower), lanes(upper)

    def project(x):
        flat = nn_dot(x.reshape(-1, width), weights).astype(BF16)
        return flat.reshape(x.shape[:-1] + (2 * width,))

    edge_kv = project(edge)
    up = [(i, i + 1) for i in range(n_dev - 1) if (i + 1) % src]
    low = Move(edge[:, 1, :, 1], up)
    high = Move(edge[:, 0, :, 0], [(target, source) for source, target in up])
    middle, edge_kv, q_pair, g_pair, lo, hi, low.block, high.block = fence(
        (middle, edge_kv, q_pair, g_pair, lo, hi, low.block, high.block)
    )
    middle_kv = beside([low, high], project, middle)
    ext = jnp.stack([low.come, high.come], axis=1)
    ext_kv = project(ext)
    tokens = (edge_kv, middle_kv, ext_kv)

    stats = beside(
        [gather],
        functools.partial(attention, 0, width // LANES, lo, hi, None),
        q_pair, g_pair, tokens,
    )
    swap = Move(stats, flips(n_dev, bits - 1))

    def all_sources(edge, middle, ext):
        below = jnp.stack([ext[:, 0], edge[:, 1, :, 0]], axis=2)
        above = jnp.stack([edge[:, 0, :, 1], ext[:, 1]], axis=2)
        halo = jnp.stack([below, above], axis=1)
        return jnp.concatenate([x.reshape(-1, width) for x in (edge, middle, halo)], axis=0)

    sources = beside([gather, swap], all_sources, edge, middle, ext)

    core = me & 1
    chips = [[2 * k + c for k in range(src)] for c in range(2)]

    def meet(term):
        rows = term.reshape(src, 2, -1, term.shape[1])
        away = lax.dynamic_index_in_dim(rows, 1 - core, 1, keepdims=False)
        keep = lax.dynamic_index_in_dim(rows, core, 1, keepdims=False)
        return Move(away, flips(n_dev, 0)), keep

    def scatter(block):
        return lax.all_to_all(block, "tm", 0, 0, axis_index_groups=chips, tiled=True)

    def add(x, y):
        return (x.astype(F32) + y.astype(F32)).astype(BF16)

    def half_context(part):
        half = upper_half.astype(jnp.int32)
        return [
            Move(lax.dynamic_index_in_dim(part, half, 0, keepdims=False), owner_one),
            Move(lax.dynamic_index_in_dim(part, 1 - half, 0, keepdims=False), owner_two),
        ]

    def weigh(g):
        return tn_dot(sources, g.reshape(sources.shape[0], -1)).astype(BF16)

    def assemble(*parts):
        sums = [(a + b).astype(BF16) for a, b in zip(parts[::2], parts[1::2])]
        return jnp.concatenate(sums, axis=2)

    trades, shares, ready, start = [], [], None, 0
    for call, groups in enumerate(SPLIT):
        work = functools.partial(attention, start, groups, lo, hi, (swap.block, swap.come))
        start += groups
        if ready is not None:
            ready, q_pair = fence((ready, q_pair))
            share = scatter(ready)
        partial, grads = beside([gather], work, q_pair, g_pair, tokens)
        trade = half_context(partial)
        trades += trade
        term = beside(trade + [gather], weigh, grads)
        if ready is not None:
            shares.append(share)
        if call < len(SPLIT) - 1:
            away, keep = meet(term)
            keep = beside([away, gather], lambda x: x, keep)
            ready = add(keep, away.come)

    context, d_query = assemble(*[move.come for move in trades])
    away, keep = meet(term)
    partner = Move(context, flips(n_dev, 0))
    keep, context = beside([away, partner], lambda *x: x, keep, context)
    ready, shares = fence((add(keep, away.come), shares))

    columns = jnp.concatenate(
        [x.reshape(n_query, src, -1).swapaxes(0, 1) for x in (context, partner.come)], axis=2
    )
    if ready.shape[1] == n_query:
        packed = scatter(jnp.concatenate([ready, columns], axis=2))
        share, columns = packed[:, :, : ready.shape[2]], packed[:, :, ready.shape[2] :]
    else:
        share, columns = scatter(ready), scatter(columns)
    shares.append(share)
    attended = (nn_dot(context, out_weight) * valid_col).astype(BF16)
    columns = columns.reshape(src * n_query, -1)
    all_grad = gather.block.reshape(2, src * n_query, width)
    cut = columns.shape[1] // 2
    d_out = tn_dot(columns[:, :cut], all_grad[0]) + tn_dot(columns[:, cut:], all_grad[1])
    d_out = lax.dynamic_slice_in_dim(d_out, core * (cut // 2), cut // 2, 0)
    sums = [jnp.sum(share.astype(F32), axis=0) for share in shares]

    def heads(which):
        cuts = [(x, (2 * i + which) * LANES) for x, n in zip(sums, SPLIT) for i in range(n)]
        return jnp.concatenate([x[:, i : i + LANES] for x, i in cuts], axis=1)

    return attended, d_query, heads(0), heads(1), d_out


def solution(mesh):
    in_specs = (
        P("rep", "tm", None),
        P(("rep", "tm"), None),
        P(),
        P(),
        P(),
        P(("rep", "tm")),
        P(("rep", "tm")),
        P(("rep", "tm"), None),
    )
    out_specs = (
        P(("rep", "tm"), None),
        P(("rep", "tm"), None),
        P(("rep", "tm"), None),
        P(("rep", "tm"), None),
        P(("rep", "tm"), None),
    )

    return jax.shard_map(shards, mesh=mesh, in_specs=in_specs, out_specs=out_specs, check_vma=False)
```

```python
import functools

import jax
import jax.numpy as jnp
from jax import lax
from jax.experimental.layout import Layout, with_layout_constraint
from jax.experimental import pallas as pl
from jax.experimental.pallas import tpu as pltpu
from jax.sharding import PartitionSpec as P


HD = 64
W = 16
GROUP = 4
LANES = GROUP * HD
SPLIT = (2, 2)
CHUNK = 256
F32 = jnp.float32
BF16 = jnp.bfloat16


def tn_dot(a, b):
    return lax.dot_general(a, b, (((0,), (0,)), ((), ())), preferred_element_type=F32)


def nt_dot(a, b):
    return lax.dot_general(a, b, (((1,), (1,)), ((), ())), preferred_element_type=F32)


def nn_dot(a, b):
    return jnp.dot(a, b, preferred_element_type=F32)


def own_head(n_query):
    wide = GROUP * n_query
    row_head = lax.broadcasted_iota(jnp.int32, (wide, LANES), 0) // (n_query // 2) % GROUP
    col_head = lax.broadcasted_iota(jnp.int32, (wide, LANES), 1) // HD
    return row_head == col_head


def spread(x, own):
    part = x.shape[0] // 2
    rows = jnp.concatenate([x[:part]] * GROUP + [x[part:]] * GROUP, 0)
    return jnp.where(own, rows, jnp.zeros_like(rows))


def scaled(x):
    return (x.astype(F32) * HD ** (-0.5)).astype(BF16)


def fill_bias(lo_ref, hi_ref, bias_ref, n_query):
    wide = GROUP * n_query
    lo = lo_ref[...]
    hi = hi_ref[...]
    rows = lax.broadcasted_iota(jnp.int32, (CHUNK, wide), 0)
    near = rows % W
    second = lax.broadcasted_iota(jnp.int32, (CHUNK, wide), 1) >= wide // 2
    frames = (
        near + jnp.where(second, n_query - W, 0),
        near + jnp.where(second, n_query, -W),
        near + W,
        near + 2 * W,
    )
    for i, frame in enumerate(frames):
        at = slice(i % 2 * CHUNK, (i % 2 + 1) * CHUNK)
        bias_ref[i // 2, at, :] = jnp.where((frame >= lo) & (frame <= hi), 0.0, -1e30)


def load(ref, side):
    return ref[:, side].reshape(CHUNK, LANES)


def row_groups(edge_ref, mid_ref, near_ref, far_ref):
    lower = pl.program_id(0) == 0
    below = jnp.where(lower, load(far_ref, 0), load(near_ref, 1))
    above = jnp.where(lower, load(near_ref, 0), load(far_ref, 1))
    return (
        jnp.concatenate([load(edge_ref, 0), below], 0),
        jnp.concatenate([load(edge_ref, 1), above], 0),
        jnp.concatenate([load(mid_ref, 0), load(mid_ref, 1)], 0),
    )


def group_dots(rows, x_ref):
    mid = x_ref.shape[0] // 2
    pair = jnp.concatenate([nt_dot(rows[0], x_ref[:mid, :]), nt_dot(rows[1], x_ref[mid:, :])], 1)
    return pair, nt_dot(rows[2], x_ref[...])


def fold(x):
    return x.reshape(x.shape[0] // 8, 8, x.shape[1])


def stats_kernel(
    lo_ref, hi_ref, q_ref, g_ref,
    ke_ref, km_ref, kn_ref, kf_ref, ve_ref, vm_ref, vn_ref, vf_ref,
    out_ref, bias_ref, bq_ref, bg_ref,
):
    n_query = q_ref.shape[0]
    own = own_head(n_query)
    bq_ref[...] = scaled(spread(q_ref[...], own))
    bg_ref[...] = scaled(spread(g_ref[...], own))

    @pl.when(pl.program_id(1) == 0)
    def _():
        fill_bias(lo_ref, hi_ref, bias_ref, n_query)

    scores = group_dots(row_groups(ke_ref, km_ref, kn_ref, kf_ref), bq_ref)
    d_probs = group_dots(row_groups(ve_ref, vm_ref, vn_ref, vf_ref), bg_ref)
    scores = [s + bias_ref[i] for i, s in enumerate(scores)]
    tops = [jnp.max(fold(s), axis=0) for s in scores]
    top = jnp.max(jnp.maximum(*tops), axis=0, keepdims=True)
    total, weighted = [], []
    for s, dp in zip(scores, d_probs):
        e = jnp.exp(s - top)
        total.append(jnp.sum(fold(e), axis=0))
        weighted.append(jnp.sum(fold(e * dp), axis=0))
    out_ref[0:1, :] = top
    out_ref[1:2, :] = jnp.sum(total[0] + total[1], axis=0, keepdims=True)
    out_ref[2:3, :] = jnp.sum(weighted[0] + weighted[1], axis=0, keepdims=True)


def grads_kernel(
    lo_ref, hi_ref, one_ref, two_ref, q_ref, g_ref,
    ke_ref, km_ref, kn_ref, kf_ref, ve_ref, vm_ref, vn_ref, vf_ref,
    out_ref, part_ref,
    bias_ref, bq_ref, bg_ref, bqs_ref, bgs_ref,
):
    n_query = q_ref.shape[0]
    part = n_query // 2
    wide = GROUP * n_query
    mid = wide // 2
    own = own_head(n_query)
    bq_ref[...] = spread(q_ref[...], own)
    bg_ref[...] = spread(g_ref[...], own)
    bqs_ref[...] = scaled(bq_ref[...])
    bgs_ref[...] = scaled(bg_ref[...])

    @pl.when(pl.program_id(1) == 0)
    def _():
        fill_bias(lo_ref, hi_ref, bias_ref, n_query)

    top = jnp.maximum(one_ref[0:1, :], two_ref[0:1, :])
    one = jnp.exp(one_ref[0:1, :] - top)
    two = jnp.exp(two_ref[0:1, :] - top)
    inverse = 1.0 / (one_ref[1:2, :] * one + two_ref[1:2, :] * two)
    mean = (one_ref[2:3, :] * one + two_ref[2:3, :] * two) * inverse
    keys = row_groups(ke_ref, km_ref, kn_ref, kf_ref)
    values = row_groups(ve_ref, vm_ref, vn_ref, vf_ref)
    probs, d_scores = [], []
    for i, (s, dp) in enumerate(zip(group_dots(keys, bqs_ref), group_dots(values, bgs_ref))):
        p = jnp.exp(s + bias_ref[i] - top) * inverse
        probs.append(p.astype(BF16))
        d_scores.append((p * (dp - mean)).astype(BF16))

    shape = part_ref.shape[1:4] + (LANES,)
    low, high, both = slice(0, mid), slice(mid, wide), slice(0, wide)
    first = pl.program_id(0) == 0

    def back(weights, x_ref, cols):
        below, above, middle = [
            nn_dot(weights[which][:, lanes], x_ref[lanes, :]).astype(BF16)
            for which, lanes in zip((0, 0, 1), (low, high, both))
        ]
        one, two = below[CHUNK:], above[CHUNK:]
        rows = (
            below[:CHUNK], above[:CHUNK], jnp.where(first, two, one),
            middle[:CHUNK], middle[CHUNK:], jnp.where(first, one, two),
        )
        for i, x in enumerate(rows):
            part_ref[i, :, :, :, cols] = x.reshape(shape)

    back(d_scores, bq_ref, slice(0, LANES))
    back(probs, bg_ref, slice(LANES, 2 * LANES))

    def forward(which, weights, rows):
        for i, lanes in enumerate((low, high)):
            left = jnp.concatenate([w[:, lanes] for w in weights], 0)
            acc = tn_dot(left, jnp.concatenate([rows[i], rows[2]], 0))
            acc = jnp.where(own[lanes], acc, 0.0)
            heads = [acc[h * part : (h + 1) * part] for h in range(GROUP)]
            out_ref[which, i * part : (i + 1) * part, :] = functools.reduce(jnp.add, heads)

    forward(0, probs, values)
    forward(1, d_scores, keys)


def attention(first_group, groups, lo, hi, stats, queries, d_context, tokens):
    n_query, width = queries.shape[1:]
    src, _, tok = tokens[0].shape[:3]
    wide = GROUP * n_query
    flat = pl.BlockSpec((None, 1, wide), lambda b, g: (b, 0, 0))
    rows = pl.BlockSpec((None, n_query, LANES), lambda b, g: (b, 0, first_group + g))
    table = pl.BlockSpec((None, None, 3, wide), lambda b, g: (b, first_group + g, 0, 0))

    def section(first, block):
        shape = (src, 2, tok, None, W, LANES)
        return pl.BlockSpec(shape, lambda b, g: (0, 0, 0, block(b), 0, first + g))

    def sections(first):
        far = pl.BlockSpec((src, 2, tok, W, LANES), lambda b, g: (0, 0, 0, 0, first + g))
        return [section(first, lambda b: b)] * 2 + [section(first, lambda b: 1 - b), far]

    edge, middle, ext = tokens
    tokens = (edge, middle, edge, ext)
    sections = sections(first_group) + sections(width // LANES + first_group)
    operand = pltpu.VMEM((wide, LANES), BF16)
    bias = pltpu.VMEM((2, 2 * CHUNK, wide), F32)
    scores = 8 * CHUNK * wide * groups
    common = dict(
        grid=(2, groups),
        compiler_params=pltpu.CompilerParams(dimension_semantics=("arbitrary", "arbitrary")),
    )
    if stats is None:
        return pl.pallas_call(
            stats_kernel,
            in_specs=[flat, flat, rows, rows] + sections,
            out_specs=table,
            out_shape=jax.ShapeDtypeStruct((2, groups, 3, wide), F32),
            scratch_shapes=[bias, operand, operand],
            cost_estimate=pl.CostEstimate(
                flops=4 * scores * LANES, bytes_accessed=6 * scores, transcendentals=scores
            ),
            name="softmax_stats",
            **common,
        )(lo, hi, queries, d_context, *tokens, *tokens)

    parts = pl.BlockSpec(
        (6, src, tok, None, W, 2 * LANES), lambda b, g: (0, 0, 0, b, 0, g)
    )
    return pl.pallas_call(
        grads_kernel,
        in_specs=[flat, flat, table, table, rows, rows] + sections,
        out_specs=[
            pl.BlockSpec((None, 2, n_query, LANES), lambda b, g: (b, 0, 0, g)),
            parts,
        ],
        out_shape=[
            jax.ShapeDtypeStruct((2, 2, n_query, groups * LANES), F32),
            jax.ShapeDtypeStruct((6, src, tok, 2, W, 2 * groups * LANES), BF16),
        ],
        scratch_shapes=[bias] + [operand] * 4,
        cost_estimate=pl.CostEstimate(
            flops=12 * scores * LANES, bytes_accessed=12 * scores, transcendentals=scores
        ),
        name="banded_grads",
        **common,
    )(lo, hi, *stats, queries, d_context, *tokens, *tokens)


TILE = 512


def project_kernel(x_ref, wk_ref, wv_ref, out_ref):
    n = pl.program_id(0)
    half = pl.num_programs(0) // 2

    @pl.when(n < half)
    def _():
        out_ref[...] = nn_dot(x_ref[...], wk_ref[...]).astype(BF16)

    @pl.when(n >= half)
    def _():
        out_ref[...] = nn_dot(x_ref[...], wv_ref[...]).astype(BF16)


def project_rows(x, key_weight, value_weight):
    width = x.shape[1]
    half = width // TILE
    return pl.pallas_call(
        project_kernel,
        grid=(2 * half,),
        in_specs=[
            pl.BlockSpec(x.shape, lambda n: (0, 0)),
            pl.BlockSpec((width, TILE), lambda n: (0, jnp.minimum(n, half - 1))),
            pl.BlockSpec((width, TILE), lambda n: (0, jnp.maximum(n - half, 0))),
        ],
        out_specs=pl.BlockSpec((x.shape[0], TILE), lambda n: (0, n)),
        out_shape=jax.ShapeDtypeStruct((x.shape[0], 2 * width), BF16),
        compiler_params=pltpu.CompilerParams(dimension_semantics=("arbitrary",)),
        cost_estimate=pl.CostEstimate(
            flops=4 * x.shape[0] * width * width,
            bytes_accessed=6 * x.shape[0] * width + 4 * width * width,
            transcendentals=0,
        ),
        name="project_rows",
    )(x, key_weight, value_weight)


def flips(n_dev, bit):
    return [(i, i ^ (1 << bit)) for i in range(n_dev)]


class Gather:
    def __init__(self, block, bits):
        self.block = block
        self.n_dev = 1 << bits
        self.order = list(range(bits - 1, -1, -1))

    def send(self):
        self.bit = self.order.pop(0)
        return self.block, flips(self.n_dev, self.bit)

    def receive(self, come):
        if self.bit == 0:
            self.block = jnp.stack([self.block, come])
            return
        mine = (lax.axis_index("tm") >> self.bit) & 1
        self.block = jnp.where(
            mine == 0,
            jnp.stack([self.block, come], axis=-3),
            jnp.stack([come, self.block], axis=-3),
        )


class Move:
    def __init__(self, block, perm):
        self.block = block
        self.order = [perm]

    def send(self):
        return self.block, self.order.pop(0)

    def receive(self, come):
        self.come = come


def beside(moving, work, *args):
    moving = [m for m in moving if m.order]
    sends = [m.send() for m in moving]
    args, aways = lax.optimization_barrier((args, [away for away, _ in sends]))
    comes = [lax.ppermute(away, "tm", perm) for away, (_, perm) in zip(aways, sends)]
    result, comes = lax.optimization_barrier((work(*args), comes))
    for m, come in zip(moving, comes):
        m.receive(come)
    return result


def shards(
    exo_tokens, queries, key_weight, value_weight, out_weight, gaze_valid, window_offset, cotangent
):
    n_query, width = queries.shape
    tok = exo_tokens.shape[1]
    n_dev = lax.axis_size("tm")
    bits = n_dev.bit_length() - 1
    src = n_dev // 2
    total = n_query * n_dev
    me = lax.axis_index("tm")
    upper_half = me >= src
    spot = me % src
    fence = lax.optimization_barrier

    owner_one = [(s, 2 * s) for s in range(src)] + [(src + s, 2 * s + 1) for s in range(src)]
    owner_two = [(s, 2 * s + 1) for s in range(src)] + [(src + s, 2 * s) for s in range(src)]
    valid_col = gaze_valid.astype(F32)[:, None]
    masked_grad = (cotangent.astype(F32) * valid_col).astype(BF16)
    note = jnp.zeros((W, width), BF16).at[0, :n_query].set(window_offset.astype(BF16))
    letter = jnp.concatenate([queries, masked_grad, note], axis=0)

    def frames(exo, *cuts):
        by_block = exo.reshape(src, 2, n_query, tok, width)
        runs = jnp.stack([by_block[:, :, cut : cut + W] for cut in cuts], axis=1)
        runs = runs.transpose(0, 1, 4, 2, 3, 5)
        return with_layout_constraint(runs, Layout(tuple(range(6))))

    later = fence(exo_tokens)
    outer = frames(exo_tokens, 0, n_query - W)
    inner = frames(later, W, 2 * W)
    halves = [list(range(src)), list(range(src, n_dev))]
    gather = Gather(masked_grad, bits)
    edge = lax.all_to_all(outer, "tm", 0, 0, axis_index_groups=halves, tiled=True)
    one = lax.ppermute(letter, "tm", [(b, a) for a, b in owner_one])
    two = lax.ppermute(letter, "tm", [(b, a) for a, b in owner_two])
    weights = jnp.concatenate([key_weight, value_weight], axis=1)
    edge, inner, weights, one, two = fence((edge, inner, weights, one, two))
    middle = lax.all_to_all(inner, "tm", 0, 0, axis_index_groups=halves, tiled=True)

    pair = jnp.where(upper_half, jnp.stack([two, one]), jnp.stack([one, two]))
    q_pair = pair[:, :n_query]
    g_pair = nt_dot(pair[:, n_query : 2 * n_query].reshape(-1, width), out_weight)
    g_pair = g_pair.astype(BF16).reshape(q_pair.shape)
    offsets = pair[:, 2 * n_query, :n_query].astype(jnp.int32)
    at = jnp.arange(n_query, dtype=jnp.int32)
    first = (2 * spot + jnp.arange(2, dtype=jnp.int32))[:, None] * n_query
    lower = jnp.maximum(at - W + offsets, -first)
    upper = jnp.minimum(at + offsets, total - 1 - first)

    def lanes(x):
        return jnp.tile(x.reshape(2, 2, 1, n_query // 2), (1, 1, GROUP, 1)).reshape(2, 1, -1)

    lo, hi = lanes(lower), lanes(upper)

    def project(x):
        flat = nn_dot(x.reshape(-1, width), weights).astype(BF16)
        return flat.reshape(x.shape[:-1] + (2 * width,))

    edge_kv = project(edge)
    up = [(i, i + 1) for i in range(n_dev - 1) if (i + 1) % src]
    local = jnp.stack([edge[:, 0, :, 1], edge[:, 1, :, 0]], axis=2)
    rows = [x.reshape(-1, width) for x in (edge[:, 0], edge[:, 1], local)]
    rows = jnp.concatenate(rows, axis=0)
    rows = jnp.pad(rows, ((0, rows.shape[0]), (0, 0)))
    low = Move(edge[:, 1, :, 1], up)
    high = Move(edge[:, 0, :, 0], [(target, source) for source, target in up])
    middle, edge_kv, q_pair, g_pair, lo, hi, rows, low.block, high.block = fence(
        (middle, edge_kv, q_pair, g_pair, lo, hi, rows, low.block, high.block)
    )
    middle_kv = beside(
        [low, high], project_rows, middle.reshape(-1, width), key_weight, value_weight
    ).reshape(middle.shape[:-1] + (2 * width,))
    ext = jnp.stack([low.come, high.come], axis=1)
    ext_kv = project(ext)
    tokens = (edge_kv, middle_kv, ext_kv)

    stats = beside(
        [gather],
        functools.partial(attention, 0, width // LANES, lo, hi, None),
        q_pair, g_pair, tokens,
    )
    swap = Move(stats, flips(n_dev, bits - 1))

    def fill(rows, middle, low, high):
        late = (middle[:, 0], middle[:, 1], jnp.stack([low, high], axis=2))
        at = rows.shape[0] // 2
        for x in late:
            x = x.reshape(-1, width)
            rows = lax.dynamic_update_slice_in_dim(rows, x, at, 0)
            at += x.shape[0]
        return rows

    sources = beside([gather, swap], fill, rows, middle, low.come, high.come)

    core = me & 1
    chips = [[2 * k + c for k in range(src)] for c in range(2)]

    def meet(term):
        rows = term.reshape(src, 2, -1, term.shape[1])
        away = lax.dynamic_index_in_dim(rows, 1 - core, 1, keepdims=False)
        keep = lax.dynamic_index_in_dim(rows, core, 1, keepdims=False)
        return Move(away, flips(n_dev, 0)), keep

    def scatter(block):
        return lax.all_to_all(block, "tm", 0, 0, axis_index_groups=chips, tiled=True)

    def add(x, y):
        return (x.astype(F32) + y.astype(F32)).astype(BF16)

    def half_context(part):
        half = upper_half.astype(jnp.int32)
        return [
            Move(lax.dynamic_index_in_dim(part, half, 0, keepdims=False), owner_one),
            Move(lax.dynamic_index_in_dim(part, 1 - half, 0, keepdims=False), owner_two),
        ]

    def weigh(g):
        return tn_dot(sources, g.reshape(sources.shape[0], -1)).astype(BF16)

    def assemble(*parts):
        sums = [(a + b).astype(BF16) for a, b in zip(parts[::2], parts[1::2])]
        return jnp.concatenate(sums, axis=2)

    trades, shares, ready, start = [], [], None, 0
    for call, groups in enumerate(SPLIT):
        work = functools.partial(attention, start, groups, lo, hi, (swap.block, swap.come))
        start += groups
        if ready is not None:
            ready, q_pair = fence((ready, q_pair))
            share = scatter(ready)
        partial, grads = beside([gather], work, q_pair, g_pair, tokens)
        trade = half_context(partial)
        trades += trade
        term = beside(trade + [gather], weigh, grads)
        if ready is not None:
            shares.append(share)
        if call < len(SPLIT) - 1:
            away, keep = meet(term)
            keep = beside([away, gather], lambda x: x, keep)
            ready = add(keep, away.come)

    context, d_query = assemble(*[move.come for move in trades])
    away, keep = meet(term)
    partner = Move(context, flips(n_dev, 0))
    keep, context = beside([away, partner], lambda *x: x, keep, context)
    ready, shares = fence((add(keep, away.come), shares))

    columns = jnp.concatenate(
        [x.reshape(n_query, src, -1).swapaxes(0, 1) for x in (context, partner.come)], axis=2
    )
    if ready.shape[1] == n_query:
        packed = scatter(jnp.concatenate([ready, columns], axis=2))
        share, columns = packed[:, :, : ready.shape[2]], packed[:, :, ready.shape[2] :]
    else:
        share, columns = scatter(ready), scatter(columns)
    shares.append(share)
    attended = (nn_dot(context, out_weight) * valid_col).astype(BF16)
    columns = columns.reshape(src * n_query, -1)
    all_grad = gather.block.reshape(2, src * n_query, width)
    cut = columns.shape[1] // 2
    d_out = tn_dot(columns[:, :cut], all_grad[0]) + tn_dot(columns[:, cut:], all_grad[1])
    d_out = lax.dynamic_slice_in_dim(d_out, core * (cut // 2), cut // 2, 0)
    sums = [jnp.sum(share.astype(F32), axis=0) for share in shares]

    def heads(which):
        cuts = [(x, (2 * i + which) * LANES) for x, n in zip(sums, SPLIT) for i in range(n)]
        return jnp.concatenate([x[:, i : i + LANES] for x, i in cuts], axis=1)

    return attended, d_query, heads(0), heads(1), d_out


def solution(mesh):
    in_specs = (
        P("rep", "tm", None),
        P(("rep", "tm"), None),
        P(),
        P(),
        P(),
        P(("rep", "tm")),
        P(("rep", "tm")),
        P(("rep", "tm"), None),
    )
    out_specs = (
        P(("rep", "tm"), None),
        P(("rep", "tm"), None),
        P(("rep", "tm"), None),
        P(("rep", "tm"), None),
        P(("rep", "tm"), None),
    )

    return jax.shard_map(shards, mesh=mesh, in_specs=in_specs, out_specs=out_specs, check_vma=False)
```

```python
import functools

import jax
import jax.numpy as jnp
from jax import lax
from jax.experimental.layout import Layout, with_layout_constraint
from jax.experimental import pallas as pl
from jax.experimental.pallas import tpu as pltpu
from jax.sharding import PartitionSpec as P


HD = 64
W = 16
GROUP = 4
LANES = GROUP * HD
SPLIT = (2, 2)
CHUNK = 256
F32 = jnp.float32
BF16 = jnp.bfloat16


def tn_dot(a, b):
    return lax.dot_general(a, b, (((0,), (0,)), ((), ())), preferred_element_type=F32)


def nt_dot(a, b):
    return lax.dot_general(a, b, (((1,), (1,)), ((), ())), preferred_element_type=F32)


def nn_dot(a, b):
    return jnp.dot(a, b, preferred_element_type=F32)


def own_head(n_query):
    wide = GROUP * n_query
    row_head = lax.broadcasted_iota(jnp.int32, (wide, LANES), 0) // (n_query // 2) % GROUP
    col_head = lax.broadcasted_iota(jnp.int32, (wide, LANES), 1) // HD
    return row_head == col_head


def spread(x, own):
    part = x.shape[0] // 2
    rows = jnp.concatenate([x[:part]] * GROUP + [x[part:]] * GROUP, 0)
    return jnp.where(own, rows, jnp.zeros_like(rows))


def scaled(x):
    return (x.astype(F32) * HD ** (-0.5)).astype(BF16)


def fill_bias(lo_ref, hi_ref, bias_ref, n_query):
    wide = GROUP * n_query
    lo = lo_ref[...]
    hi = hi_ref[...]
    rows = lax.broadcasted_iota(jnp.int32, (CHUNK, wide), 0)
    near = rows % W
    second = lax.broadcasted_iota(jnp.int32, (CHUNK, wide), 1) >= wide // 2
    frames = (
        near + jnp.where(second, n_query - W, 0),
        near + jnp.where(second, n_query, -W),
        near + W,
        near + 2 * W,
    )
    for i, frame in enumerate(frames):
        at = slice(i % 2 * CHUNK, (i % 2 + 1) * CHUNK)
        bias_ref[i // 2, at, :] = jnp.where((frame >= lo) & (frame <= hi), 0.0, -1e30)


def load(ref, side):
    return ref[:, side].reshape(CHUNK, LANES)


def row_groups(edge_ref, mid_ref, near_ref, far_ref):
    lower = pl.program_id(0) == 0
    below = jnp.where(lower, load(far_ref, 0), load(near_ref, 1))
    above = jnp.where(lower, load(near_ref, 0), load(far_ref, 1))
    return (
        jnp.concatenate([load(edge_ref, 0), below], 0),
        jnp.concatenate([load(edge_ref, 1), above], 0),
        jnp.concatenate([load(mid_ref, 0), load(mid_ref, 1)], 0),
    )


def group_dots(rows, x_ref):
    mid = x_ref.shape[0] // 2
    pair = jnp.concatenate([nt_dot(rows[0], x_ref[:mid, :]), nt_dot(rows[1], x_ref[mid:, :])], 1)
    return pair, nt_dot(rows[2], x_ref[...])


def fold(x):
    return x.reshape(x.shape[0] // 8, 8, x.shape[1])


def stats_kernel(
    lo_ref, hi_ref, q_ref, g_ref,
    ke_ref, km_ref, kn_ref, kf_ref, ve_ref, vm_ref, vn_ref, vf_ref,
    out_ref, bias_ref, bq_ref, bg_ref,
):
    n_query = q_ref.shape[0]
    own = own_head(n_query)
    bq_ref[...] = scaled(spread(q_ref[...], own))
    bg_ref[...] = scaled(spread(g_ref[...], own))

    @pl.when(pl.program_id(1) == 0)
    def _():
        fill_bias(lo_ref, hi_ref, bias_ref, n_query)

    scores = group_dots(row_groups(ke_ref, km_ref, kn_ref, kf_ref), bq_ref)
    d_probs = group_dots(row_groups(ve_ref, vm_ref, vn_ref, vf_ref), bg_ref)
    scores = [s + bias_ref[i] for i, s in enumerate(scores)]
    tops = [jnp.max(fold(s), axis=0) for s in scores]
    top = jnp.max(jnp.maximum(*tops), axis=0, keepdims=True)
    total, weighted = [], []
    for s, dp in zip(scores, d_probs):
        e = jnp.exp(s - top)
        total.append(jnp.sum(fold(e), axis=0))
        weighted.append(jnp.sum(fold(e * dp), axis=0))
    out_ref[0:1, :] = top
    out_ref[1:2, :] = jnp.sum(total[0] + total[1], axis=0, keepdims=True)
    out_ref[2:3, :] = jnp.sum(weighted[0] + weighted[1], axis=0, keepdims=True)


def grads_kernel(
    lo_ref, hi_ref, one_ref, two_ref, q_ref, g_ref,
    ke_ref, km_ref, kn_ref, kf_ref, ve_ref, vm_ref, vn_ref, vf_ref,
    out_ref, part_ref,
    bias_ref, bq_ref, bg_ref, bqs_ref, bgs_ref,
):
    n_query = q_ref.shape[0]
    part = n_query // 2
    wide = GROUP * n_query
    mid = wide // 2
    own = own_head(n_query)
    bq_ref[...] = spread(q_ref[...], own)
    bg_ref[...] = spread(g_ref[...], own)
    bqs_ref[...] = scaled(bq_ref[...])
    bgs_ref[...] = scaled(bg_ref[...])

    @pl.when(pl.program_id(1) == 0)
    def _():
        fill_bias(lo_ref, hi_ref, bias_ref, n_query)

    top = jnp.maximum(one_ref[0:1, :], two_ref[0:1, :])
    one = jnp.exp(one_ref[0:1, :] - top)
    two = jnp.exp(two_ref[0:1, :] - top)
    inverse = 1.0 / (one_ref[1:2, :] * one + two_ref[1:2, :] * two)
    mean = (one_ref[2:3, :] * one + two_ref[2:3, :] * two) * inverse
    keys = row_groups(ke_ref, km_ref, kn_ref, kf_ref)
    values = row_groups(ve_ref, vm_ref, vn_ref, vf_ref)
    probs, d_scores = [], []
    for i, (s, dp) in enumerate(zip(group_dots(keys, bqs_ref), group_dots(values, bgs_ref))):
        p = jnp.exp(s + bias_ref[i] - top) * inverse
        probs.append(p.astype(BF16))
        d_scores.append((p * (dp - mean)).astype(BF16))

    shape = part_ref.shape[1:4] + (LANES,)
    low, high, both = slice(0, mid), slice(mid, wide), slice(0, wide)
    first = pl.program_id(0) == 0

    def back(weights, x_ref, cols):
        below, above, middle = [
            nn_dot(weights[which][:, lanes], x_ref[lanes, :]).astype(BF16)
            for which, lanes in zip((0, 0, 1), (low, high, both))
        ]
        one, two = below[CHUNK:], above[CHUNK:]
        rows = (
            below[:CHUNK], above[:CHUNK], jnp.where(first, two, one),
            middle[:CHUNK], middle[CHUNK:], jnp.where(first, one, two),
        )
        for i, x in enumerate(rows):
            part_ref[i, :, :, :, cols] = x.reshape(shape)

    back(d_scores, bq_ref, slice(0, LANES))
    back(probs, bg_ref, slice(LANES, 2 * LANES))

    def forward(which, weights, rows):
        for i, lanes in enumerate((low, high)):
            left = jnp.concatenate([w[:, lanes] for w in weights], 0)
            acc = tn_dot(left, jnp.concatenate([rows[i], rows[2]], 0))
            acc = jnp.where(own[lanes], acc, 0.0)
            heads = [acc[h * part : (h + 1) * part] for h in range(GROUP)]
            out_ref[which, i * part : (i + 1) * part, :] = functools.reduce(jnp.add, heads)

    forward(0, probs, values)
    forward(1, d_scores, keys)


def attention(first_group, groups, lo, hi, stats, queries, d_context, tokens):
    n_query, width = queries.shape[1:]
    src, _, tok = tokens[0].shape[:3]
    wide = GROUP * n_query
    flat = pl.BlockSpec((None, 1, wide), lambda b, g: (b, 0, 0))
    rows = pl.BlockSpec((None, n_query, LANES), lambda b, g: (b, 0, first_group + g))
    table = pl.BlockSpec((None, None, 3, wide), lambda b, g: (b, first_group + g, 0, 0))

    def section(first, block):
        shape = (src, 2, tok, None, W, LANES)
        return pl.BlockSpec(shape, lambda b, g: (0, 0, 0, block(b), 0, first + g))

    def sections(first):
        far = pl.BlockSpec((src, 2, tok, W, LANES), lambda b, g: (0, 0, 0, 0, first + g))
        return [section(first, lambda b: b)] * 2 + [section(first, lambda b: 1 - b), far]

    edge, middle, ext = tokens
    tokens = (edge, middle, edge, ext)
    sections = sections(first_group) + sections(width // LANES + first_group)
    operand = pltpu.VMEM((wide, LANES), BF16)
    bias = pltpu.VMEM((2, 2 * CHUNK, wide), F32)
    scores = 8 * CHUNK * wide * groups
    common = dict(
        grid=(2, groups),
        compiler_params=pltpu.CompilerParams(dimension_semantics=("arbitrary", "arbitrary")),
    )
    if stats is None:
        return pl.pallas_call(
            stats_kernel,
            in_specs=[flat, flat, rows, rows] + sections,
            out_specs=table,
            out_shape=jax.ShapeDtypeStruct((2, groups, 3, wide), F32),
            scratch_shapes=[bias, operand, operand],
            cost_estimate=pl.CostEstimate(
                flops=4 * scores * LANES, bytes_accessed=6 * scores, transcendentals=scores
            ),
            name="softmax_stats",
            **common,
        )(lo, hi, queries, d_context, *tokens, *tokens)

    parts = pl.BlockSpec(
        (6, src, tok, None, W, 2 * LANES), lambda b, g: (0, 0, 0, b, 0, g)
    )
    return pl.pallas_call(
        grads_kernel,
        in_specs=[flat, flat, table, table, rows, rows] + sections,
        out_specs=[
            pl.BlockSpec((None, 2, n_query, LANES), lambda b, g: (b, 0, 0, g)),
            parts,
        ],
        out_shape=[
            jax.ShapeDtypeStruct((2, 2, n_query, groups * LANES), F32),
            jax.ShapeDtypeStruct((6, src, tok, 2, W, 2 * groups * LANES), BF16),
        ],
        scratch_shapes=[bias] + [operand] * 4,
        cost_estimate=pl.CostEstimate(
            flops=12 * scores * LANES, bytes_accessed=12 * scores, transcendentals=scores
        ),
        name="banded_grads",
        **common,
    )(lo, hi, *stats, queries, d_context, *tokens, *tokens)


TILE = 512


def project_kernel(x_ref, wk_ref, wv_ref, out_ref):
    n = pl.program_id(0)
    half = pl.num_programs(0) // 2

    @pl.when(n < half)
    def _():
        out_ref[...] = nn_dot(x_ref[...], wk_ref[...]).astype(BF16)

    @pl.when(n >= half)
    def _():
        out_ref[...] = nn_dot(x_ref[...], wv_ref[...]).astype(BF16)


def project_rows(x, key_weight, value_weight):
    width = x.shape[1]
    half = width // TILE
    return pl.pallas_call(
        project_kernel,
        grid=(2 * half,),
        in_specs=[
            pl.BlockSpec(x.shape, lambda n: (0, 0)),
            pl.BlockSpec((width, TILE), lambda n: (0, jnp.minimum(n, half - 1))),
            pl.BlockSpec((width, TILE), lambda n: (0, jnp.maximum(n - half, 0))),
        ],
        out_specs=pl.BlockSpec((x.shape[0], TILE), lambda n: (0, n)),
        out_shape=jax.ShapeDtypeStruct((x.shape[0], 2 * width), BF16),
        compiler_params=pltpu.CompilerParams(dimension_semantics=("arbitrary",)),
        cost_estimate=pl.CostEstimate(
            flops=4 * x.shape[0] * width * width,
            bytes_accessed=6 * x.shape[0] * width + 4 * width * width,
            transcendentals=0,
        ),
        name="project_rows",
    )(x, key_weight, value_weight)


def flips(n_dev, bit):
    return [(i, i ^ (1 << bit)) for i in range(n_dev)]


def place(rows, blocks, at):
    for x in blocks:
        rows = lax.dynamic_update_slice_in_dim(rows, x, at, 0)
        at += x.shape[0]
    return rows


class Gather:
    def __init__(self, block, bits):
        self.block = block
        self.n_dev = 1 << bits
        self.order = list(range(bits - 1, -1, -1))

    def send(self):
        self.bit = self.order.pop(0)
        return self.block, flips(self.n_dev, self.bit)

    def receive(self, come):
        if self.bit == 0:
            self.block = jnp.stack([self.block, come])
            return
        mine = (lax.axis_index("tm") >> self.bit) & 1
        self.block = jnp.where(
            mine == 0,
            jnp.stack([self.block, come], axis=-3),
            jnp.stack([come, self.block], axis=-3),
        )


class Move:
    def __init__(self, block, perm):
        self.block = block
        self.order = [perm]

    def send(self):
        return self.block, self.order.pop(0)

    def receive(self, come):
        self.come = come


def beside(moving, work, *args):
    moving = [m for m in moving if m.order]
    sends = [m.send() for m in moving]
    args, aways = lax.optimization_barrier((args, [away for away, _ in sends]))
    comes = [lax.ppermute(away, "tm", perm) for away, (_, perm) in zip(aways, sends)]
    result, comes = lax.optimization_barrier((work(*args), comes))
    for m, come in zip(moving, comes):
        m.receive(come)
    return result


def shards(
    exo_tokens, queries, key_weight, value_weight, out_weight, gaze_valid, window_offset, cotangent
):
    n_query, width = queries.shape
    tok = exo_tokens.shape[1]
    n_dev = lax.axis_size("tm")
    bits = n_dev.bit_length() - 1
    src = n_dev // 2
    total = n_query * n_dev
    me = lax.axis_index("tm")
    upper_half = me >= src
    spot = me % src
    fence = lax.optimization_barrier

    owner_one = [(s, 2 * s) for s in range(src)] + [(src + s, 2 * s + 1) for s in range(src)]
    owner_two = [(s, 2 * s + 1) for s in range(src)] + [(src + s, 2 * s) for s in range(src)]
    valid_col = gaze_valid.astype(F32)[:, None]
    masked_grad = (cotangent.astype(F32) * valid_col).astype(BF16)
    note = jnp.zeros((W, width), BF16).at[0, :n_query].set(window_offset.astype(BF16))
    letter = jnp.concatenate([queries, masked_grad, note], axis=0)

    def frames(exo, *cuts):
        by_block = exo.reshape(src, 2, n_query, tok, width)
        runs = jnp.stack([by_block[:, :, cut : cut + W] for cut in cuts], axis=1)
        runs = runs.transpose(0, 1, 4, 2, 3, 5)
        return with_layout_constraint(runs, Layout(tuple(range(6))))

    later = fence(exo_tokens)
    outer = frames(exo_tokens, 0, n_query - W)
    inner = frames(later, W, 2 * W)
    halves = [list(range(src)), list(range(src, n_dev))]
    gather = Gather(masked_grad, bits)
    edge = lax.all_to_all(outer, "tm", 0, 0, axis_index_groups=halves, tiled=True)
    one = lax.ppermute(letter, "tm", [(b, a) for a, b in owner_one])
    two = lax.ppermute(letter, "tm", [(b, a) for a, b in owner_two])
    weights = jnp.concatenate([key_weight, value_weight], axis=1)
    edge, inner, weights, one, two = fence((edge, inner, weights, one, two))
    middle = lax.all_to_all(inner, "tm", 0, 0, axis_index_groups=halves, tiled=True)

    pair = jnp.where(upper_half, jnp.stack([two, one]), jnp.stack([one, two]))
    q_pair = pair[:, :n_query]
    g_pair = nt_dot(pair[:, n_query : 2 * n_query].reshape(-1, width), out_weight)
    g_pair = g_pair.astype(BF16).reshape(q_pair.shape)
    offsets = pair[:, 2 * n_query, :n_query].astype(jnp.int32)
    at = jnp.arange(n_query, dtype=jnp.int32)
    first = (2 * spot + jnp.arange(2, dtype=jnp.int32))[:, None] * n_query
    lower = jnp.maximum(at - W + offsets, -first)
    upper = jnp.minimum(at + offsets, total - 1 - first)

    def lanes(x):
        return jnp.tile(x.reshape(2, 2, 1, n_query // 2), (1, 1, GROUP, 1)).reshape(2, 1, -1)

    lo, hi = lanes(lower), lanes(upper)

    def project(x):
        flat = nn_dot(x.reshape(-1, width), weights).astype(BF16)
        return flat.reshape(x.shape[:-1] + (2 * width,))

    edge_kv = project(edge)
    up = [(i, i + 1) for i in range(n_dev - 1) if (i + 1) % src]
    local = jnp.stack([edge[:, 0, :, 1], edge[:, 1, :, 0]], axis=2)
    early = [x.reshape(-1, width) for x in (edge[:, 0], edge[:, 1], local)]
    n_early = sum(x.shape[0] for x in early)
    rows = place(jnp.zeros((2 * n_early, width), BF16), early, 0)
    low = Move(edge[:, 1, :, 1], up)
    high = Move(edge[:, 0, :, 0], [(target, source) for source, target in up])
    middle, edge_kv, q_pair, g_pair, lo, hi, rows, low.block, high.block = fence(
        (middle, edge_kv, q_pair, g_pair, lo, hi, rows, low.block, high.block)
    )
    middle_kv = beside(
        [low, high], project_rows, middle.reshape(-1, width), key_weight, value_weight
    ).reshape(middle.shape[:-1] + (2 * width,))
    ext = jnp.stack([low.come, high.come], axis=1)
    ext_kv = project(ext)
    tokens = (edge_kv, middle_kv, ext_kv)

    stats = beside(
        [gather],
        functools.partial(attention, 0, width // LANES, lo, hi, None),
        q_pair, g_pair, tokens,
    )
    swap = Move(stats, flips(n_dev, bits - 1))

    def fill(rows, middle, low, high):
        late = (middle[:, 0], middle[:, 1], jnp.stack([low, high], axis=2))
        return place(rows, [x.reshape(-1, width) for x in late], n_early)

    sources = beside([gather, swap], fill, rows, middle, low.come, high.come)

    core = me & 1
    chips = [[2 * k + c for k in range(src)] for c in range(2)]

    def meet(term):
        rows = term.reshape(src, 2, -1, term.shape[1])
        away = lax.dynamic_index_in_dim(rows, 1 - core, 1, keepdims=False)
        keep = lax.dynamic_index_in_dim(rows, core, 1, keepdims=False)
        return Move(away, flips(n_dev, 0)), keep

    def scatter(block):
        return lax.all_to_all(block, "tm", 0, 0, axis_index_groups=chips, tiled=True)

    def add(x, y):
        return (x.astype(F32) + y.astype(F32)).astype(BF16)

    def half_context(part):
        half = upper_half.astype(jnp.int32)
        return [
            Move(lax.dynamic_index_in_dim(part, half, 0, keepdims=False), owner_one),
            Move(lax.dynamic_index_in_dim(part, 1 - half, 0, keepdims=False), owner_two),
        ]

    def weigh(g):
        return tn_dot(sources, g.reshape(sources.shape[0], -1)).astype(BF16)

    def assemble(*parts):
        sums = [(a + b).astype(BF16) for a, b in zip(parts[::2], parts[1::2])]
        return jnp.concatenate(sums, axis=2)

    trades, shares, ready, start = [], [], None, 0
    for call, groups in enumerate(SPLIT):
        work = functools.partial(attention, start, groups, lo, hi, (swap.block, swap.come))
        start += groups
        if ready is not None:
            ready, q_pair = fence((ready, q_pair))
            share = scatter(ready)
        partial, grads = beside([gather], work, q_pair, g_pair, tokens)
        trade = half_context(partial)
        trades += trade
        term = beside(trade + [gather], weigh, grads)
        if ready is not None:
            shares.append(share)
        if call < len(SPLIT) - 1:
            away, keep = meet(term)
            keep = beside([away, gather], lambda x: x, keep)
            ready = add(keep, away.come)

    context, d_query = assemble(*[move.come for move in trades])
    away, keep = meet(term)
    partner = Move(context, flips(n_dev, 0))
    keep, context = beside([away, partner], lambda *x: x, keep, context)
    ready, shares = fence((add(keep, away.come), shares))

    columns = jnp.concatenate(
        [x.reshape(n_query, src, -1).swapaxes(0, 1) for x in (context, partner.come)], axis=2
    )
    if ready.shape[1] == n_query:
        packed = scatter(jnp.concatenate([ready, columns], axis=2))
        share, columns = packed[:, :, : ready.shape[2]], packed[:, :, ready.shape[2] :]
    else:
        share, columns = scatter(ready), scatter(columns)
    shares.append(share)
    attended = (nn_dot(context, out_weight) * valid_col).astype(BF16)
    columns = columns.reshape(src * n_query, -1)
    all_grad = gather.block.reshape(2, src * n_query, width)
    cut = columns.shape[1] // 2
    d_out = tn_dot(columns[:, :cut], all_grad[0]) + tn_dot(columns[:, cut:], all_grad[1])
    d_out = lax.dynamic_slice_in_dim(d_out, core * (cut // 2), cut // 2, 0)
    sums = [jnp.sum(share.astype(F32), axis=0) for share in shares]

    def heads(which):
        cuts = [(x, (2 * i + which) * LANES) for x, n in zip(sums, SPLIT) for i in range(n)]
        return jnp.concatenate([x[:, i : i + LANES] for x, i in cuts], axis=1)

    return attended, d_query, heads(0), heads(1), d_out


def solution(mesh):
    in_specs = (
        P("rep", "tm", None),
        P(("rep", "tm"), None),
        P(),
        P(),
        P(),
        P(("rep", "tm")),
        P(("rep", "tm")),
        P(("rep", "tm"), None),
    )
    out_specs = (
        P(("rep", "tm"), None),
        P(("rep", "tm"), None),
        P(("rep", "tm"), None),
        P(("rep", "tm"), None),
        P(("rep", "tm"), None),
    )

    return jax.shard_map(shards, mesh=mesh, in_specs=in_specs, out_specs=out_specs, check_vma=False)
```

```python
import functools

import jax
import jax.numpy as jnp
from jax import lax
from jax.experimental.layout import Layout, with_layout_constraint
from jax.experimental import pallas as pl
from jax.experimental.pallas import tpu as pltpu
from jax.sharding import PartitionSpec as P


HD = 64
W = 16
GROUP = 4
LANES = GROUP * HD
SPLIT = (2, 2)
CHUNK = 256
F32 = jnp.float32
BF16 = jnp.bfloat16


def tn_dot(a, b):
    return lax.dot_general(a, b, (((0,), (0,)), ((), ())), preferred_element_type=F32)


def nt_dot(a, b):
    return lax.dot_general(a, b, (((1,), (1,)), ((), ())), preferred_element_type=F32)


def nn_dot(a, b):
    return jnp.dot(a, b, preferred_element_type=F32)


def own_head(n_query):
    wide = GROUP * n_query
    row_head = lax.broadcasted_iota(jnp.int32, (wide, LANES), 0) // (n_query // 2) % GROUP
    col_head = lax.broadcasted_iota(jnp.int32, (wide, LANES), 1) // HD
    return row_head == col_head


def spread(x, own):
    part = x.shape[0] // 2
    rows = jnp.concatenate([x[:part]] * GROUP + [x[part:]] * GROUP, 0)
    return jnp.where(own, rows, jnp.zeros_like(rows))


def scaled(x):
    return (x.astype(F32) * HD ** (-0.5)).astype(BF16)


def fill_bias(lo_ref, hi_ref, bias_ref, n_query):
    wide = GROUP * n_query
    lo = lo_ref[...]
    hi = hi_ref[...]
    rows = lax.broadcasted_iota(jnp.int32, (CHUNK, wide), 0)
    near = rows % W
    second = lax.broadcasted_iota(jnp.int32, (CHUNK, wide), 1) >= wide // 2
    frames = (
        near + jnp.where(second, n_query - W, 0),
        near + jnp.where(second, n_query, -W),
        near + W,
        near + 2 * W,
    )
    for i, frame in enumerate(frames):
        at = slice(i % 2 * CHUNK, (i % 2 + 1) * CHUNK)
        bias_ref[i // 2, at, :] = jnp.where((frame >= lo) & (frame <= hi), 0.0, -1e30)


def load(ref, side):
    return ref[:, side].reshape(CHUNK, LANES)


def row_groups(edge_ref, mid_ref, near_ref, far_ref):
    lower = pl.program_id(0) == 0
    below = jnp.where(lower, load(far_ref, 0), load(near_ref, 1))
    above = jnp.where(lower, load(near_ref, 0), load(far_ref, 1))
    return (
        jnp.concatenate([load(edge_ref, 0), below], 0),
        jnp.concatenate([load(edge_ref, 1), above], 0),
        jnp.concatenate([load(mid_ref, 0), load(mid_ref, 1)], 0),
    )


def group_dots(rows, x_ref):
    mid = x_ref.shape[0] // 2
    pair = jnp.concatenate([nt_dot(rows[0], x_ref[:mid, :]), nt_dot(rows[1], x_ref[mid:, :])], 1)
    return pair, nt_dot(rows[2], x_ref[...])


def fold(x):
    return x.reshape(x.shape[0] // 8, 8, x.shape[1])


def stats_kernel(
    lo_ref, hi_ref, q_ref, g_ref,
    ke_ref, km_ref, kn_ref, kf_ref, ve_ref, vm_ref, vn_ref, vf_ref,
    out_ref, bias_ref, bq_ref, bg_ref,
):
    n_query = q_ref.shape[0]
    own = own_head(n_query)
    bq_ref[...] = scaled(spread(q_ref[...], own))
    bg_ref[...] = scaled(spread(g_ref[...], own))

    @pl.when(pl.program_id(1) == 0)
    def _():
        fill_bias(lo_ref, hi_ref, bias_ref, n_query)

    scores = group_dots(row_groups(ke_ref, km_ref, kn_ref, kf_ref), bq_ref)
    d_probs = group_dots(row_groups(ve_ref, vm_ref, vn_ref, vf_ref), bg_ref)
    scores = [s + bias_ref[i] for i, s in enumerate(scores)]
    tops = [jnp.max(fold(s), axis=0) for s in scores]
    top = jnp.max(jnp.maximum(*tops), axis=0, keepdims=True)
    total, weighted = [], []
    for s, dp in zip(scores, d_probs):
        e = jnp.exp(s - top)
        total.append(jnp.sum(fold(e), axis=0))
        weighted.append(jnp.sum(fold(e * dp), axis=0))
    out_ref[0:1, :] = top
    out_ref[1:2, :] = jnp.sum(total[0] + total[1], axis=0, keepdims=True)
    out_ref[2:3, :] = jnp.sum(weighted[0] + weighted[1], axis=0, keepdims=True)


def grads_kernel(
    lo_ref, hi_ref, one_ref, two_ref, q_ref, g_ref,
    ke_ref, km_ref, kn_ref, kf_ref, ve_ref, vm_ref, vn_ref, vf_ref,
    out_ref, part_ref,
    bias_ref, bq_ref, bg_ref, bqs_ref, bgs_ref,
):
    n_query = q_ref.shape[0]
    part = n_query // 2
    wide = GROUP * n_query
    mid = wide // 2
    own = own_head(n_query)
    bq_ref[...] = spread(q_ref[...], own)
    bg_ref[...] = spread(g_ref[...], own)
    bqs_ref[...] = scaled(bq_ref[...])
    bgs_ref[...] = scaled(bg_ref[...])

    @pl.when(pl.program_id(1) == 0)
    def _():
        fill_bias(lo_ref, hi_ref, bias_ref, n_query)

    top = jnp.maximum(one_ref[0:1, :], two_ref[0:1, :])
    one = jnp.exp(one_ref[0:1, :] - top)
    two = jnp.exp(two_ref[0:1, :] - top)
    inverse = 1.0 / (one_ref[1:2, :] * one + two_ref[1:2, :] * two)
    mean = (one_ref[2:3, :] * one + two_ref[2:3, :] * two) * inverse
    keys = row_groups(ke_ref, km_ref, kn_ref, kf_ref)
    values = row_groups(ve_ref, vm_ref, vn_ref, vf_ref)
    probs, d_scores = [], []
    for i, (s, dp) in enumerate(zip(group_dots(keys, bqs_ref), group_dots(values, bgs_ref))):
        p = jnp.exp(s + bias_ref[i] - top) * inverse
        probs.append(p.astype(BF16))
        d_scores.append((p * (dp - mean)).astype(BF16))

    shape = part_ref.shape[1:4] + (LANES,)
    low, high, both = slice(0, mid), slice(mid, wide), slice(0, wide)
    first = pl.program_id(0) == 0

    def back(weights, x_ref, cols):
        below, above, middle = [
            nn_dot(weights[which][:, lanes], x_ref[lanes, :]).astype(BF16)
            for which, lanes in zip((0, 0, 1), (low, high, both))
        ]
        one, two = below[CHUNK:], above[CHUNK:]
        rows = (
            below[:CHUNK], above[:CHUNK], jnp.where(first, two, one),
            middle[:CHUNK], middle[CHUNK:], jnp.where(first, one, two),
        )
        for i, x in enumerate(rows):
            part_ref[i, :, :, :, cols] = x.reshape(shape)

    back(d_scores, bq_ref, slice(0, LANES))
    back(probs, bg_ref, slice(LANES, 2 * LANES))

    def forward(which, weights, rows):
        for i, lanes in enumerate((low, high)):
            left = jnp.concatenate([w[:, lanes] for w in weights], 0)
            acc = tn_dot(left, jnp.concatenate([rows[i], rows[2]], 0))
            acc = jnp.where(own[lanes], acc, 0.0)
            heads = [acc[h * part : (h + 1) * part] for h in range(GROUP)]
            out_ref[which, i * part : (i + 1) * part, :] = functools.reduce(jnp.add, heads)

    forward(0, probs, values)
    forward(1, d_scores, keys)


def attention(first_group, groups, lo, hi, stats, queries, d_context, tokens):
    n_query, width = queries.shape[1:]
    src, _, tok = tokens[0].shape[:3]
    wide = GROUP * n_query
    flat = pl.BlockSpec((None, 1, wide), lambda b, g: (b, 0, 0))
    rows = pl.BlockSpec((None, n_query, LANES), lambda b, g: (b, 0, first_group + g))
    table = pl.BlockSpec((None, None, 3, wide), lambda b, g: (b, first_group + g, 0, 0))

    def section(first, block):
        shape = (src, 2, tok, None, W, LANES)
        return pl.BlockSpec(shape, lambda b, g: (0, 0, 0, block(b), 0, first + g))

    def sections(first):
        far = pl.BlockSpec((src, 2, tok, W, LANES), lambda b, g: (0, 0, 0, 0, first + g))
        return [section(first, lambda b: b)] * 2 + [section(first, lambda b: 1 - b), far]

    edge, middle, ext = tokens
    tokens = (edge, middle, edge, ext)
    sections = sections(first_group) + sections(width // LANES + first_group)
    operand = pltpu.VMEM((wide, LANES), BF16)
    bias = pltpu.VMEM((2, 2 * CHUNK, wide), F32)
    scores = 8 * CHUNK * wide * groups
    common = dict(
        grid=(2, groups),
        compiler_params=pltpu.CompilerParams(dimension_semantics=("arbitrary", "arbitrary")),
    )
    if stats is None:
        return pl.pallas_call(
            stats_kernel,
            in_specs=[flat, flat, rows, rows] + sections,
            out_specs=table,
            out_shape=jax.ShapeDtypeStruct((2, groups, 3, wide), F32),
            scratch_shapes=[bias, operand, operand],
            cost_estimate=pl.CostEstimate(
                flops=4 * scores * LANES, bytes_accessed=6 * scores, transcendentals=scores
            ),
            name="softmax_stats",
            **common,
        )(lo, hi, queries, d_context, *tokens, *tokens)

    parts = pl.BlockSpec(
        (6, src, tok, None, W, 2 * LANES), lambda b, g: (0, 0, 0, b, 0, g)
    )
    return pl.pallas_call(
        grads_kernel,
        in_specs=[flat, flat, table, table, rows, rows] + sections,
        out_specs=[
            pl.BlockSpec((None, 2, n_query, LANES), lambda b, g: (b, 0, 0, g)),
            parts,
        ],
        out_shape=[
            jax.ShapeDtypeStruct((2, 2, n_query, groups * LANES), F32),
            jax.ShapeDtypeStruct((6, src, tok, 2, W, 2 * groups * LANES), BF16),
        ],
        scratch_shapes=[bias] + [operand] * 4,
        cost_estimate=pl.CostEstimate(
            flops=12 * scores * LANES, bytes_accessed=12 * scores, transcendentals=scores
        ),
        name="banded_grads",
        **common,
    )(lo, hi, *stats, queries, d_context, *tokens, *tokens)


TILE = 512


def project_kernel(x_ref, wk_ref, wv_ref, out_ref):
    n = pl.program_id(0)
    half = pl.num_programs(0) // 2

    @pl.when(n < half)
    def _():
        out_ref[...] = nn_dot(x_ref[...], wk_ref[...]).astype(BF16)

    @pl.when(n >= half)
    def _():
        out_ref[...] = nn_dot(x_ref[...], wv_ref[...]).astype(BF16)


def project_rows(x, key_weight, value_weight):
    width = x.shape[1]
    half = width // TILE
    return pl.pallas_call(
        project_kernel,
        grid=(2 * half,),
        in_specs=[
            pl.BlockSpec(x.shape, lambda n: (0, 0)),
            pl.BlockSpec((width, TILE), lambda n: (0, jnp.minimum(n, half - 1))),
            pl.BlockSpec((width, TILE), lambda n: (0, jnp.maximum(n - half, 0))),
        ],
        out_specs=pl.BlockSpec((x.shape[0], TILE), lambda n: (0, n)),
        out_shape=jax.ShapeDtypeStruct((x.shape[0], 2 * width), BF16),
        compiler_params=pltpu.CompilerParams(dimension_semantics=("arbitrary",)),
        cost_estimate=pl.CostEstimate(
            flops=4 * x.shape[0] * width * width,
            bytes_accessed=6 * x.shape[0] * width + 4 * width * width,
            transcendentals=0,
        ),
        name="project_rows",
    )(x, key_weight, value_weight)


def flips(n_dev, bit):
    return [(i, i ^ (1 << bit)) for i in range(n_dev)]


def place(rows, blocks, at):
    for x in blocks:
        rows = lax.dynamic_update_slice_in_dim(rows, x, at, 0)
        at += x.shape[0]
    return rows


class Gather:
    def __init__(self, block, bits):
        self.block = block
        self.n_dev = 1 << bits
        self.order = list(range(bits - 1, -1, -1))

    def send(self):
        self.bit = self.order.pop(0)
        return self.block, flips(self.n_dev, self.bit)

    def receive(self, come):
        if self.bit == 0:
            self.block = jnp.stack([self.block, come])
            return
        mine = (lax.axis_index("tm") >> self.bit) & 1
        self.block = jnp.where(
            mine == 0,
            jnp.stack([self.block, come], axis=-3),
            jnp.stack([come, self.block], axis=-3),
        )


class Move:
    def __init__(self, block, perm):
        self.block = block
        self.order = [perm]

    def send(self):
        return self.block, self.order.pop(0)

    def receive(self, come):
        self.come = come


def beside(moving, work, *args):
    moving = [m for m in moving if m.order]
    sends = [m.send() for m in moving]
    args, aways = lax.optimization_barrier((args, [away for away, _ in sends]))
    comes = [lax.ppermute(away, "tm", perm) for away, (_, perm) in zip(aways, sends)]
    result, comes = lax.optimization_barrier((work(*args), comes))
    for m, come in zip(moving, comes):
        m.receive(come)
    return result


def shards(
    exo_tokens, queries, key_weight, value_weight, out_weight, gaze_valid, window_offset, cotangent
):
    n_query, width = queries.shape
    tok = exo_tokens.shape[1]
    n_dev = lax.axis_size("tm")
    bits = n_dev.bit_length() - 1
    src = n_dev // 2
    total = n_query * n_dev
    me = lax.axis_index("tm")
    upper_half = me >= src
    spot = me % src
    fence = lax.optimization_barrier

    owner_one = [(s, 2 * s) for s in range(src)] + [(src + s, 2 * s + 1) for s in range(src)]
    owner_two = [(s, 2 * s + 1) for s in range(src)] + [(src + s, 2 * s) for s in range(src)]
    valid_col = gaze_valid.astype(F32)[:, None]
    masked_grad = (cotangent.astype(F32) * valid_col).astype(BF16)
    note = jnp.zeros((W, width), BF16).at[0, :n_query].set(window_offset.astype(BF16))
    letter = jnp.concatenate([queries, masked_grad, note], axis=0)

    def frames(exo, *cuts):
        by_block = exo.reshape(src, 2, n_query, tok, width)
        runs = jnp.stack([by_block[:, :, cut : cut + W] for cut in cuts], axis=1)
        runs = runs.transpose(0, 1, 4, 2, 3, 5)
        return with_layout_constraint(runs, Layout(tuple(range(6))))

    later = fence(exo_tokens)
    outer = frames(exo_tokens, 0, n_query - W)
    inner = frames(later, W, 2 * W)
    halves = [list(range(src)), list(range(src, n_dev))]
    gather = Gather(masked_grad, bits)
    edge = lax.all_to_all(outer, "tm", 0, 0, axis_index_groups=halves, tiled=True)
    one = lax.ppermute(letter, "tm", [(b, a) for a, b in owner_one])
    two = lax.ppermute(letter, "tm", [(b, a) for a, b in owner_two])
    weights = jnp.concatenate([key_weight, value_weight], axis=1)
    edge, inner, weights, one, two = fence((edge, inner, weights, one, two))
    middle = lax.all_to_all(inner, "tm", 0, 0, axis_index_groups=halves, tiled=True)

    pair = jnp.where(upper_half, jnp.stack([two, one]), jnp.stack([one, two]))
    q_pair = pair[:, :n_query]
    g_pair = nt_dot(pair[:, n_query : 2 * n_query].reshape(-1, width), out_weight)
    g_pair = g_pair.astype(BF16).reshape(q_pair.shape)
    offsets = pair[:, 2 * n_query, :n_query].astype(jnp.int32)
    at = jnp.arange(n_query, dtype=jnp.int32)
    first = (2 * spot + jnp.arange(2, dtype=jnp.int32))[:, None] * n_query
    lower = jnp.maximum(at - W + offsets, -first)
    upper = jnp.minimum(at + offsets, total - 1 - first)

    def lanes(x):
        return jnp.tile(x.reshape(2, 2, 1, n_query // 2), (1, 1, GROUP, 1)).reshape(2, 1, -1)

    lo, hi = lanes(lower), lanes(upper)

    def project(x):
        flat = nn_dot(x.reshape(-1, width), weights).astype(BF16)
        return flat.reshape(x.shape[:-1] + (2 * width,))

    edge_kv = project(edge)
    up = [(i, i + 1) for i in range(n_dev - 1) if (i + 1) % src]
    local = jnp.stack([edge[:, 0, :, 1], edge[:, 1, :, 0]], axis=2)
    early = [x.reshape(-1, width) for x in (edge[:, 0], edge[:, 1], local)]
    n_early = sum(x.shape[0] for x in early)
    rows = place(jnp.zeros((2 * n_early, width), BF16), early, 0)
    low = Move(edge[:, 1, :, 1], up)
    high = Move(edge[:, 0, :, 0], [(target, source) for source, target in up])
    middle, edge_kv, q_pair, g_pair, lo, hi, rows, low.block, high.block = fence(
        (middle, edge_kv, q_pair, g_pair, lo, hi, rows, low.block, high.block)
    )
    middle_kv = beside(
        [low, high], project_rows, middle.reshape(-1, width), key_weight, value_weight
    ).reshape(middle.shape[:-1] + (2 * width,))
    ext = jnp.stack([low.come, high.come], axis=1)
    ext_kv = project(ext)
    tokens = (edge_kv, middle_kv, ext_kv)

    stats = beside(
        [gather],
        functools.partial(attention, 0, width // LANES, lo, hi, None),
        q_pair, g_pair, tokens,
    )
    swap = Move(stats, flips(n_dev, bits - 1))

    def fill(rows, middle, low, high):
        late = (middle[:, 0], middle[:, 1], jnp.stack([low, high], axis=2))
        return place(rows, [x.reshape(-1, width) for x in late], n_early)

    sources = beside([gather, swap], fill, rows, middle, low.come, high.come)

    core = me & 1
    chips = [[2 * k + c for k in range(src)] for c in range(2)]

    def meet(term):
        rows = term.reshape(src, 2, -1, term.shape[1])
        away = lax.dynamic_index_in_dim(rows, 1 - core, 1, keepdims=False)
        keep = lax.dynamic_index_in_dim(rows, core, 1, keepdims=False)
        return add(keep, lax.ppermute(away, "tm", flips(n_dev, 0)))

    def scatter(block):
        return lax.all_to_all(block, "tm", 0, 0, axis_index_groups=chips, tiled=True)

    def add(x, y):
        return (x.astype(F32) + y.astype(F32)).astype(BF16)

    def half_context(part):
        half = upper_half.astype(jnp.int32)
        return [
            Move(lax.dynamic_index_in_dim(part, half, 0, keepdims=False), owner_one),
            Move(lax.dynamic_index_in_dim(part, 1 - half, 0, keepdims=False), owner_two),
        ]

    def weigh(g):
        return tn_dot(sources, g.reshape(sources.shape[0], -1)).astype(BF16)

    def weigh_and_meet(g):
        term = weigh(g)
        return meet(term)

    def assemble(*parts):
        sums = [(a + b).astype(BF16) for a, b in zip(parts[::2], parts[1::2])]
        return jnp.concatenate(sums, axis=2)

    trades, shares, ready, start = [], [], None, 0
    for groups in SPLIT:
        work = functools.partial(attention, start, groups, lo, hi, (swap.block, swap.come))
        start += groups
        if ready is not None:
            ready, q_pair = fence((ready, q_pair))
            share = scatter(ready)
        partial, grads = beside([gather], work, q_pair, g_pair, tokens)
        trade = half_context(partial)
        trades += trade
        sent = beside(trade + [gather], weigh_and_meet, grads)
        if ready is not None:
            shares.append(share)
        ready = sent

    context, d_query = assemble(*[move.come for move in trades])
    partner = Move(context, flips(n_dev, 0))
    context = beside([partner], lambda x: x, context)
    ready, shares = fence((ready, shares))

    columns = jnp.concatenate(
        [x.reshape(n_query, src, -1).swapaxes(0, 1) for x in (context, partner.come)], axis=2
    )
    if ready.shape[1] == n_query:
        packed = scatter(jnp.concatenate([ready, columns], axis=2))
        share, columns = packed[:, :, : ready.shape[2]], packed[:, :, ready.shape[2] :]
    else:
        share, columns = scatter(ready), scatter(columns)
    shares.append(share)
    attended = (nn_dot(context, out_weight) * valid_col).astype(BF16)
    columns = columns.reshape(src * n_query, -1)
    all_grad = gather.block.reshape(2, src * n_query, width)
    cut = columns.shape[1] // 2
    d_out = tn_dot(columns[:, :cut], all_grad[0]) + tn_dot(columns[:, cut:], all_grad[1])
    d_out = lax.dynamic_slice_in_dim(d_out, core * (cut // 2), cut // 2, 0)
    sums = [jnp.sum(share.astype(F32), axis=0) for share in shares]

    def heads(which):
        cuts = [(x, (2 * i + which) * LANES) for x, n in zip(sums, SPLIT) for i in range(n)]
        return jnp.concatenate([x[:, i : i + LANES] for x, i in cuts], axis=1)

    return attended, d_query, heads(0), heads(1), d_out


def solution(mesh):
    in_specs = (
        P("rep", "tm", None),
        P(("rep", "tm"), None),
        P(),
        P(),
        P(),
        P(("rep", "tm")),
        P(("rep", "tm")),
        P(("rep", "tm"), None),
    )
    out_specs = (
        P(("rep", "tm"), None),
        P(("rep", "tm"), None),
        P(("rep", "tm"), None),
        P(("rep", "tm"), None),
        P(("rep", "tm"), None),
    )

    return jax.shard_map(shards, mesh=mesh, in_specs=in_specs, out_specs=out_specs, check_vma=False)
```
